32 devices in a mesh: tm: 2 (over x), cell: 16 (over z, y, core).
Axes of the slice: x: 2, y: 2, z: 4, core: 2. Of those that a mesh axis runs over, the one named last changes fastest.
Arguments:
- initial: float32 [4096, 128], P('cell'), may hold values from 0.2 to 6, as said below
- source: float32 [4, 4096, 128], P('tm', 'cell'), may hold values from -1.8 to 1.8
- mix_rate: float32 [128], replicated, may hold values from 0.05 to 0.4
- fine_inverse: float32 [4, 32, 128, 128], P('tm', 'cell'), may hold values from -0.1 to 0.9, as said below
- coarse_inverse: float32 [4, 32, 128, 128], P('tm', 'cell'), may hold values from -0.1 to 1, as said below
- step_counts: int32 [4096], P('cell'), may hold values from 4 to 8
Outputs:
- finals: float32 [4, 4096, 128], P('tm', 'cell')
The draws below stay inside these ranges and needn't reach their ends.
Inputs may be any that keep to these rules, and one draw needn't show every extreme that they name: `initial`: positive compositions. `fine_inverse`: each matrix is a positive diagonal plus small off-diagonal entries. `coarse_inverse`: each matrix is a positive diagonal plus small off-diagonal entries.
All inputs are finite; a program needn't handle non-finite values.
Results may differ from the reference program's by a relative error of at most 0.00011.
Values sent between devices are 32-bit elements; how exact they have to be, the bound alone decides.
No kernel may reach another device: no remote copies, remote signals or barrier semaphores. Data moves between devices by JAX's collectives and lax.ppermute only.
A program may use at most 64 MiB of HBM per device.

```python
import math
import jax
import jax.numpy as jnp
from jax import lax

S = 128
FINE_MAX = 8
ITERS = 2
CELLS = 4096
SLICES = 4
GROUPS = 32


def draw_initial(key, part):
    first = jax.random.fold_in(key, 0)
    base = jnp.exp(jax.random.uniform(first, (CELLS, S), jnp.float32, math.log(0.2), math.log(2.0)))
    ramp = 1.0 + 2.0 * jnp.arange(CELLS, dtype=jnp.float32)[:, None] / CELLS
    return base * ramp


def inverse_family(key, lowest, highest, spread):
    first, second = jax.random.split(key)
    diagonal = jnp.exp(jax.random.uniform(first, (SLICES, GROUPS, S), jnp.float32, math.log(lowest), math.log(highest)))
    offdiag = jnp.clip(jax.random.normal(second, (SLICES, GROUPS, S, S), jnp.float32) * spread / math.sqrt(S), -0.1, 0.1)
    return offdiag + diagonal[..., None] * jnp.eye(S, dtype=jnp.float32)


def draw_fine_inverse(key, part):
    return inverse_family(jax.random.fold_in(key, 11), 0.3, 0.8, 0.1)


def draw_coarse_inverse(key, part):
    return inverse_family(jax.random.fold_in(key, 23), 0.3, 0.9, 0.08)


def set_ends(drawn, key, smallest, largest):
    place = [jax.random.randint(jax.random.fold_in(key, axis), (), 0, length) for axis, length in enumerate(drawn.shape)]
    main_axis = drawn.shape.index(max(drawn.shape))
    beside = place[:main_axis] + [(place[main_axis] + 1) % drawn.shape[main_axis]] + place[main_axis + 1:]
    return drawn.at[tuple(place)].set(smallest).at[tuple(beside)].set(largest)


def level_of(key, extent, cuts, low, top_value):
    def one(axis_at, shards_of):
        heights = jax.random.uniform(jax.random.fold_in(jax.random.fold_in(key, 6), axis_at), (shards_of,), jnp.float32, low / len(cuts), top_value / len(cuts))
        return jnp.repeat(jnp.exp(heights), extent[axis_at] // shards_of).reshape((-1,) + (1,) * (len(extent) - axis_at - 1))

    loudness = one(*cuts[0])
    for cut in cuts[1:]:
        loudness = loudness * one(*cut)
    return loudness


def centred(stream_key, extent, scale, reach, pieces=(), kind=jnp.bfloat16):
    values = scale * jax.random.normal(stream_key, extent, jnp.float32)
    if pieces:
        values = values * level_of(stream_key, extent, pieces, -0.22, 0.18)
    return jnp.clip(values, -reach, reach).astype(kind)


def setup_inputs(seed: int = 0) -> dict:
    seeds = jax.random.split(jax.random.key(seed), 7)
    initial = draw_initial(jax.random.fold_in(seeds[6], 71), 0)
    source = centred(seeds[1], (SLICES, CELLS, S), 0.3, 1.8, ((0, 2), (1, 16)), jnp.float32)
    mix_rate = jnp.clip(jax.random.uniform(seeds[2], (S,), jnp.float32, 0.05, 0.4), 0.05, 0.4)
    fine_inverse = draw_fine_inverse(jax.random.fold_in(seeds[6], 71), 0)
    coarse_inverse = draw_coarse_inverse(jax.random.fold_in(seeds[6], 71), 0)
    step_counts = set_ends(jax.random.randint(seeds[5], (CELLS,), FINE_MAX // 2, FINE_MAX + 1), jax.random.fold_in(seeds[5], 1), FINE_MAX // 2, FINE_MAX).astype(jnp.int32)
    return dict(initial=initial, source=source, mix_rate=mix_rate, fine_inverse=fine_inverse, coarse_inverse=coarse_inverse, step_counts=step_counts)


def group_apply(state, matrices):
    lead, count, width = state.shape
    groups = matrices.shape[1]
    shaped = state.reshape(lead, groups, count // groups, width)
    result = jnp.einsum("lgcs,lgst->lgct", shaped, matrices, precision=lax.Precision.HIGHEST)
    return result.reshape(lead, count, width)


def chain(initial, offsets, coarse_inverse):
    def advance(state, inputs):
        matrices, offset = inputs
        nxt = group_apply(state[None], matrices[None])[0] + offset
        return nxt, nxt

    _, finals = lax.scan(advance, initial, (coarse_inverse, offsets))
    return finals


def reference(initial, source, mix_rate, fine_inverse, coarse_inverse, step_counts):
    offsets0 = group_apply(source, coarse_inverse)
    finals = chain(initial, offsets0, coarse_inverse)
    for sweep_round in range(ITERS):
        starts = jnp.concatenate([initial[None], finals[:-1]], axis=0)
        state = starts
        for substep in range(FINE_MAX):
            average = jnp.sum(state, axis=1, keepdims=True) / CELLS
            moved = group_apply(state + source + mix_rate * (average - state), fine_inverse)
            active = (substep < step_counts)[None, :, None]
            state = jnp.where(active, moved, state)
        coarse_ends = group_apply(starts, coarse_inverse) + offsets0
        offsets = offsets0 + state - coarse_ends
        finals = chain(initial, offsets, coarse_inverse)
    return finals
```

```python
import jax
import jax.numpy as jnp
from jax import lax
from jax.sharding import PartitionSpec as P

FINE_MAX = 8
FINE_MIN = 4
CLASSES = FINE_MAX - FINE_MIN + 1
MATS = 7


def mm(a, b):
    return jnp.dot(a, b, precision=lax.Precision.HIGHEST)


def from_behind(block, axis, distance):
    devices = range(lax.axis_size(axis))
    route = [(i - distance, i) for i in devices if i - distance in devices]
    return lax.ppermute(block, axis, route)


def swap_core(block):
    n = lax.axis_size("cell")
    return lax.ppermute(block, "cell", [(i, i ^ 1) for i in range(n)])


def same_core():
    n = lax.axis_size("cell")
    return [list(range(c, n, 2)) for c in range(2)]


def spread(block, groups=None):
    n = lax.axis_size("cell") if groups is None else len(groups[0])
    return lax.all_to_all(
        jnp.broadcast_to(block[None], (n,) + block.shape), "cell", 0, 0,
        axis_index_groups=groups,
    )


def total(block):
    return spread(block).sum(0)


def body(initial, source, mix_rate, fine_inverse, coarse_inverse, step_counts):
    slices, groups, width, _ = fine_inverse.shape
    cells = initial.shape[0]
    per = cells // groups
    n_cell = lax.axis_size("cell")
    turns = lax.axis_size("tm") - 1
    everyone = cells * n_cell
    leading = lax.axis_index("tm") == 0
    core = lax.axis_index("cell") % 2
    rate = mix_rate[None, :]
    keep = 1.0 - rate
    keep_col = keep.reshape(width, 1)

    W = []
    for l in range(slices):
        row = []
        for g in range(groups):
            w1 = fine_inverse[l, g]
            w2 = mm(w1, keep_col * w1)
            w34 = mm(jnp.concatenate([w1, w2]), keep_col * w2)
            w4 = w34[width:]
            w58 = mm(jnp.concatenate([w1, w2, w34]), keep_col * w4)
            row.append([None, w1, w2, w34[:width], w4] + [w58[i * width:(i + 1) * width] for i in range(4)])
        W.append(row)
    counts = step_counts.reshape(groups, per)
    active = {q: jnp.sum((counts >= q).astype(jnp.float32), axis=1) for q in range(FINE_MIN, FINE_MAX + 2)}
    parts = []
    for l in range(slices):
        mats = [sum(W[l][g][d] for g in range(groups)) * (per / everyone) for d in range(1, 5)]
        e6 = sum(active[6][g] * W[l][g][1] for g in range(groups)) / everyone
        e7 = sum(active[7][g] * W[l][g][1] for g in range(groups)) / everyone
        e72 = sum(active[7][g] * W[l][g][2] for g in range(groups)) / everyone
        parts.append(jnp.stack(mats + [e6, e6 + e72 - e7, e7]))
    half = slices // 2
    parts = jnp.stack(parts)
    low, high = parts[:half], parts[half:]
    mine = jnp.where(core == 0, low, high)
    other = jnp.where(core == 0, high, low)
    mine = mine + swap_core(other)
    shard = lax.all_to_all(
        mine.reshape(n_cell // 2, -1, width), "cell", 0, 0, axis_index_groups=same_core()
    ).sum(0)
    mixing = spread(shard, same_core()).reshape(half, MATS, width, width)
    theirs = swap_core(mixing)
    mixing = jnp.where(
        core == 0, jnp.concatenate([mixing, theirs]), jnp.concatenate([theirs, mixing])
    )

    def by_group(state, matrices):
        return jnp.concatenate(
            [mm(state[g * per:(g + 1) * per], matrices[g]) for g in range(groups)]
        )

    def fine_alone(state, l):
        rows = []
        for g in range(groups):
            here = slice(g * per, (g + 1) * per)
            v, s = state[here] * keep, source[l, here]
            k = step_counts[here][:, None]
            summed = sum(W[l][g][d] for d in range(1, FINE_MIN))
            out = 0.0
            for d in range(FINE_MIN, FINE_MAX + 1):
                summed = summed + W[l][g][d]
                out = jnp.where(k == d, mm(v, W[l][g][d]) + mm(s, summed), out)
            rows.append(out)
        return jnp.concatenate(rows)

    def handed(start, advance):
        incoming = start
        for _ in range(turns):
            received = from_behind(advance(incoming), "tm", 1)
            incoming = jnp.where(leading, start, received)
        return incoming

    def coarse_run(incoming):
        states = [incoming]
        for l in range(slices):
            states.append(by_group(states[-1] + source[l], coarse_inverse[l]))
        return states

    starts = coarse_run(handed(initial, lambda u: coarse_run(u)[-1]))
    alone = [starts]
    for _ in range(2):
        old = alone[-1]
        fines = [fine_alone(old[l], l) for l in range(slices)]

        def run(incoming):
            states = [incoming]
            for l in range(slices):
                states.append(fines[l] + by_group(states[l] - old[l], coarse_inverse[l]))
            return states

        alone.append(run(handed(initial, lambda u: run(u)[-1])))

    def sums(state):
        rows = []
        for g in range(groups):
            here = slice(g * per, (g + 1) * per)
            mask = (step_counts[here][None, :] >= jnp.arange(FINE_MIN, FINE_MAX + 1)[:, None])
            rows.append(mm(mask.astype(jnp.float32), state[here]))
        return rows

    source_sums = [sums(source[l]) for l in range(slices)]

    def first_rows(V, l):
        out = [sum(V[g][0:1] for g in range(groups))]
        for m in range(1, FINE_MIN + 1):
            row = 0.0
            for g in range(groups):
                row = row + mm(V[g][0:1] * keep, W[l][g][m])
                row = row + mm(source_sums[l][g][0:1], sum(W[l][g][d] for d in range(1, m + 1)))
            out.append(row)
        return jnp.concatenate(out) / everyone

    def folded(a, W_lg, m, known):
        return sum(mm(a[j] * rate, W_lg[m - j]) for j in range(min(m, known)))

    def second_rows(V, a, l):
        out = []
        base = 0.0
        for g in range(groups):
            w = W[l][g]
            base = base + mm(V[g][0:1] * keep, w[4]) + mm(source_sums[l][g][0:1], w[1] + w[2] + w[3] + w[4])
            base = base + per * folded(a, w, 4, 5)
        for m in range(5, 8):
            q = m - FINE_MIN
            for g in range(groups):
                w = W[l][g]
                base = base + mm(V[g][q:q + 1] * keep, w[m] - w[m - 1]) + mm(source_sums[l][g][q:q + 1], w[m])
                base = base + active[m][g] * (folded(a, w, m, 5) - folded(a, w, m - 1, 5))
            out.append(base)
        return jnp.concatenate(out) / everyone

    def averages(V):
        rows = jnp.stack([first_rows(V[l], l) for l in range(slices)])
        rows = total(rows)
        a = []
        for l in range(slices):
            known = []
            for m in range(5):
                known.append(rows[l, m:m + 1] + sum(mm(known[j] * rate, mixing[l, m - j - 1]) for j in range(m)))
            a.append(known)
        rows = jnp.stack([second_rows(V[l], a[l], l) for l in range(slices)])
        rows = total(rows)
        for l in range(slices):
            a5 = rows[l, 0:1]
            a6 = rows[l, 1:2] + mm(a5 * rate, mixing[l, 4])
            a7 = rows[l, 2:3] + mm(a5 * rate, mixing[l, 5]) + mm(a6 * rate, mixing[l, 6])
            a[l] = a[l] + [a5, a6, a7]
        return a

    def pushes(a, l):
        return [
            jnp.concatenate([folded(a, W[l][g], k, k) for k in range(FINE_MIN, FINE_MAX + 1)])
            for g in range(groups)
        ]

    def coarse_vectors(x, l):
        return [mm(x[g], coarse_inverse[l, g]) for g in range(groups)]

    V = [sums(alone[0][l]) for l in range(slices)]
    a = averages(V)
    h = [pushes(a[l], l) for l in range(slices)]

    def run1(incoming):
        xs = [[incoming[g] for g in range(groups)]]
        for l in range(slices):
            moved = coarse_vectors(xs[l], l)
            xs.append([h[l][g] + moved[g] for g in range(groups)])
        return xs

    zero = jnp.zeros((groups, CLASSES, width), jnp.float32)
    x1 = run1(handed(zero, lambda x: jnp.stack(run1(x)[-1])))
    V = []
    for l in range(slices):
        plain = sums(alone[1][l])
        rows = []
        for g in range(groups):
            row = plain[g]
            exact = [active[k][g] - active[k + 1][g] for k in range(FINE_MIN, FINE_MAX + 1)]
            weighted = [exact[i] * x1[l][g][i:i + 1] for i in range(CLASSES)]
            tails = [sum(weighted[i:]) for i in range(CLASSES)]
            rows.append(row + jnp.concatenate(tails))
        V.append(rows)
    a = averages(V)
    h = [pushes(a[l], l) for l in range(slices)]
    y = [
        [
            h[l][g] + jnp.concatenate(
                [mm(x1[l][g][i:i + 1] * keep, W[l][g][FINE_MIN + i]) for i in range(CLASSES)]
            )
            for g in range(groups)
        ]
        for l in range(slices)
    ]

    def run2(incoming):
        xs = [[incoming[g] for g in range(groups)]]
        for l in range(slices):
            moved = coarse_vectors([xs[l][g] - x1[l][g] for g in range(groups)], l)
            xs.append([y[l][g] + moved[g] for g in range(groups)])
        return xs

    x2 = run2(handed(zero, lambda x: jnp.stack(run2(x)[-1])))
    outs = []
    for l in range(slices):
        rows = []
        for g in range(groups):
            here = slice(g * per, (g + 1) * per)
            k = step_counts[here][:, None]
            out = alone[2][l + 1][here]
            for i in range(CLASSES):
                out = out + jnp.where(k == FINE_MIN + i, x2[l + 1][g][i:i + 1], 0.0)
            rows.append(out)
        outs.append(jnp.concatenate(rows))
    return jnp.stack(outs)


def solution(mesh):
    return jax.shard_map(
        body,
        mesh=mesh,
        in_specs=(
            P("cell", None),
            P("tm", "cell", None),
            P(),
            P("tm", "cell", None, None),
            P("tm", "cell", None, None),
            P("cell"),
        ),
        out_specs=P("tm", "cell", None),
        check_vma=False,
    )
```

```python
import functools

import jax
import jax.numpy as jnp
from jax import lax
from jax.experimental import pallas as pl
from jax.experimental.pallas import tpu as pltpu
from jax.sharding import PartitionSpec as P

FINE_MAX = 8
FINE_MIN = 4
CLASSES = FINE_MAX - FINE_MIN + 1
MATS = 7
ROWS = 8
F32 = jnp.float32
BF16 = jnp.bfloat16


def high_low(x):
    high = x.astype(BF16).astype(F32)
    return high, x - high


def stacked(w):
    high, low = high_low(w)
    return jnp.concatenate([high, low], axis=0).astype(BF16)


def mul(x, w):
    rows = x.shape[0]
    high, low = high_low(x)
    left = jnp.concatenate([high, low], axis=0).astype(BF16)
    right = jnp.concatenate([high, jnp.zeros_like(low)], axis=0).astype(BF16)
    out = jnp.dot(jnp.concatenate([left, right], axis=1), w, preferred_element_type=F32)
    return out[:rows] + out[rows:]


def row_is(i, shape):
    return lax.broadcasted_iota(jnp.int32, shape, 0) == i


def leading():
    return lax.axis_index("tm") == 0


def from_behind(block, axis, distance):
    devices = range(lax.axis_size(axis))
    route = [(i - distance, i) for i in devices if i - distance in devices]
    return lax.ppermute(block, axis, route)


def swap_core(block):
    n = lax.axis_size("cell")
    return lax.ppermute(block, "cell", [(i, i ^ 1) for i in range(n)])


def same_core():
    n = lax.axis_size("cell")
    return [list(range(c, n, 2)) for c in range(2)]


def exchange(block, groups=None):
    return lax.all_to_all(block, "cell", 0, 0, axis_index_groups=groups)


def call(kernel, name, outs, args, scratch=(), flops=0):
    size = sum(x.size * x.dtype.itemsize for x in args)
    size += sum(x.size * x.dtype.itemsize for x in outs)
    return pl.pallas_call(
        kernel,
        out_shape=outs,
        in_specs=[pl.BlockSpec(memory_space=pltpu.VMEM)] * len(args),
        out_specs=[pl.BlockSpec(memory_space=pltpu.VMEM)] * len(outs),
        scratch_shapes=list(scratch),
        compiler_params=pltpu.CompilerParams(vmem_limit_bytes=24 << 20),
        cost_estimate=pl.CostEstimate(flops=flops, bytes_accessed=size, transcendentals=0),
        name=name,
    )(*args)


def shape(*dims, dtype=F32):
    return jax.ShapeDtypeStruct(dims, dtype)


def group_rows(g, per):
    return slice(g * per, (g + 1) * per)


def block(d, width):
    return slice((d - 1) * width, d * width)


def coarse_kernel(start, received, source, coarse, out):
    slices, groups, width, _ = coarse.shape
    per = start.shape[0] // groups
    for g in range(groups):
        here = group_rows(g, per)
        u = jnp.where(leading(), start[here], received[here])
        for l in range(slices):
            u = mul(u + source[l, here], stacked(coarse[l, g]))
        out[here] = u


def setup_kernel(everyone, fine, rate, counts, own, other, powers, spread, active):
    slices, groups, width, _ = fine.shape
    per = counts.shape[1]
    half = slices // 2
    keep = 1.0 - rate[...]
    core = lax.rem(lax.axis_index("cell"), 2)
    alive = []
    for g in range(groups):
        k = counts[g:g + 1].astype(F32)
        spread[group_rows(g, per)] = jnp.broadcast_to(k, (per, per)).T
        rows = [
            jnp.sum((k >= q).astype(F32), axis=1, keepdims=True)
            for q in range(FINE_MIN, FINE_MAX + 1)
        ]
        alive.append(rows)
        filled = jnp.zeros((ROWS, width), F32)
        for i, n in enumerate(rows):
            filled = jnp.where(row_is(i, filled.shape), n, filled)
        active[g] = filled
    for l in range(slices):
        sums = [0.0] * 4
        e6, e7, e72 = 0.0, 0.0, 0.0
        for g in range(groups):
            w1 = fine[l, g]
            st1 = stacked(w1)
            w2 = mul(w1 * keep, st1)
            st2 = stacked(w2)
            first = jnp.concatenate([w1, w2], axis=0)
            w34 = mul(first * keep, st2)
            w3, w4 = w34[:width], w34[width:]
            st4 = stacked(w4)
            w58 = mul(jnp.concatenate([first, w34], axis=0) * keep, st4)
            powers[l, g, :, block(1, width)] = st1
            powers[l, g, :, block(2, width)] = st2
            powers[l, g, :, block(3, width)] = stacked(w3)
            powers[l, g, :, block(4, width)] = st4
            for i in range(4):
                powers[l, g, :, block(5 + i, width)] = stacked(w58[i * width:(i + 1) * width])
            sums = [t + w for t, w in zip(sums, (w1, w2, w3, w4))]
            e6 = e6 + alive[g][2] * w1
            e7 = e7 + alive[g][3] * w1
            e72 = e72 + alive[g][3] * w2
        mats = [t * (per / everyone) for t in sums]
        mats += [e6 / everyone, (e6 + e72 - e7) / everyone, e7 / everyone]
        for i, m in enumerate(mats):
            at = slice(((l % half) * MATS + i) * width, ((l % half) * MATS + i + 1) * width)

            @pl.when(core == l // half)
            def _():
                own[at] = m

            @pl.when(core != l // half)
            def _():
                other[at] = m


def class_sums(state, k):
    mask = k >= (FINE_MIN + lax.broadcasted_iota(jnp.int32, (ROWS, k.shape[1]), 0))
    mask = mask.astype(F32)
    left = jnp.concatenate([mask, mask], axis=1)
    left = jnp.concatenate([left, jnp.zeros_like(left)], axis=0).astype(BF16)
    return jnp.dot(left, stacked(state), preferred_element_type=F32)[:ROWS]


def picked(products, first, width):
    out = jnp.zeros((ROWS, width), F32)
    for i in range(CLASSES):
        d = first + i
        if 1 <= d <= FINE_MAX:
            out = out + jnp.where(row_is(i, out.shape), products[:, block(d, width)], 0.0)
    return out


def sums_of_state(V, keep, powers, width):
    x = mul(V * keep, powers)
    rows = [V[0:1]] + [x[0:1, block(m, width)] for m in range(1, FINE_MIN + 1)]
    gain = picked(x, FINE_MIN, width) - picked(x, FINE_MIN - 1, width)
    for i in range(1, 4):
        rows.append(rows[-1] + gain[i:i + 1])
    return jnp.concatenate(rows, axis=0)


def sums_of_source(S, powers, width):
    x = mul(S, powers)
    rows = [jnp.zeros((1, width), F32)]
    for m in range(1, FINE_MAX):
        i = max(m - FINE_MIN, 0)
        rows.append(rows[-1] + x[i:i + 1, block(m, width)])
    return jnp.concatenate(rows, axis=0)


def by_count(products, k, first, width):
    out = jnp.zeros(k.shape, F32)
    for i in range(CLASSES):
        d = i * width
        out = jnp.where(k == float(FINE_MIN + i), products[:, d:d + width], out)
    return out


def fine_of_state(v, keep, powers, k, width):
    return by_count(mul(v * keep, powers), k, FINE_MIN, width)


def start_kernel(everyone, initial, received, source, coarse, powers, rate, counts, spread,
                 base, ofsource, starts, fines, sourced):
    slices, groups, width, _ = coarse.shape
    per = counts.shape[1]
    keep = 1.0 - rate[...]
    states = [
        jnp.where(leading(), initial[group_rows(g, per)], received[group_rows(g, per)])
        for g in range(groups)
    ]
    for l in range(slices):
        rows, rows_source = 0.0, 0.0
        for g in range(groups):
            here = group_rows(g, per)
            k = counts[g:g + 1]
            u, s, w = states[g], source[l, here], powers[l, g]
            starts[l, here] = u
            rows = rows + sums_of_state(class_sums(u, k), keep, w, width)
            rows_source = rows_source + sums_of_source(class_sums(s, k), w, width)
            if l + 1 < slices:
                states[g] = mul(u + s, stacked(coarse[l, g]))
        rows_source = rows_source / everyone
        at = slice(l * ROWS, (l + 1) * ROWS)
        ofsource[at] = rows_source
        base[at] = rows / everyone + rows_source
    for l in range(slices):
        for g in range(groups):
            here = group_rows(g, per)
            n = spread[here]
            w = powers[l, g]
            x = mul(source[l, here], w)
            total = x[:, block(1, width)]
            for d in range(2, FINE_MIN + 1):
                total = total + x[:, block(d, width)]
            out = jnp.where(n == float(FINE_MIN), total, 0.0)
            for d in range(FINE_MIN + 1, FINE_MAX + 1):
                total = total + x[:, block(d, width)]
                out = jnp.where(n == float(d), total, out)
            sourced[l, here] = out
            v = starts[l, here]
            w = powers[l, g, :, (FINE_MIN - 1) * width:]
            fines[l, here] = out + fine_of_state(v, keep, w, n, width)


def chain_kernel(start, received, old, fines, coarse, out):
    slices, groups, _, _ = coarse.shape
    per = start.shape[0] // groups
    for g in range(groups):
        here = group_rows(g, per)
        u = jnp.where(leading(), start[here], received[here])
        for l in range(slices):
            u = fines[l, here] + mul(u - old[l, here], stacked(coarse[l, g]))
        out[here] = u


def again_kernel(start, received, old, fines, sourced, coarse, powers, rate, counts, spread,
                 starts, fines_out, sums):
    slices, groups, width, _ = coarse.shape
    per = counts.shape[1]
    keep = 1.0 - rate[...]
    for g in range(groups):
        here = group_rows(g, per)
        n = spread[here]
        u = jnp.where(leading(), start[here], received[here])
        for l in range(slices):
            starts[l, here] = u
            sums[l, g] = class_sums(u, counts[g:g + 1])
            w = powers[l, g, :, (FINE_MIN - 1) * width:]
            fines_out[l, here] = sourced[l, here] + fine_of_state(u, keep, w, n, width)
            if l + 1 < slices:
                u = fines[l, here] + mul(u - old[l, here], stacked(coarse[l, g]))


def ends_kernel(start, received, old, fines, coarse, out):
    slices, groups, _, _ = coarse.shape
    per = start.shape[0] // groups
    for g in range(groups):
        here = group_rows(g, per)
        u = jnp.where(leading(), start[here], received[here])
        for l in range(slices):
            u = fines[l, here] + mul(u - old[l, here], stacked(coarse[l, g]))
            out[l, here] = u


def gather_kernel(parts, base, out):
    n, rows, _ = parts.shape
    total = parts[0]
    for p in range(1, n):
        total = total + parts[p]
    for p in range(n):
        out[p, :rows] = total
        out[p, rows:] = base[...]


def wide(row):
    return jnp.broadcast_to(row, (ROWS, row.shape[-1]))


def assembled(known, width):
    out = jnp.zeros((ROWS, width), F32)
    for m, a in enumerate(known):
        out = jnp.where(row_is(m, out.shape), a, out)
    return out


def first_averages(rows, mixing, rate, width):
    known, sent = [], []
    for m in range(FINE_MIN + 1):
        a = wide(rows[m:m + 1])
        for j in range(m):
            a = a + sent[j][:, block(m - j, width)]
        known.append(a)
        if m < FINE_MIN:
            sent.append(mul(a * rate, mixing[:, :(FINE_MIN - m) * width]))
    return assembled(known, width)


def folded(a, rate, powers, width):
    x = mul(a * rate, powers)
    out = jnp.zeros((2 * ROWS, width), F32)
    for d in range(1, FINE_MAX + 1):
        z = jnp.concatenate([x[:, block(d, width)], jnp.zeros((ROWS, width), F32)], axis=0)
        out = out + pltpu.roll(z, d, 0)
    return out


def second_rows(everyone, per, a, base, rate, powers, active, l, width):
    groups = powers.shape[1]
    rows = [0.0] * 3
    for g in range(groups):
        h = folded(a, rate, powers[l, g], width)
        total = per * h[4:5]
        for i in range(1, 4):
            total = total + active[g, i:i + 1] * (h[4 + i:5 + i] - h[3 + i:4 + i])
            rows[i - 1] = rows[i - 1] + total
    at = l * ROWS + FINE_MIN + 1
    return [rows[i] / everyone + base[at + i:at + i + 1] for i in range(3)]


def send_rows(everyone, per, a, base, rate, powers, active, out, width):
    slices = powers.shape[0]
    rows = []
    for l in range(slices):
        rows += second_rows(everyone, per, a[l], base, rate, powers, active, l, width)
        rows.append(jnp.zeros((1, width), F32))
    rows = jnp.concatenate(rows, axis=0)
    for p in range(out.shape[0]):
        out[p] = rows


def mixing_kernel(everyone, per, mine, theirs, base, powers, rate, active,
                  mixing, averages, out, held):
    slices, _, _, wider = powers.shape
    width = wider // FINE_MAX
    half = slices // 2
    n, rows, _ = mine.shape
    rows -= slices * ROWS
    core = lax.rem(lax.axis_index("cell"), 2)
    mixed = 0.0
    for ref, at in ((mine, core), (theirs, 1 - core)):
        for p in range(n):
            place = at * (half * MATS * width) + p * rows
            held[pl.ds(place, rows), :] = ref[p, :rows]
            mixed = mixed + ref[p, rows:]
    a = []
    for l in range(slices):
        for i in range(MATS):
            at = (l * MATS + i) * width
            mixing[l, :, block(i + 1, width)] = stacked(held[at:at + width])
        a.append(first_averages(mixed[l * ROWS:(l + 1) * ROWS], mixing[l], rate[...], width))
        averages[l] = a[-1]
    send_rows(everyone, per, a, base, rate[...], powers, active, out, width)


def first_kernel(everyone, per, received, base, mixing, powers, rate, active, averages, out):
    slices, _, _, wider = powers.shape
    width = wider // FINE_MAX
    total = received[0]
    for p in range(1, received.shape[0]):
        total = total + received[p]
    a = []
    for l in range(slices):
        rows = total[l * (FINE_MIN + 1):(l + 1) * (FINE_MIN + 1)]
        a.append(first_averages(rows, mixing[l], rate[...], width))
        averages[l] = a[-1]
    send_rows(everyone, per, a, base, rate[...], powers, active, out, width)


def push_kernel(received, averages, mixing, powers, rate, coarse, *refs):
    if len(refs) == 2:
        plain, starts, (pushes, end) = None, None, refs
    else:
        plain, starts, pushes, end = refs
    slices, groups, _, wider = powers.shape
    width = wider // FINE_MAX
    r = rate[...]
    total = received[0]
    for p in range(1, received.shape[0]):
        total = total + received[p]
    x = [jnp.zeros((ROWS, width), F32) for _ in range(groups)]
    for l in range(slices):
        a5 = wide(total[l * 4:l * 4 + 1])
        z = mul(a5 * r, mixing[l, :, 4 * width:6 * width])
        a6 = wide(total[l * 4 + 1:l * 4 + 2]) + z[:, :width]
        a7 = wide(total[l * 4 + 2:l * 4 + 3]) + z[:, width:]
        a7 = a7 + mul(a6 * r, mixing[l, :, 6 * width:])
        a = averages[l]
        for m, row in ((5, a5), (6, a6), (7, a7)):
            a = jnp.where(row_is(m, a.shape), row, a)
        for g in range(groups):
            h = folded(a, r, powers[l, g], width)[FINE_MIN:FINE_MIN + ROWS]
            if plain is not None:
                h = h + plain[l, g]
            pushes[l, g] = h
            old = x[g] if starts is None else x[g] - starts[l, g]
            x[g] = h + mul(old, stacked(coarse[l, g]))
    for g in range(groups):
        end[g] = x[g]


def vectors_kernel(received, pushes, starts, coarse, end):
    slices, groups, _, _ = coarse.shape
    for g in range(groups):
        x = jnp.where(leading(), 0.0, received[g])
        for l in range(slices):
            x = pushes[l, g] + mul(x - starts[l, g], stacked(coarse[l, g]))
        end[g] = x


def second_kernel(everyone, received, pushes, coarse, sums, active, powers, rate, ofsource,
                  starts, base, out):
    slices, groups, width, _ = coarse.shape
    keep = 1.0 - rate[...]
    x = [jnp.where(leading(), 0.0, received[g]) for g in range(groups)]
    sent = []
    for l in range(slices):
        rows = 0.0
        for g in range(groups):
            starts[l, g] = x[g]
            n = active[g]
            exact = n - pltpu.roll(n, ROWS - 1, 0)
            exact = jnp.where(row_is(ROWS - 1, n.shape), 0.0, exact)
            weighted = exact * x[g]
            tail = jnp.zeros((1, width), F32)
            V = sums[l, g]
            for i in reversed(range(CLASSES)):
                tail = tail + weighted[i:i + 1]
                V = jnp.where(row_is(i, V.shape), V + tail, V)
            rows = rows + sums_of_state(V, keep, powers[l, g], width)
            if l + 1 < slices:
                x[g] = pushes[l, g] + mul(x[g], stacked(coarse[l, g]))
        at = slice(l * ROWS, (l + 1) * ROWS)
        rows = rows / everyone + ofsource[at]
        base[at] = rows
        sent.append(rows[:FINE_MIN + 1])
    sent = jnp.concatenate(sent, axis=0)
    for p in range(out.shape[0]):
        out[p] = sent


def plain_kernel(starts, powers, rate, out):
    slices, groups, _, wider = powers.shape
    width = wider // FINE_MAX
    keep = 1.0 - rate[...]
    for l in range(slices):
        for g in range(groups):
            out[l, g] = picked(mul(starts[l, g] * keep, powers[l, g]), FINE_MIN, width)


def finish_kernel(received, pushes, starts, coarse, ends, spread, out):
    slices, groups, width, _ = coarse.shape
    per = spread.shape[0] // groups
    for g in range(groups):
        here = group_rows(g, per)
        n = spread[here]
        x = jnp.where(leading(), 0.0, received[g])
        for l in range(slices):
            x = pushes[l, g] + mul(x - starts[l, g], stacked(coarse[l, g]))
            add = jnp.zeros((per, width), F32)
            for i in range(CLASSES):
                add = jnp.where(n == float(FINE_MIN + i), x[i:i + 1], add)
            out[l, here] = ends[l, here] + add


def body(initial, source, mix_rate, fine, coarse, step_counts):
    slices, groups, width, _ = fine.shape
    cells = initial.shape[0]
    per = cells // groups
    n_cell = lax.axis_size("cell")
    turns = lax.axis_size("tm") - 1
    everyone = cells * n_cell
    half = slices // 2
    peers = n_cell // 2
    shard = half * MATS * width // peers
    rate = mix_rate.reshape(1, width)
    counts = step_counts.reshape(groups, per)
    state = shape(cells, width)
    states = shape(slices, cells, width)
    vectors = shape(slices, groups, ROWS, width)
    vector = shape(groups, ROWS, width)
    rows8 = shape(slices * ROWS, width)
    rows4 = shape(n_cell, slices * 4, width)
    averages = shape(slices, ROWS, width)

    def handed(first, advance):
        received = first
        for _ in range(turns):
            received = from_behind(advance(received), "tm", 1)
        return received

    received = handed(
        initial, lambda u: call(coarse_kernel, "coarse", [state], (initial, u, source, coarse))[0]
    )
    mats = shape(half * MATS * width, width)
    own, other, powers, spread, active = call(
        functools.partial(setup_kernel, everyone), "setup",
        [mats, mats, shape(slices, groups, 2 * width, FINE_MAX * width, dtype=BF16), state, vector],
        (fine, rate, counts),
    )
    mine = (own + swap_core(other)).reshape(peers, shard, width)
    parts = exchange(mine, same_core())
    base, ofsource, starts0, fines1, sourced = call(
        functools.partial(start_kernel, everyone), "start",
        [rows8, rows8, states, states, states],
        (initial, received, source, coarse, powers, rate, counts, spread),
    )
    payload, = call(
        gather_kernel, "gather", [shape(peers, shard + slices * ROWS, width)], (parts, base)
    )
    gathered = exchange(payload, same_core())
    received = handed(
        initial,
        lambda u: call(chain_kernel, "chain", [state], (initial, u, starts0, fines1, coarse))[0],
    )
    starts1, fines2, sums = call(
        again_kernel, "again", [states, states, vectors],
        (initial, received, starts0, fines1, sourced, coarse, powers, rate, counts, spread),
    )
    theirs = swap_core(gathered)
    mixing, first, out = call(
        functools.partial(mixing_kernel, everyone, per), "mixing",
        [shape(slices, 2 * width, MATS * width, dtype=BF16), averages, rows4],
        (gathered, theirs, base, powers, rate, active),
        scratch=[pltpu.VMEM((slices * MATS * width, width), F32)],
    )
    pushes1, end = call(
        push_kernel, "push", [vectors, vector],
        (exchange(out), first, mixing, powers, rate, coarse),
    )
    nothing = jnp.zeros(vectors.shape, F32)
    moved = end
    for turn in range(turns):
        moved = from_behind(moved, "tm", 1)
        if turn + 1 < turns:
            moved, = call(vectors_kernel, "vectors", [vector], (moved, pushes1, nothing, coarse))
    moved1, base, out = call(
        functools.partial(second_kernel, everyone), "second",
        [vectors, rows8, shape(n_cell, slices * (FINE_MIN + 1), width)],
        (moved, pushes1, coarse, sums, active, powers, rate, ofsource),
    )
    got = exchange(out)
    plain, = call(plain_kernel, "plain", [vectors], (moved1, powers, rate))
    received = handed(
        initial,
        lambda u: call(chain_kernel, "chain", [state], (initial, u, starts1, fines2, coarse))[0],
    )
    ends, = call(
        ends_kernel, "ends", [states], (initial, received, starts1, fines2, coarse)
    )
    first, out = call(
        functools.partial(first_kernel, everyone, per), "first", [averages, rows4],
        (got, base, mixing, powers, rate, active),
    )
    pushes2, end = call(
        push_kernel, "push", [vectors, vector],
        (exchange(out), first, mixing, powers, rate, coarse, plain, moved1),
    )
    moved = end
    for turn in range(turns):
        moved = from_behind(moved, "tm", 1)
        if turn + 1 < turns:
            moved, = call(vectors_kernel, "vectors", [vector], (moved, pushes2, moved1, coarse))
    out, = call(
        finish_kernel, "finish", [states], (moved, pushes2, moved1, coarse, ends, spread)
    )
    return out


def solution(mesh):
    return jax.shard_map(
        body,
        mesh=mesh,
        in_specs=(
            P("cell", None),
            P("tm", "cell", None),
            P(),
            P("tm", "cell", None, None),
            P("tm", "cell", None, None),
            P("cell"),
        ),
        out_specs=P("tm", "cell", None),
        check_vma=False,
    )
```

```python
import functools

import jax
import jax.numpy as jnp
from jax import lax
from jax.experimental import pallas as pl
from jax.experimental.pallas import tpu as pltpu
from jax.sharding import PartitionSpec as P

FINE_MAX = 8
FINE_MIN = 4
CLASSES = FINE_MAX - FINE_MIN + 1
MATS = 7
ROWS = 8
F32 = jnp.float32
BF16 = jnp.bfloat16


def high_low(x):
    high = x.astype(BF16).astype(F32)
    return high, x - high


def stacked(w):
    high, low = high_low(w)
    return jnp.concatenate([high, low], axis=0).astype(BF16)


def mul(x, w):
    rows = x.shape[0]
    high, low = high_low(x)
    left = jnp.concatenate([high, low], axis=0).astype(BF16)
    right = jnp.concatenate([high, jnp.zeros_like(low)], axis=0).astype(BF16)
    out = jnp.dot(jnp.concatenate([left, right], axis=1), w, preferred_element_type=F32)
    return out[:rows] + out[rows:]


def row_is(i, shape):
    return lax.broadcasted_iota(jnp.int32, shape, 0) == i


def leading():
    return lax.axis_index("tm") == 0


def from_behind(block, axis, distance):
    devices = range(lax.axis_size(axis))
    route = [(i - distance, i) for i in devices if i - distance in devices]
    return lax.ppermute(block, axis, route)


def swap_core(block):
    n = lax.axis_size("cell")
    return lax.ppermute(block, "cell", [(i, i ^ 1) for i in range(n)])


def same_core():
    n = lax.axis_size("cell")
    return [list(range(c, n, 2)) for c in range(2)]


def exchange(block, groups=None):
    return lax.all_to_all(block, "cell", 0, 0, axis_index_groups=groups)


def call(kernel, name, outs, args, scratch=(), flops=0):
    size = sum(x.size * x.dtype.itemsize for x in args)
    size += sum(x.size * x.dtype.itemsize for x in outs)
    return pl.pallas_call(
        kernel,
        out_shape=outs,
        in_specs=[pl.BlockSpec(memory_space=pltpu.VMEM)] * len(args),
        out_specs=[pl.BlockSpec(memory_space=pltpu.VMEM)] * len(outs),
        scratch_shapes=list(scratch),
        compiler_params=pltpu.CompilerParams(vmem_limit_bytes=24 << 20),
        cost_estimate=pl.CostEstimate(flops=flops, bytes_accessed=size, transcendentals=0),
        name=name,
    )(*args)


def shape(*dims, dtype=F32):
    return jax.ShapeDtypeStruct(dims, dtype)


def group_rows(g, per):
    return slice(g * per, (g + 1) * per)


def block(d, width):
    return slice((d - 1) * width, d * width)


def spread_counts(row):
    per = row.shape[1]
    return jnp.broadcast_to(row.astype(F32), (per, per)).T


def lead_kernel(start, source, coarse, counts, sums, source_sums, end):
    slices, groups, _, _ = coarse.shape
    per = counts.shape[1]
    for g in range(groups):
        here = group_rows(g, per)
        k = counts[g:g + 1]
        V = class_sums(start[here], k)
        sums[g] = V
        for l in range(slices):
            S = class_sums(source[l, here], k)
            source_sums[l, g] = S
            V = mul(V + S, stacked(coarse[l, g]))
        end[g] = V


def relay_kernel(start, received, source_sums, coarse, end):
    slices, groups, _, _ = coarse.shape
    for g in range(groups):
        V = jnp.where(leading(), start[g], received[g])
        for l in range(slices):
            V = mul(V + source_sums[l, g], stacked(coarse[l, g]))
        end[g] = V


def setup_kernel(everyone, fine, rate, counts, own, other, powers, spread, active):
    slices, groups, width, _ = fine.shape
    per = counts.shape[1]
    half = slices // 2
    keep = 1.0 - rate[...]
    core = lax.rem(lax.axis_index("cell"), 2)
    alive = []
    for g in range(groups):
        k = counts[g:g + 1].astype(F32)
        spread[group_rows(g, per)] = spread_counts(k)
        rows = [
            jnp.sum((k >= q).astype(F32), axis=1, keepdims=True)
            for q in range(FINE_MIN, FINE_MAX + 1)
        ]
        alive.append(rows)
        filled = jnp.zeros((ROWS, width), F32)
        for i, n in enumerate(rows):
            filled = jnp.where(row_is(i, filled.shape), n, filled)
        active[g] = filled
    for l in range(slices):
        sums = [0.0] * 4
        e6, e7, e72 = 0.0, 0.0, 0.0
        for g in range(groups):
            w1 = fine[l, g]
            st1 = stacked(w1)
            w2 = mul(w1 * keep, st1)
            st2 = stacked(w2)
            first = jnp.concatenate([w1, w2], axis=0)
            w34 = mul(first * keep, st2)
            w3, w4 = w34[:width], w34[width:]
            st4 = stacked(w4)
            w58 = mul(jnp.concatenate([first, w34], axis=0) * keep, st4)
            powers[l, g, :, block(1, width)] = st1
            powers[l, g, :, block(2, width)] = st2
            powers[l, g, :, block(3, width)] = stacked(w3)
            powers[l, g, :, block(4, width)] = st4
            powers[l, g, :, block(FINE_MAX + 1, width)] = stacked((w1 + w2) + (w3 + w4))
            for i in range(4):
                powers[l, g, :, block(5 + i, width)] = stacked(w58[i * width:(i + 1) * width])
            sums = [t + w for t, w in zip(sums, (w1, w2, w3, w4))]
            e6 = e6 + alive[g][2] * w1
            e7 = e7 + alive[g][3] * w1
            e72 = e72 + alive[g][3] * w2
        mats = [t * (per / everyone) for t in sums]
        mats += [e6 / everyone, (e6 + e72 - e7) / everyone, e7 / everyone]
        for i, m in enumerate(mats):
            at = slice(((l % half) * MATS + i) * width, ((l % half) * MATS + i + 1) * width)

            @pl.when(core == l // half)
            def _():
                own[at] = m

            @pl.when(core != l // half)
            def _():
                other[at] = m


def class_sums(state, k):
    mask = k >= (FINE_MIN + lax.broadcasted_iota(jnp.int32, (ROWS, k.shape[1]), 0))
    mask = mask.astype(F32)
    left = jnp.concatenate([mask, mask], axis=1)
    left = jnp.concatenate([left, jnp.zeros_like(left)], axis=0).astype(BF16)
    return jnp.dot(left, stacked(state), preferred_element_type=F32)[:ROWS]


def picked(products, first, width):
    out = jnp.zeros((ROWS, width), F32)
    for i in range(CLASSES):
        d = first + i
        if 1 <= d <= FINE_MAX:
            out = out + jnp.where(row_is(i, out.shape), products[:, block(d, width)], 0.0)
    return out


def sums_of_state(V, keep, powers, width):
    x = mul(V * keep, powers)
    rows = [V[0:1]] + [x[0:1, block(m, width)] for m in range(1, FINE_MIN + 1)]
    gain = picked(x, FINE_MIN, width) - picked(x, FINE_MIN - 1, width)
    for i in range(1, 4):
        rows.append(rows[-1] + gain[i:i + 1])
    return jnp.concatenate(rows, axis=0)


def sums_of_source(S, powers, width):
    x = mul(S, powers)
    rows = [jnp.zeros((1, width), F32)]
    for m in range(1, FINE_MAX):
        i = max(m - FINE_MIN, 0)
        rows.append(rows[-1] + x[i:i + 1, block(m, width)])
    return jnp.concatenate(rows, axis=0)


def by_count(products, k, first, width):
    out = jnp.zeros(k.shape, F32)
    for i in range(CLASSES):
        d = i * width
        out = jnp.where(k == float(FINE_MIN + i), products[:, d:d + width], out)
    return out


def base_kernel(everyone, sums, received, source_sums, coarse, powers, rate, base, ofsource):
    slices, groups, width, _ = coarse.shape
    keep = 1.0 - rate[...]
    states = [jnp.where(leading(), sums[g], received[g]) for g in range(groups)]
    for l in range(slices):
        rows, rows_source = 0.0, 0.0
        for g in range(groups):
            V, S, w = states[g], source_sums[l, g], powers[l, g, :, :FINE_MAX * width]
            rows = rows + sums_of_state(V, keep, w, width)
            rows_source = rows_source + sums_of_source(S, w, width)
            if l + 1 < slices:
                states[g] = mul(V + S, stacked(coarse[l, g]))
        rows_source = rows_source / everyone
        at = slice(l * ROWS, (l + 1) * ROWS)
        ofsource[at] = rows_source
        base[at] = rows / everyone + rows_source


def sweep_kernel(first, last, *refs):
    if first:
        initial, source, coarse, powers, rate, spread, *outs = refs
    else:
        initial, received, source, coarse, powers, rate, spread, *outs = refs
    slices, groups, width, _ = coarse.shape
    per = spread.shape[0] // groups
    keep = 1.0 - rate[...]
    for g in range(groups):
        here = group_rows(g, per)
        n = spread[here]
        start = initial[here]
        states = [start] * 3
        if not first:
            states = [jnp.where(leading(), start, received[i, here]) for i in range(3)]
        for l in range(slices):
            s = source[l, here]
            if last is not None:
                outs[0][l, g] = class_sums(states[1], last[g:g + 1])
            w = powers[l, g, :, FINE_MIN * width:]
            x = mul(s, w)
            total = x[:, FINE_MIN * width:]
            sourced = jnp.where(n == float(FINE_MIN), total, 0.0)
            for i in range(CLASSES - 1):
                total = total + x[:, i * width:(i + 1) * width]
                sourced = jnp.where(n == float(FINE_MIN + 1 + i), total, sourced)
            both = jnp.concatenate(states[:2], axis=0) * keep
            x = mul(both, powers[l, g, :, (FINE_MIN - 1) * width:FINE_MAX * width])
            moved = mul(
                jnp.concatenate(
                    [states[0] + s, states[1] - states[0], states[2] - states[1]], axis=0
                ),
                stacked(coarse[l, g]),
            )
            states = [
                moved[:per],
                sourced + by_count(x[:per], n, FINE_MIN, width) + moved[per:2 * per],
                sourced + by_count(x[per:], n, FINE_MIN, width) + moved[2 * per:],
            ]
            if last is not None:
                outs[1][l, here] = states[2]
        if last is None:
            for i in range(3):
                outs[0][i, here] = states[i]


def last_sweep_kernel(initial, received, source, coarse, powers, rate, counts, spread, *outs):
    sweep_kernel(False, counts, initial, received, source, coarse, powers, rate, spread, *outs)


def gather_kernel(parts, base, out):
    n, rows, _ = parts.shape
    total = parts[0]
    for p in range(1, n):
        total = total + parts[p]
    for p in range(n):
        out[p, :rows] = total
        out[p, rows:] = base[...]


def wide(row):
    return jnp.broadcast_to(row, (ROWS, row.shape[-1]))


def assembled(known, width):
    out = jnp.zeros((ROWS, width), F32)
    for m, a in enumerate(known):
        out = jnp.where(row_is(m, out.shape), a, out)
    return out


def first_averages(rows, mixing, rate, width):
    known, sent = [], []
    for m in range(FINE_MIN + 1):
        a = wide(rows[m:m + 1])
        for j in range(m):
            a = a + sent[j][:, block(m - j, width)]
        known.append(a)
        if m < FINE_MIN:
            sent.append(mul(a * rate, mixing[:, :(FINE_MIN - m) * width]))
    return assembled(known, width)


def folded(a, rate, powers, width):
    x = mul(a * rate, powers)
    out = jnp.zeros((2 * ROWS, width), F32)
    for d in range(1, FINE_MAX + 1):
        z = jnp.concatenate([x[:, block(d, width)], jnp.zeros((ROWS, width), F32)], axis=0)
        out = out + pltpu.roll(z, d, 0)
    return out


def second_rows(everyone, per, a, base, rate, powers, active, l, width):
    groups = powers.shape[1]
    rows = [0.0] * 3
    for g in range(groups):
        h = folded(a, rate, powers[l, g, :, :FINE_MAX * width], width)
        total = per * h[4:5]
        for i in range(1, 4):
            total = total + active[g, i:i + 1] * (h[4 + i:5 + i] - h[3 + i:4 + i])
            rows[i - 1] = rows[i - 1] + total
    at = l * ROWS + FINE_MIN + 1
    return [rows[i] / everyone + base[at + i:at + i + 1] for i in range(3)]


def send_rows(everyone, per, a, base, rate, powers, active, out, width):
    slices = powers.shape[0]
    rows = []
    for l in range(slices):
        rows += second_rows(everyone, per, a[l], base, rate, powers, active, l, width)
        rows.append(jnp.zeros((1, width), F32))
    rows = jnp.concatenate(rows, axis=0)
    for p in range(out.shape[0]):
        out[p] = rows


def mixing_kernel(everyone, per, mine, theirs, base, powers, rate, active,
                  mixing, averages, out, held):
    slices, _, _, wider = powers.shape
    width = wider // (FINE_MAX + 1)
    half = slices // 2
    n, rows, _ = mine.shape
    rows -= slices * ROWS
    core = lax.rem(lax.axis_index("cell"), 2)
    mixed = 0.0
    for ref, at in ((mine, core), (theirs, 1 - core)):
        for p in range(n):
            place = at * (half * MATS * width) + p * rows
            held[pl.ds(place, rows), :] = ref[p, :rows]
            mixed = mixed + ref[p, rows:]
    a = []
    for l in range(slices):
        for i in range(MATS):
            at = (l * MATS + i) * width
            mixing[l, :, block(i + 1, width)] = stacked(held[at:at + width])
        a.append(first_averages(mixed[l * ROWS:(l + 1) * ROWS], mixing[l], rate[...], width))
        averages[l] = a[-1]
    send_rows(everyone, per, a, base, rate[...], powers, active, out, width)


def first_kernel(everyone, per, received, base, mixing, powers, rate, active, averages, out):
    slices, _, _, wider = powers.shape
    width = wider // (FINE_MAX + 1)
    total = received[0]
    for p in range(1, received.shape[0]):
        total = total + received[p]
    a = []
    for l in range(slices):
        rows = total[l * (FINE_MIN + 1):(l + 1) * (FINE_MIN + 1)]
        a.append(first_averages(rows, mixing[l], rate[...], width))
        averages[l] = a[-1]
    send_rows(everyone, per, a, base, rate[...], powers, active, out, width)


def push_kernel(received, averages, mixing, powers, rate, coarse, *refs):
    if len(refs) == 2:
        plain, starts, (pushes, end) = None, None, refs
    else:
        plain, starts, pushes, end = refs
    slices, groups, _, wider = powers.shape
    width = wider // (FINE_MAX + 1)
    r = rate[...]
    total = received[0]
    for p in range(1, received.shape[0]):
        total = total + received[p]
    x = [jnp.zeros((ROWS, width), F32) for _ in range(groups)]
    for l in range(slices):
        a5 = wide(total[l * 4:l * 4 + 1])
        z = mul(a5 * r, mixing[l, :, 4 * width:6 * width])
        a6 = wide(total[l * 4 + 1:l * 4 + 2]) + z[:, :width]
        a7 = wide(total[l * 4 + 2:l * 4 + 3]) + z[:, width:]
        a7 = a7 + mul(a6 * r, mixing[l, :, 6 * width:])
        a = averages[l]
        for m, row in ((5, a5), (6, a6), (7, a7)):
            a = jnp.where(row_is(m, a.shape), row, a)
        for g in range(groups):
            h = folded(a, r, powers[l, g, :, :FINE_MAX * width], width)[FINE_MIN:FINE_MIN + ROWS]
            if plain is not None:
                h = h + plain[l, g]
            pushes[l, g] = h
            old = x[g] if starts is None else x[g] - starts[l, g]
            x[g] = h + mul(old, stacked(coarse[l, g]))
    for g in range(groups):
        end[g] = x[g]


def vectors_kernel(received, pushes, starts, coarse, end):
    slices, groups, _, _ = coarse.shape
    for g in range(groups):
        x = jnp.where(leading(), 0.0, received[g])
        for l in range(slices):
            x = pushes[l, g] + mul(x - starts[l, g], stacked(coarse[l, g]))
        end[g] = x


def second_kernel(everyone, received, pushes, coarse, sums, active, powers, rate, ofsource,
                  starts, base, out):
    slices, groups, width, _ = coarse.shape
    keep = 1.0 - rate[...]
    x = [jnp.where(leading(), 0.0, received[g]) for g in range(groups)]
    sent = []
    for l in range(slices):
        rows = 0.0
        for g in range(groups):
            starts[l, g] = x[g]
            n = active[g]
            exact = n - pltpu.roll(n, ROWS - 1, 0)
            exact = jnp.where(row_is(ROWS - 1, n.shape), 0.0, exact)
            weighted = exact * x[g]
            tail = jnp.zeros((1, width), F32)
            V = sums[l, g]
            for i in reversed(range(CLASSES)):
                tail = tail + weighted[i:i + 1]
                V = jnp.where(row_is(i, V.shape), V + tail, V)
            rows = rows + sums_of_state(V, keep, powers[l, g, :, :FINE_MAX * width], width)
            if l + 1 < slices:
                x[g] = pushes[l, g] + mul(x[g], stacked(coarse[l, g]))
        at = slice(l * ROWS, (l + 1) * ROWS)
        rows = rows / everyone + ofsource[at]
        base[at] = rows
        sent.append(rows[:FINE_MIN + 1])
    sent = jnp.concatenate(sent, axis=0)
    for p in range(out.shape[0]):
        out[p] = sent


def plain_kernel(starts, powers, rate, out):
    slices, groups, _, wider = powers.shape
    width = wider // (FINE_MAX + 1)
    keep = 1.0 - rate[...]
    for l in range(slices):
        for g in range(groups):
            out[l, g] = picked(mul(starts[l, g] * keep, powers[l, g, :, :FINE_MAX * width]), FINE_MIN, width)


def finish_kernel(received, pushes, starts, coarse, ends, counts, out):
    slices, groups, width, _ = coarse.shape
    per = counts.shape[1]
    for g in range(groups):
        here = group_rows(g, per)
        n = spread_counts(counts[g:g + 1])
        x = jnp.where(leading(), 0.0, received[g])
        for l in range(slices):
            x = pushes[l, g] + mul(x - starts[l, g], stacked(coarse[l, g]))
            add = jnp.zeros((per, width), F32)
            for i in range(CLASSES):
                add = jnp.where(n == float(FINE_MIN + i), x[i:i + 1], add)
            out[l, here] = ends[l, here] + add


def body(initial, source, mix_rate, fine, coarse, step_counts):
    slices, groups, width, _ = fine.shape
    cells = initial.shape[0]
    per = cells // groups
    n_cell = lax.axis_size("cell")
    turns = lax.axis_size("tm") - 1
    everyone = cells * n_cell
    half = slices // 2
    peers = n_cell // 2
    shard = half * MATS * width // peers
    rate = mix_rate.reshape(1, width)
    counts = step_counts.reshape(groups, per)
    state = shape(cells, width)
    states = shape(slices, cells, width)
    vectors = shape(slices, groups, ROWS, width)
    vector = shape(groups, ROWS, width)
    rows8 = shape(slices * ROWS, width)
    rows4 = shape(n_cell, slices * 4, width)
    averages = shape(slices, ROWS, width)

    mats = shape(half * MATS * width, width)
    own, other, powers, spread, active = call(
        functools.partial(setup_kernel, everyone), "setup",
        [
            mats, mats,
            shape(slices, groups, 2 * width, (FINE_MAX + 1) * width, dtype=BF16),
            state, vector,
        ],
        (fine, rate, counts),
    )
    sums0, source_sums, moved = call(
        lead_kernel, "lead", [vector, vectors, vector], (initial, source, coarse, counts)
    )
    for turn in range(turns):
        moved = from_behind(moved, "tm", 1)
        if turn + 1 < turns:
            moved, = call(relay_kernel, "relay", [vector], (sums0, moved, source_sums, coarse))
    mine = (own + swap_core(other)).reshape(peers, shard, width)
    parts = exchange(mine, same_core())
    base, ofsource = call(
        functools.partial(base_kernel, everyone), "base", [rows8, rows8],
        (sums0, moved, source_sums, coarse, powers, rate),
    )
    bundle = shape(3, cells, width)
    sent, = call(
        functools.partial(sweep_kernel, True, None), "sweep", [bundle],
        (initial, source, coarse, powers, rate, spread),
    )
    for turn in range(turns):
        sent = from_behind(sent, "tm", 1)
        if turn + 1 < turns:
            sent, = call(
                functools.partial(sweep_kernel, False, None), "sweep", [bundle],
                (initial, sent, source, coarse, powers, rate, spread),
            )
    payload, = call(
        gather_kernel, "gather", [shape(peers, shard + slices * ROWS, width)], (parts, base)
    )
    gathered = exchange(payload, same_core())
    sums, ends = call(
        last_sweep_kernel, "sweep", [vectors, states],
        (initial, sent, source, coarse, powers, rate, counts, spread),
    )
    theirs = swap_core(gathered)
    mixing, first, out = call(
        functools.partial(mixing_kernel, everyone, per), "mixing",
        [shape(slices, 2 * width, MATS * width, dtype=BF16), averages, rows4],
        (gathered, theirs, base, powers, rate, active),
        scratch=[pltpu.VMEM((slices * MATS * width, width), F32)],
    )
    pushes1, end = call(
        push_kernel, "push", [vectors, vector],
        (exchange(out), first, mixing, powers, rate, coarse),
    )
    nothing = jnp.zeros(vectors.shape, F32)
    moved = end
    for turn in range(turns):
        moved = from_behind(moved, "tm", 1)
        if turn + 1 < turns:
            moved, = call(vectors_kernel, "vectors", [vector], (moved, pushes1, nothing, coarse))
    moved1, base, out = call(
        functools.partial(second_kernel, everyone), "second",
        [vectors, rows8, shape(n_cell, slices * (FINE_MIN + 1), width)],
        (moved, pushes1, coarse, sums, active, powers, rate, ofsource),
    )
    got = exchange(out)
    plain, = call(plain_kernel, "plain", [vectors], (moved1, powers, rate))
    first, out = call(
        functools.partial(first_kernel, everyone, per), "first", [averages, rows4],
        (got, base, mixing, powers, rate, active),
    )
    pushes2, end = call(
        push_kernel, "push", [vectors, vector],
        (exchange(out), first, mixing, powers, rate, coarse, plain, moved1),
    )
    moved = end
    for turn in range(turns):
        moved = from_behind(moved, "tm", 1)
        if turn + 1 < turns:
            moved, = call(vectors_kernel, "vectors", [vector], (moved, pushes2, moved1, coarse))
    out, = call(
        finish_kernel, "finish", [states], (moved, pushes2, moved1, coarse, ends, counts)
    )
    return out


def solution(mesh):
    return jax.shard_map(
        body,
        mesh=mesh,
        in_specs=(
            P("cell", None),
            P("tm", "cell", None),
            P(),
            P("tm", "cell", None, None),
            P("tm", "cell", None, None),
            P("cell"),
        ),
        out_specs=P("tm", "cell", None),
        check_vma=False,
    )
```

```python
import functools

import jax
import jax.numpy as jnp
from jax import lax
from jax.experimental import pallas as pl
from jax.experimental.pallas import tpu as pltpu
from jax.sharding import PartitionSpec as P

FINE_MAX = 8
FINE_MIN = 4
CLASSES = FINE_MAX - FINE_MIN + 1
MATS = 7
ROWS = 8
COUNT_ROW = slice(6, 7)
RATE_ROW = slice(7, 8)
F32 = jnp.float32
BF16 = jnp.bfloat16


def high_low(x):
    high = x.astype(BF16).astype(F32)
    return high, x - high


def stacked(w):
    high, low = high_low(w)
    return jnp.concatenate([high, low], axis=0).astype(BF16)


def mul(x, w):
    rows = x.shape[0]
    high, low = high_low(x)
    left = jnp.concatenate([high, low], axis=0).astype(BF16)
    right = jnp.concatenate([high, jnp.zeros_like(low)], axis=0).astype(BF16)
    out = jnp.dot(jnp.concatenate([left, right], axis=1), w, preferred_element_type=F32)
    return out[:rows] + out[rows:]


def row_is(i, shape):
    return lax.broadcasted_iota(jnp.int32, shape, 0) == i


def leading():
    return lax.axis_index("tm") == 0


def from_behind(block, axis, distance):
    devices = range(lax.axis_size(axis))
    route = [(i - distance, i) for i in devices if i - distance in devices]
    return lax.ppermute(block, axis, route)


def swap_core(block):
    n = lax.axis_size("cell")
    return lax.ppermute(block, "cell", [(i, i ^ 1) for i in range(n)])


def near_size():
    n = lax.axis_size("cell")
    return 4 if n % 8 == 0 else n // 2


def near_groups():
    n, near = lax.axis_size("cell"), near_size()
    return [
        [at + core + 2 * i for i in range(near)]
        for at in range(0, n, 2 * near)
        for core in range(2)
    ]


def far_swap(block, distance):
    n = lax.axis_size("cell")
    return lax.ppermute(block, "cell", [(i, i ^ distance) for i in range(n)])


def exchange(block, groups=None):
    return lax.all_to_all(block, "cell", 0, 0, axis_index_groups=groups)


def call(kernel, name, outs, args, scratch=(), flops=0, space=pltpu.VMEM):
    size = sum(x.size * x.dtype.itemsize for x in args)
    size += sum(x.size * x.dtype.itemsize for x in outs)
    return pl.pallas_call(
        kernel,
        out_shape=outs,
        in_specs=[pl.BlockSpec(memory_space=space)] * len(args),
        out_specs=[pl.BlockSpec(memory_space=pltpu.VMEM)] * len(outs),
        scratch_shapes=list(scratch),
        compiler_params=pltpu.CompilerParams(vmem_limit_bytes=24 << 20),
        cost_estimate=pl.CostEstimate(flops=flops, bytes_accessed=size, transcendentals=0),
        name=name,
    )(*args)


def shape(*dims, dtype=F32):
    return jax.ShapeDtypeStruct(dims, dtype)


def group_rows(g, per):
    return slice(g * per, (g + 1) * per)


def block(d, width):
    return slice((d - 1) * width, d * width)


def spread_counts(row):
    per = row.shape[1]
    return jnp.broadcast_to(row.astype(F32), (per, per)).T


def relay_kernel(start, received, source_sums, coarse, end):
    slices, groups, _, _ = coarse.shape
    for g in range(groups):
        V = jnp.where(leading(), start[g], received[g])
        for l in range(slices):
            V = mul(V + source_sums[l, g], stacked(coarse[l, g]))
        end[g] = V


def setup_kernel(everyone, *refs):
    outside, refs = refs[:6], refs[6:]
    own, other, powers, spread, table, start_sums, source_sums, end = refs[:8]
    held, arrived = refs[8:14], refs[14]
    loads = [pltpu.make_async_copy(x, y, arrived.at[i]) for i, (x, y) in enumerate(zip(outside, held))]
    for load in loads:
        load.start()
    fine, rate, counts, initial, source, coarse = held
    slices, groups, width, _ = fine.shape
    per = counts.shape[1]
    half = slices // 2
    core = lax.rem(lax.axis_index("cell"), 2)
    for load in loads[:3]:
        load.wait()
    keep = 1.0 - rate[...]
    alive = []
    for g in range(groups):
        k = counts[g:g + 1].astype(F32)
        spread[group_rows(g, per)] = spread_counts(k)
        rows = [
            jnp.sum((k >= q).astype(F32), axis=1, keepdims=True)
            for q in range(FINE_MIN, FINE_MAX + 1)
        ]
        alive.append(rows)
        filled = jnp.zeros((ROWS, width), F32)
        for i, n in enumerate(rows + [None, k, rate[...]]):
            if n is not None:
                filled = jnp.where(row_is(i, filled.shape), n, filled)
        table[g] = filled
    for l in range(slices):
        sums = [0.0] * 4
        e6, e7, e72 = 0.0, 0.0, 0.0
        for g in range(groups):
            w1 = fine[l, g]
            st1 = stacked(w1)
            w2 = mul(w1 * keep, st1)
            st2 = stacked(w2)
            first = jnp.concatenate([w1, w2], axis=0)
            w34 = mul(first * keep, st2)
            w3, w4 = w34[:width], w34[width:]
            st4 = stacked(w4)
            w58 = mul(jnp.concatenate([first, w34], axis=0) * keep, st4)
            powers[l, g, :, block(1, width)] = st1
            powers[l, g, :, block(2, width)] = st2
            powers[l, g, :, block(3, width)] = stacked(w3)
            powers[l, g, :, block(4, width)] = st4
            powers[l, g, :, block(FINE_MAX + 1, width)] = stacked((w1 + w2) + (w3 + w4))
            for i in range(4):
                powers[l, g, :, block(5 + i, width)] = stacked(w58[i * width:(i + 1) * width])
            sums = [t + w for t, w in zip(sums, (w1, w2, w3, w4))]
            e6 = e6 + alive[g][2] * w1
            e7 = e7 + alive[g][3] * w1
            e72 = e72 + alive[g][3] * w2
        mats = [t * (per / everyone) for t in sums]
        mats += [e6 / everyone, (e6 + e72 - e7) / everyone, e7 / everyone]
        for i, m in enumerate(mats):
            at = slice(((l % half) * MATS + i) * width, ((l % half) * MATS + i + 1) * width)

            @pl.when(core == l // half)
            def _():
                own[at] = m

            @pl.when(core != l // half)
            def _():
                other[at] = m
    for load in loads[3:]:
        load.wait()
    for g in range(groups):
        here = group_rows(g, per)
        k = table[g, COUNT_ROW]
        V = class_sums(initial[here], k)
        start_sums[g] = V
        for l in range(slices):
            S = class_sums(source[l, here], k)
            source_sums[l, g] = S
            V = mul(V + S, stacked(coarse[l, g]))
        end[g] = V


def add_kernel(a, b, out):
    out[...] = a[...] + b[...]


def class_sums(state, k):
    least = (FINE_MIN + lax.broadcasted_iota(jnp.int32, (ROWS, k.shape[1]), 0)).astype(F32)
    mask = (k >= least).astype(F32)
    left = jnp.concatenate([mask, mask], axis=1)
    left = jnp.concatenate([left, jnp.zeros_like(left)], axis=0).astype(BF16)
    return jnp.dot(left, stacked(state), preferred_element_type=F32)[:ROWS]


def picked(products, first, width):
    out = jnp.zeros((ROWS, width), F32)
    for i in range(CLASSES):
        d = first + i
        if 1 <= d <= FINE_MAX:
            out = out + jnp.where(row_is(i, out.shape), products[:, block(d, width)], 0.0)
    return out


def sums_of_state(V, keep, powers, width):
    x = mul(V * keep, powers)
    rows = [V[0:1]] + [x[0:1, block(m, width)] for m in range(1, FINE_MIN + 1)]
    gain = picked(x, FINE_MIN, width) - picked(x, FINE_MIN - 1, width)
    for i in range(1, 4):
        rows.append(rows[-1] + gain[i:i + 1])
    return jnp.concatenate(rows, axis=0)


def sums_of_source(S, powers, width):
    x = mul(S, powers)
    rows = [jnp.zeros((1, width), F32)]
    for m in range(1, FINE_MAX):
        i = max(m - FINE_MIN, 0)
        rows.append(rows[-1] + x[i:i + 1, block(m, width)])
    return jnp.concatenate(rows, axis=0)


def by_count(products, k, first, width):
    out = jnp.zeros(k.shape, F32)
    for i in range(CLASSES):
        d = i * width
        out = jnp.where(k == float(FINE_MIN + i), products[:, d:d + width], out)
    return out


def base_kernel(everyone, sums, received, source_sums, coarse, powers, table, base, ofsource):
    slices, groups, width, _ = coarse.shape
    keep = 1.0 - table[0, RATE_ROW]
    states = [jnp.where(leading(), sums[g], received[g]) for g in range(groups)]
    for l in range(slices):
        rows, rows_source = 0.0, 0.0
        for g in range(groups):
            V, S, w = states[g], source_sums[l, g], powers[l, g, :, :FINE_MAX * width]
            rows = rows + sums_of_state(V, keep, w, width)
            rows_source = rows_source + sums_of_source(S, w, width)
            if l + 1 < slices:
                states[g] = mul(V + S, stacked(coarse[l, g]))
        rows_source = rows_source / everyone
        at = slice(l * ROWS, (l + 1) * ROWS)
        ofsource[at] = rows_source
        base[at] = rows / everyone + rows_source


def sweep_kernel(first, last, *refs):
    if first:
        initial, source, coarse, powers, table, spread, *outs = refs
    else:
        initial, received, source, coarse, powers, table, spread, *outs = refs
    slices, groups, width, _ = coarse.shape
    per = spread.shape[0] // groups
    keep = 1.0 - table[0, RATE_ROW]
    for g in range(groups):
        here = group_rows(g, per)
        n = spread[here]
        start = initial[here]
        states = [start] * 3
        if not first:
            states = [jnp.where(leading(), start, received[i, here]) for i in range(3)]
        for l in range(slices):
            s = source[l, here]
            if last:
                outs[0][l, g] = class_sums(states[1], table[g, COUNT_ROW])
            w = powers[l, g, :, FINE_MIN * width:]
            x = mul(s, w)
            total = x[:, FINE_MIN * width:]
            sourced = jnp.where(n == float(FINE_MIN), total, 0.0)
            for i in range(CLASSES - 1):
                total = total + x[:, i * width:(i + 1) * width]
                sourced = jnp.where(n == float(FINE_MIN + 1 + i), total, sourced)
            both = jnp.concatenate(states[:2], axis=0) * keep
            x = mul(both, powers[l, g, :, (FINE_MIN - 1) * width:FINE_MAX * width])
            moved = mul(
                jnp.concatenate(
                    [states[0] + s, states[1] - states[0], states[2] - states[1]], axis=0
                ),
                stacked(coarse[l, g]),
            )
            states = [
                moved[:per],
                sourced + by_count(x[:per], n, FINE_MIN, width) + moved[per:2 * per],
                sourced + by_count(x[per:], n, FINE_MIN, width) + moved[2 * per:],
            ]
            if last:
                outs[1][l, here] = states[2]
        if not last:
            for i in range(3):
                outs[0][i, here] = states[i]


def middle_kernel(parts, base, out):
    n, rows, _ = parts.shape
    total = parts[0]
    for p in range(1, n):
        total = total + parts[p]
    out[:rows] = total
    out[rows:] = base[...]


def gather_kernel(a, b, out):
    total = a[...] + b[...]
    for p in range(out.shape[0]):
        out[p] = total


def wide(row):
    return jnp.broadcast_to(row, (ROWS, row.shape[-1]))


def assembled(known, width):
    out = jnp.zeros((ROWS, width), F32)
    for m, a in enumerate(known):
        out = jnp.where(row_is(m, out.shape), a, out)
    return out


def first_averages(rows, mixing, rate, width):
    known, sent = [], []
    for m in range(FINE_MIN + 1):
        a = wide(rows[m:m + 1])
        for j in range(m):
            a = a + sent[j][:, block(m - j, width)]
        known.append(a)
        if m < FINE_MIN:
            sent.append(mul(a * rate, mixing[:, :(FINE_MIN - m) * width]))
    return assembled(known, width)


def shifted(products, width):
    out = jnp.zeros((2 * ROWS, width), F32)
    empty = jnp.zeros((ROWS, width), F32)
    for d in range(1, FINE_MAX + 1):
        z = jnp.concatenate([products[:, block(d, width)], empty], axis=0)
        out = out + pltpu.roll(z, d, 0)
    return out


def second_rows(everyone, per, a, base, rate, powers, active, l, width):
    groups = powers.shape[1]
    rows = [0.0] * 3
    for g in range(groups):
        h = shifted(mul(a * rate, powers[l, g, :, :FINE_MAX * width]), width)
        total = per * h[4:5]
        for i in range(1, 4):
            total = total + active[g, i:i + 1] * (h[4 + i:5 + i] - h[3 + i:4 + i])
            rows[i - 1] = rows[i - 1] + total
    at = l * ROWS + FINE_MIN + 1
    return [rows[i] / everyone + base[at + i:at + i + 1] for i in range(3)]


def send_rows(everyone, per, a, base, rate, powers, active, out, width):
    slices = powers.shape[0]
    rows = []
    for l in range(slices):
        rows += second_rows(everyone, per, a[l], base, rate, powers, active, l, width)
        rows.append(jnp.zeros((1, width), F32))
    rows = jnp.concatenate(rows, axis=0)
    for p in range(out.shape[0]):
        out[p] = rows


def mixing_kernel(everyone, per, mine, theirs, base, powers, table,
                  mixing, averages, out, held):
    slices, _, _, wider = powers.shape
    width = wider // (FINE_MAX + 1)
    half = slices // 2
    n, rows, _ = mine.shape
    rows -= slices * ROWS
    rate = table[0, RATE_ROW]
    core = lax.rem(lax.axis_index("cell"), 2)
    mixed = 0.0
    for ref, at in ((mine, core), (theirs, 1 - core)):
        for p in range(n):
            place = at * (half * MATS * width) + p * rows
            held[pl.ds(place, rows), :] = ref[p, :rows]
            mixed = mixed + ref[p, rows:]
    a = []
    for l in range(slices):
        for i in range(MATS):
            at = (l * MATS + i) * width
            mixing[l, :, block(i + 1, width)] = stacked(held[at:at + width])
        a.append(first_averages(mixed[l * ROWS:(l + 1) * ROWS], mixing[l], rate, width))
        averages[l] = a[-1]
    send_rows(everyone, per, a, base, rate, powers, table, out, width)


def first_kernel(everyone, per, received, base, mixing, powers, table, averages, out):
    slices, _, _, wider = powers.shape
    width = wider // (FINE_MAX + 1)
    rate = table[0, RATE_ROW]
    total = received[0]
    for p in range(1, received.shape[0]):
        total = total + received[p]
    a = []
    for l in range(slices):
        rows = total[l * (FINE_MIN + 1):(l + 1) * (FINE_MIN + 1)]
        a.append(first_averages(rows, mixing[l], rate, width))
        averages[l] = a[-1]
    send_rows(everyone, per, a, base, rate, powers, table, out, width)


def push_kernel(received, averages, mixing, powers, table, coarse, *refs):
    starts, (pushes, end) = (None, refs) if len(refs) == 2 else (refs[0], refs[1:])
    slices, groups, _, wider = powers.shape
    width = wider // (FINE_MAX + 1)
    r = table[0, RATE_ROW]
    total = received[0]
    for p in range(1, received.shape[0]):
        total = total + received[p]
    x = [jnp.zeros((ROWS, width), F32) for _ in range(groups)]
    for l in range(slices):
        a5 = wide(total[l * 4:l * 4 + 1])
        z = mul(a5 * r, mixing[l, :, 4 * width:6 * width])
        a6 = wide(total[l * 4 + 1:l * 4 + 2]) + z[:, :width]
        a7 = wide(total[l * 4 + 2:l * 4 + 3]) + z[:, width:]
        a7 = a7 + mul(a6 * r, mixing[l, :, 6 * width:])
        a = averages[l]
        for m, row in ((5, a5), (6, a6), (7, a7)):
            a = jnp.where(row_is(m, a.shape), row, a)
        for g in range(groups):
            w = powers[l, g, :, :FINE_MAX * width]
            if starts is None:
                h = shifted(mul(a * r, w), width)[FINE_MIN:FINE_MIN + ROWS]
                old = x[g]
            else:
                both = jnp.concatenate([a * r, starts[l, g] * (1.0 - r)], axis=0)
                z = mul(both, w)
                h = shifted(z[:ROWS], width)[FINE_MIN:FINE_MIN + ROWS]
                h = h + picked(z[ROWS:], FINE_MIN, width)
                old = x[g] - starts[l, g]
            pushes[l, g] = h
            x[g] = h + mul(old, stacked(coarse[l, g]))
    for g in range(groups):
        end[g] = x[g]


def vectors_kernel(received, pushes, starts, coarse, end):
    slices, groups, _, _ = coarse.shape
    for g in range(groups):
        x = jnp.where(leading(), 0.0, received[g])
        for l in range(slices):
            x = pushes[l, g] + mul(x - starts[l, g], stacked(coarse[l, g]))
        end[g] = x


def second_kernel(everyone, received, pushes, coarse, sums, table, powers, ofsource,
                  starts, base, out):
    slices, groups, width, _ = coarse.shape
    keep = 1.0 - table[0, RATE_ROW]
    x = [jnp.where(leading(), 0.0, received[g]) for g in range(groups)]
    sent = []
    for l in range(slices):
        rows = 0.0
        for g in range(groups):
            starts[l, g] = x[g]
            n = table[g]
            exact = n - pltpu.roll(n, ROWS - 1, 0)
            exact = jnp.where(row_is(ROWS - 1, n.shape), 0.0, exact)
            weighted = exact * x[g]
            tail = jnp.zeros((1, width), F32)
            V = sums[l, g]
            for i in reversed(range(CLASSES)):
                tail = tail + weighted[i:i + 1]
                V = jnp.where(row_is(i, V.shape), V + tail, V)
            rows = rows + sums_of_state(V, keep, powers[l, g, :, :FINE_MAX * width], width)
            if l + 1 < slices:
                x[g] = pushes[l, g] + mul(x[g], stacked(coarse[l, g]))
        at = slice(l * ROWS, (l + 1) * ROWS)
        rows = rows / everyone + ofsource[at]
        base[at] = rows
        sent.append(rows[:FINE_MIN + 1])
    sent = jnp.concatenate(sent, axis=0)
    for p in range(out.shape[0]):
        out[p] = sent


def finish_kernel(received, pushes, starts, coarse, ends, table, out):
    slices, groups, width, _ = coarse.shape
    per = ends.shape[1] // groups
    for g in range(groups):
        here = group_rows(g, per)
        n = spread_counts(table[g, COUNT_ROW])
        x = jnp.where(leading(), 0.0, received[g])
        for l in range(slices):
            x = pushes[l, g] + mul(x - starts[l, g], stacked(coarse[l, g]))
            add = jnp.zeros((per, width), F32)
            for i in range(CLASSES):
                add = jnp.where(n == float(FINE_MIN + i), x[i:i + 1], add)
            out[l, here] = ends[l, here] + add


def body(initial, source, mix_rate, fine, coarse, step_counts):
    slices, groups, width, _ = fine.shape
    cells = initial.shape[0]
    per = cells // groups
    n_cell = lax.axis_size("cell")
    turns = lax.axis_size("tm") - 1
    everyone = cells * n_cell
    half = slices // 2
    near = near_size()
    shard = half * MATS * width // near
    rate = mix_rate.reshape(1, width)
    counts = step_counts.reshape(groups, per)
    state = shape(cells, width)
    states = shape(slices, cells, width)
    vectors = shape(slices, groups, ROWS, width)
    vector = shape(groups, ROWS, width)
    rows8 = shape(slices * ROWS, width)
    rows4 = shape(n_cell, slices * 4, width)
    averages = shape(slices, ROWS, width)
    mats = shape(half * MATS * width, width)
    inputs = (fine, rate, counts, initial, source, coarse)
    own, other, powers, spread, table, sums0, source_sums, moved = call(
        functools.partial(setup_kernel, everyone), "setup",
        [
            mats, mats,
            shape(slices, groups, 2 * width, (FINE_MAX + 1) * width, dtype=BF16),
            state, vector, vector, vectors, vector,
        ],
        inputs,
        scratch=[pltpu.VMEM(x.shape, x.dtype) for x in inputs]
        + [pltpu.SemaphoreType.DMA((len(inputs),))],
        space=pltpu.HBM,
    )
    for turn in range(turns):
        moved = from_behind(moved, "tm", 1)
        if turn + 1 < turns:
            moved, = call(relay_kernel, "relay", [vector], (sums0, moved, source_sums, coarse))
    mine, = call(add_kernel, "add", [mats], (own, swap_core(other)))
    parts = exchange(mine.reshape(near, shard, width), near_groups())
    base, ofsource = call(
        functools.partial(base_kernel, everyone), "base", [rows8, rows8],
        (sums0, moved, source_sums, coarse, powers, table),
    )
    bundle = shape(3, cells, width)
    sent, = call(
        functools.partial(sweep_kernel, True, False), "sweep", [bundle],
        (initial, source, coarse, powers, table, spread),
    )
    for turn in range(turns):
        sent = from_behind(sent, "tm", 1)
        if turn + 1 < turns:
            sent, = call(
                functools.partial(sweep_kernel, False, False), "sweep", [bundle],
                (initial, sent, source, coarse, powers, table, spread),
            )
    block, = call(
        middle_kernel, "middle", [shape(shard + slices * ROWS, width)], (parts, base)
    )
    far = jnp.zeros_like(block)
    distance = 2 * near
    while distance < n_cell:
        far = far_swap(block, distance)
        distance *= 2
        if distance < n_cell:
            block = block + far
    payload, = call(
        gather_kernel, "gather", [shape(near, shard + slices * ROWS, width)], (block, far)
    )
    gathered = exchange(payload, near_groups())
    sums, ends = call(
        functools.partial(sweep_kernel, False, True), "sweep", [vectors, states],
        (initial, sent, source, coarse, powers, table, spread),
    )
    theirs = swap_core(gathered)
    mixing, first, out = call(
        functools.partial(mixing_kernel, everyone, per), "mixing",
        [shape(slices, 2 * width, MATS * width, dtype=BF16), averages, rows4],
        (gathered, theirs, base, powers, table),
        scratch=[pltpu.VMEM((slices * MATS * width, width), F32)],
    )
    pushes1, end = call(
        push_kernel, "push", [vectors, vector],
        (exchange(out), first, mixing, powers, table, coarse),
    )
    nothing = jnp.zeros(vectors.shape, F32)
    moved = end
    for turn in range(turns):
        moved = from_behind(moved, "tm", 1)
        if turn + 1 < turns:
            moved, = call(vectors_kernel, "vectors", [vector], (moved, pushes1, nothing, coarse))
    moved1, base, out = call(
        functools.partial(second_kernel, everyone), "second",
        [vectors, rows8, shape(n_cell, slices * (FINE_MIN + 1), width)],
        (moved, pushes1, coarse, sums, table, powers, ofsource),
    )
    first, out = call(
        functools.partial(first_kernel, everyone, per), "first", [averages, rows4],
        (exchange(out), base, mixing, powers, table),
    )
    pushes2, end = call(
        push_kernel, "push", [vectors, vector],
        (exchange(out), first, mixing, powers, table, coarse, moved1),
    )
    moved = end
    for turn in range(turns):
        moved = from_behind(moved, "tm", 1)
        if turn + 1 < turns:
            moved, = call(vectors_kernel, "vectors", [vector], (moved, pushes2, moved1, coarse))
    out, = call(
        finish_kernel, "finish", [states], (moved, pushes2, moved1, coarse, ends, table)
    )
    return out


def solution(mesh):
    return jax.shard_map(
        body,
        mesh=mesh,
        in_specs=(
            P("cell", None),
            P("tm", "cell", None),
            P(),
            P("tm", "cell", None, None),
            P("tm", "cell", None, None),
            P("cell"),
        ),
        out_specs=P("tm", "cell", None),
        check_vma=False,
    )
```

```python
import functools

import jax
import jax.numpy as jnp
from jax import lax
from jax.experimental import pallas as pl
from jax.experimental.pallas import tpu as pltpu
from jax.sharding import PartitionSpec as P

FINE_MAX = 8
FINE_MIN = 4
CLASSES = FINE_MAX - FINE_MIN + 1
MATS = 7
ROWS = 8
COUNT_ROW = slice(6, 7)
RATE_ROW = slice(7, 8)
F32 = jnp.float32
BF16 = jnp.bfloat16


def high_low(x):
    high = x.astype(BF16).astype(F32)
    return high, x - high


def stacked(w):
    high, low = high_low(w)
    return jnp.concatenate([high, low], axis=0).astype(BF16)


def mul(x, w):
    rows = x.shape[0]
    high, low = high_low(x)
    left = jnp.concatenate([high, low], axis=0).astype(BF16)
    right = jnp.concatenate([high, jnp.zeros_like(low)], axis=0).astype(BF16)
    out = jnp.dot(jnp.concatenate([left, right], axis=1), w, preferred_element_type=F32)
    return out[:rows] + out[rows:]


def row_is(i, shape):
    return lax.broadcasted_iota(jnp.int32, shape, 0) == i


def leading():
    return lax.axis_index("tm") == 0


def from_behind(block, axis, distance):
    devices = range(lax.axis_size(axis))
    route = [(i - distance, i) for i in devices if i - distance in devices]
    return lax.ppermute(block, axis, route)


def swap_core(block):
    n = lax.axis_size("cell")
    return lax.ppermute(block, "cell", [(i, i ^ 1) for i in range(n)])


def near_size():
    n = lax.axis_size("cell")
    return 4 if n % 8 == 0 else n // 2


def near_groups():
    n, near = lax.axis_size("cell"), near_size()
    return [
        [at + core + 2 * i for i in range(near)]
        for at in range(0, n, 2 * near)
        for core in range(2)
    ]


def far_swap(block, distance):
    n = lax.axis_size("cell")
    return lax.ppermute(block, "cell", [(i, i ^ distance) for i in range(n)])


def exchange(block, groups=None):
    return lax.all_to_all(block, "cell", 0, 0, axis_index_groups=groups)


def call(kernel, name, outs, args, scratch=(), flops=0):
    size = sum(x.size * x.dtype.itemsize for x in args)
    size += sum(x.size * x.dtype.itemsize for x in outs)
    return pl.pallas_call(
        kernel,
        out_shape=outs,
        in_specs=[pl.BlockSpec(memory_space=pltpu.VMEM)] * len(args),
        out_specs=[pl.BlockSpec(memory_space=pltpu.VMEM)] * len(outs),
        scratch_shapes=list(scratch),
        compiler_params=pltpu.CompilerParams(vmem_limit_bytes=24 << 20),
        cost_estimate=pl.CostEstimate(flops=flops, bytes_accessed=size, transcendentals=0),
        name=name,
    )(*args)


def shape(*dims, dtype=F32):
    return jax.ShapeDtypeStruct(dims, dtype)


def group_rows(g, per):
    return slice(g * per, (g + 1) * per)


def block(d, width):
    return slice((d - 1) * width, d * width)


def spread_counts(row):
    per = row.shape[1]
    return jnp.broadcast_to(row.astype(F32), (per, per)).T


def relay_kernel(start, received, source_sums, coarse, end):
    slices, groups, _, _ = coarse.shape
    for g in range(groups):
        V = jnp.where(leading(), start[g], received[g])
        for l in range(slices):
            V = mul(V + source_sums[l, g], stacked(coarse[l, g]))
        end[g] = V


def setup_kernel(everyone, fine, rate, counts, own, other, lows, table):
    slices, groups, width, _ = fine.shape
    per = counts.shape[1]
    half = slices // 2
    core = lax.rem(lax.axis_index("cell"), 2)
    keep = 1.0 - rate[...]
    alive = []
    for g in range(groups):
        k = counts[g:g + 1].astype(F32)
        rows = [
            jnp.sum((k >= q).astype(F32), axis=1, keepdims=True)
            for q in range(FINE_MIN, FINE_MAX + 1)
        ]
        alive.append(rows)
        filled = jnp.zeros((ROWS, width), F32)
        for i, n in enumerate(rows + [None, k, rate[...]]):
            if n is not None:
                filled = jnp.where(row_is(i, filled.shape), n, filled)
        table[g] = filled
    for l in range(slices):
        sums = [0.0] * 4
        e6, e7, e72 = 0.0, 0.0, 0.0
        for g in range(groups):
            w1 = fine[l, g]
            w2 = mul(w1 * keep, stacked(w1))
            first = jnp.concatenate([w1, w2], axis=0)
            w34 = mul(first * keep, stacked(w2))
            w3, w4 = w34[:width], w34[width:]
            lows[l, g, :2 * width] = first
            lows[l, g, 2 * width:] = w34
            sums = [t + w for t, w in zip(sums, (w1, w2, w3, w4))]
            e6 = e6 + alive[g][2] * w1
            e7 = e7 + alive[g][3] * w1
            e72 = e72 + alive[g][3] * w2
        mats = [t * (per / everyone) for t in sums]
        mats += [e6 / everyone, (e6 + e72 - e7) / everyone, e7 / everyone]
        for i, m in enumerate(mats):
            at = slice(((l % half) * MATS + i) * width, ((l % half) * MATS + i + 1) * width)

            @pl.when(core == l // half)
            def _():
                own[at] = m

            @pl.when(core != l // half)
            def _():
                other[at] = m


def extend_kernel(lows, table, powers):
    slices, groups, _, width = lows.shape
    keep = 1.0 - table[0, RATE_ROW]
    for l in range(slices):
        for g in range(groups):
            ws = [lows[l, g, i * width:(i + 1) * width] for i in range(4)]
            w58 = mul(lows[l, g] * keep, stacked(ws[3]))
            ws += [w58[i * width:(i + 1) * width] for i in range(4)]
            ws.append((ws[0] + ws[1]) + (ws[2] + ws[3]))
            for i, w in enumerate(ws):
                powers[l, g, :, block(i + 1, width)] = stacked(w)


def lead_kernel(table, initial, source, coarse, start_sums, source_sums, end):
    slices, groups, _, _ = coarse.shape
    per = initial.shape[0] // groups
    for g in range(groups):
        here = group_rows(g, per)
        k = table[g, COUNT_ROW]
        V = class_sums(initial[here], k)
        start_sums[g] = V
        for l in range(slices):
            S = class_sums(source[l, here], k)
            source_sums[l, g] = S
            V = mul(V + S, stacked(coarse[l, g]))
        end[g] = V


def add_kernel(a, b, out):
    out[...] = a[...] + b[...]


def class_sums(state, k):
    least = (FINE_MIN + lax.broadcasted_iota(jnp.int32, (ROWS, k.shape[1]), 0)).astype(F32)
    mask = (k >= least).astype(F32)
    left = jnp.concatenate([mask, mask], axis=1)
    left = jnp.concatenate([left, jnp.zeros_like(left)], axis=0).astype(BF16)
    return jnp.dot(left, stacked(state), preferred_element_type=F32)[:ROWS]


def picked(products, first, width):
    out = jnp.zeros((ROWS, width), F32)
    for i in range(CLASSES):
        d = first + i
        if 1 <= d <= FINE_MAX:
            out = out + jnp.where(row_is(i, out.shape), products[:, block(d, width)], 0.0)
    return out


def sums_of_state(V, keep, powers, width):
    x = mul(V * keep, powers)
    rows = [V[0:1]] + [x[0:1, block(m, width)] for m in range(1, FINE_MIN + 1)]
    gain = picked(x, FINE_MIN, width) - picked(x, FINE_MIN - 1, width)
    for i in range(1, 4):
        rows.append(rows[-1] + gain[i:i + 1])
    return jnp.concatenate(rows, axis=0)


def sums_of_source(S, powers, width):
    x = mul(S, powers)
    rows = [jnp.zeros((1, width), F32)]
    for m in range(1, FINE_MAX):
        i = max(m - FINE_MIN, 0)
        rows.append(rows[-1] + x[i:i + 1, block(m, width)])
    return jnp.concatenate(rows, axis=0)


def by_count(products, k, first, width):
    out = jnp.zeros(k.shape, F32)
    for i in range(CLASSES):
        d = i * width
        out = jnp.where(k == float(FINE_MIN + i), products[:, d:d + width], out)
    return out


def base_kernel(everyone, sums, received, source_sums, coarse, powers, table, base, ofsource):
    slices, groups, width, _ = coarse.shape
    keep = 1.0 - table[0, RATE_ROW]
    states = [jnp.where(leading(), sums[g], received[g]) for g in range(groups)]
    for l in range(slices):
        rows, rows_source = 0.0, 0.0
        for g in range(groups):
            V, S, w = states[g], source_sums[l, g], powers[l, g, :, :FINE_MAX * width]
            rows = rows + sums_of_state(V, keep, w, width)
            rows_source = rows_source + sums_of_source(S, w, width)
            if l + 1 < slices:
                states[g] = mul(V + S, stacked(coarse[l, g]))
        rows_source = rows_source / everyone
        at = slice(l * ROWS, (l + 1) * ROWS)
        ofsource[at] = rows_source
        base[at] = rows / everyone + rows_source


def sweep_kernel(first, last, *refs):
    if first:
        initial, source, coarse, powers, table, *outs = refs
    else:
        initial, received, source, coarse, powers, table, *outs = refs
    slices, groups, width, _ = coarse.shape
    per = initial.shape[0] // groups
    keep = 1.0 - table[0, RATE_ROW]
    for g in range(groups):
        here = group_rows(g, per)
        n = spread_counts(table[g, COUNT_ROW])
        start = initial[here]
        states = [start] * 3
        if not first:
            states = [jnp.where(leading(), start, received[i, here]) for i in range(3)]
        for l in range(slices):
            s = source[l, here]
            if last:
                outs[0][l, g] = class_sums(states[1], table[g, COUNT_ROW])
            w = powers[l, g, :, FINE_MIN * width:]
            x = mul(s, w)
            total = x[:, FINE_MIN * width:]
            sourced = jnp.where(n == float(FINE_MIN), total, 0.0)
            for i in range(CLASSES - 1):
                total = total + x[:, i * width:(i + 1) * width]
                sourced = jnp.where(n == float(FINE_MIN + 1 + i), total, sourced)
            both = jnp.concatenate(states[:2], axis=0) * keep
            x = mul(both, powers[l, g, :, (FINE_MIN - 1) * width:FINE_MAX * width])
            moved = mul(
                jnp.concatenate(
                    [states[0] + s, states[1] - states[0], states[2] - states[1]], axis=0
                ),
                stacked(coarse[l, g]),
            )
            states = [
                moved[:per],
                sourced + by_count(x[:per], n, FINE_MIN, width) + moved[per:2 * per],
                sourced + by_count(x[per:], n, FINE_MIN, width) + moved[2 * per:],
            ]
            if last:
                outs[1][l, here] = states[2]
        if not last:
            for i in range(3):
                outs[0][i, here] = states[i]


def middle_kernel(parts, base, out):
    n, rows, _ = parts.shape
    total = parts[0]
    for p in range(1, n):
        total = total + parts[p]
    out[:rows] = total
    out[rows:] = base[...]


def gather_kernel(a, b, out):
    total = a[...] + b[...]
    for p in range(out.shape[0]):
        out[p] = total


def wide(row):
    return jnp.broadcast_to(row, (ROWS, row.shape[-1]))


def assembled(known, width):
    out = jnp.zeros((ROWS, width), F32)
    for m, a in enumerate(known):
        out = jnp.where(row_is(m, out.shape), a, out)
    return out


def first_averages(rows, mixing, rate, width):
    known, sent = [], []
    for m in range(FINE_MIN + 1):
        a = wide(rows[m:m + 1])
        for j in range(m):
            a = a + sent[j][:, block(m - j, width)]
        known.append(a)
        if m < FINE_MIN:
            sent.append(mul(a * rate, mixing[:, :(FINE_MIN - m) * width]))
    return assembled(known, width)


def shifted(products, width):
    out = jnp.zeros((2 * ROWS, width), F32)
    empty = jnp.zeros((ROWS, width), F32)
    for d in range(1, FINE_MAX + 1):
        z = jnp.concatenate([products[:, block(d, width)], empty], axis=0)
        out = out + pltpu.roll(z, d, 0)
    return out


def second_rows(everyone, per, a, base, rate, powers, active, l, width):
    groups = powers.shape[1]
    rows = [0.0] * 3
    for g in range(groups):
        h = shifted(mul(a * rate, powers[l, g, :, :FINE_MAX * width]), width)
        total = per * h[4:5]
        for i in range(1, 4):
            total = total + active[g, i:i + 1] * (h[4 + i:5 + i] - h[3 + i:4 + i])
            rows[i - 1] = rows[i - 1] + total
    at = l * ROWS + FINE_MIN + 1
    return [rows[i] / everyone + base[at + i:at + i + 1] for i in range(3)]


def send_rows(everyone, per, a, base, rate, powers, active, out, width):
    slices = powers.shape[0]
    rows = []
    for l in range(slices):
        rows += second_rows(everyone, per, a[l], base, rate, powers, active, l, width)
        rows.append(jnp.zeros((1, width), F32))
    rows = jnp.concatenate(rows, axis=0)
    for p in range(out.shape[0]):
        out[p] = rows


def mixing_kernel(everyone, per, mine, theirs, base, powers, table,
                  mixing, averages, out, held):
    slices, _, _, wider = powers.shape
    width = wider // (FINE_MAX + 1)
    half = slices // 2
    n, rows, _ = mine.shape
    rows -= slices * ROWS
    rate = table[0, RATE_ROW]
    core = lax.rem(lax.axis_index("cell"), 2)
    mixed = 0.0
    for ref, at in ((mine, core), (theirs, 1 - core)):
        for p in range(n):
            place = at * (half * MATS * width) + p * rows
            held[pl.ds(place, rows), :] = ref[p, :rows]
            mixed = mixed + ref[p, rows:]
    a = []
    for l in range(slices):
        for i in range(MATS):
            at = (l * MATS + i) * width
            mixing[l, :, block(i + 1, width)] = stacked(held[at:at + width])
        a.append(first_averages(mixed[l * ROWS:(l + 1) * ROWS], mixing[l], rate, width))
        averages[l] = a[-1]
    send_rows(everyone, per, a, base, rate, powers, table, out, width)


def first_kernel(everyone, per, received, base, mixing, powers, table, averages, out):
    slices, _, _, wider = powers.shape
    width = wider // (FINE_MAX + 1)
    rate = table[0, RATE_ROW]
    total = received[0]
    for p in range(1, received.shape[0]):
        total = total + received[p]
    a = []
    for l in range(slices):
        rows = total[l * (FINE_MIN + 1):(l + 1) * (FINE_MIN + 1)]
        a.append(first_averages(rows, mixing[l], rate, width))
        averages[l] = a[-1]
    send_rows(everyone, per, a, base, rate, powers, table, out, width)


def push_kernel(received, averages, mixing, powers, table, coarse, *refs):
    starts, (pushes, end) = (None, refs) if len(refs) == 2 else (refs[0], refs[1:])
    slices, groups, _, wider = powers.shape
    width = wider // (FINE_MAX + 1)
    r = table[0, RATE_ROW]
    total = received[0]
    for p in range(1, received.shape[0]):
        total = total + received[p]
    x = [jnp.zeros((ROWS, width), F32) for _ in range(groups)]
    for l in range(slices):
        a5 = wide(total[l * 4:l * 4 + 1])
        z = mul(a5 * r, mixing[l, :, 4 * width:6 * width])
        a6 = wide(total[l * 4 + 1:l * 4 + 2]) + z[:, :width]
        a7 = wide(total[l * 4 + 2:l * 4 + 3]) + z[:, width:]
        a7 = a7 + mul(a6 * r, mixing[l, :, 6 * width:])
        a = averages[l]
        for m, row in ((5, a5), (6, a6), (7, a7)):
            a = jnp.where(row_is(m, a.shape), row, a)
        for g in range(groups):
            w = powers[l, g, :, :FINE_MAX * width]
            if starts is None:
                h = shifted(mul(a * r, w), width)[FINE_MIN:FINE_MIN + ROWS]
                old = x[g]
            else:
                both = jnp.concatenate([a * r, starts[l, g] * (1.0 - r)], axis=0)
                z = mul(both, w)
                h = shifted(z[:ROWS], width)[FINE_MIN:FINE_MIN + ROWS]
                h = h + picked(z[ROWS:], FINE_MIN, width)
                old = x[g] - starts[l, g]
            pushes[l, g] = h
            x[g] = h + mul(old, stacked(coarse[l, g]))
    for g in range(groups):
        end[g] = x[g]


def vectors_kernel(received, pushes, starts, coarse, end):
    slices, groups, _, _ = coarse.shape
    for g in range(groups):
        x = jnp.where(leading(), 0.0, received[g])
        for l in range(slices):
            x = pushes[l, g] + mul(x - starts[l, g], stacked(coarse[l, g]))
        end[g] = x


def second_kernel(everyone, received, pushes, coarse, sums, table, powers, ofsource,
                  starts, base, out):
    slices, groups, width, _ = coarse.shape
    keep = 1.0 - table[0, RATE_ROW]
    x = [jnp.where(leading(), 0.0, received[g]) for g in range(groups)]
    sent = []
    for l in range(slices):
        rows = 0.0
        for g in range(groups):
            starts[l, g] = x[g]
            n = table[g]
            exact = n - pltpu.roll(n, ROWS - 1, 0)
            exact = jnp.where(row_is(ROWS - 1, n.shape), 0.0, exact)
            weighted = exact * x[g]
            tail = jnp.zeros((1, width), F32)
            V = sums[l, g]
            for i in reversed(range(CLASSES)):
                tail = tail + weighted[i:i + 1]
                V = jnp.where(row_is(i, V.shape), V + tail, V)
            rows = rows + sums_of_state(V, keep, powers[l, g, :, :FINE_MAX * width], width)
            if l + 1 < slices:
                x[g] = pushes[l, g] + mul(x[g], stacked(coarse[l, g]))
        at = slice(l * ROWS, (l + 1) * ROWS)
        rows = rows / everyone + ofsource[at]
        base[at] = rows
        sent.append(rows[:FINE_MIN + 1])
    sent = jnp.concatenate(sent, axis=0)
    for p in range(out.shape[0]):
        out[p] = sent


def finish_kernel(received, pushes, starts, coarse, ends, table, out):
    slices, groups, width, _ = coarse.shape
    per = ends.shape[1] // groups
    for g in range(groups):
        here = group_rows(g, per)
        n = spread_counts(table[g, COUNT_ROW])
        x = jnp.where(leading(), 0.0, received[g])
        for l in range(slices):
            x = pushes[l, g] + mul(x - starts[l, g], stacked(coarse[l, g]))
            add = jnp.zeros((per, width), F32)
            for i in range(CLASSES):
                add = jnp.where(n == float(FINE_MIN + i), x[i:i + 1], add)
            out[l, here] = ends[l, here] + add


def body(initial, source, mix_rate, fine, coarse, step_counts):
    slices, groups, width, _ = fine.shape
    cells = initial.shape[0]
    per = cells // groups
    n_cell = lax.axis_size("cell")
    turns = lax.axis_size("tm") - 1
    everyone = cells * n_cell
    half = slices // 2
    near = near_size()
    shard = half * MATS * width // near
    rate = mix_rate.reshape(1, width)
    counts = step_counts.reshape(groups, per)
    state = shape(cells, width)
    states = shape(slices, cells, width)
    vectors = shape(slices, groups, ROWS, width)
    vector = shape(groups, ROWS, width)
    rows8 = shape(slices * ROWS, width)
    rows4 = shape(n_cell, slices * 4, width)
    averages = shape(slices, ROWS, width)
    mats = shape(half * MATS * width, width)
    own, other, lows, table = call(
        functools.partial(setup_kernel, everyone), "setup",
        [mats, mats, shape(slices, groups, 4 * width, width), vector],
        (fine, rate, counts),
    )
    swapped = swap_core(other)
    powers, = call(
        extend_kernel, "extend",
        [shape(slices, groups, 2 * width, (FINE_MAX + 1) * width, dtype=BF16)], (lows, table),
    )
    swapped, powers = lax.optimization_barrier((swapped, powers))
    sums0, source_sums, moved = call(
        lead_kernel, "lead", [vector, vectors, vector], (table, initial, source, coarse)
    )
    for turn in range(turns):
        moved = from_behind(moved, "tm", 1)
        if turn + 1 < turns:
            moved, = call(relay_kernel, "relay", [vector], (sums0, moved, source_sums, coarse))
    mine, = call(add_kernel, "add", [mats], (own, swapped))
    parts = exchange(mine.reshape(near, shard, width), near_groups())
    base, ofsource = call(
        functools.partial(base_kernel, everyone), "base", [rows8, rows8],
        (sums0, moved, source_sums, coarse, powers, table),
    )
    block, = call(
        middle_kernel, "middle", [shape(shard + slices * ROWS, width)], (parts, base)
    )
    block, later = lax.optimization_barrier((block, initial))
    bundle = shape(3, cells, width)
    sent, = call(
        functools.partial(sweep_kernel, True, False), "sweep", [bundle],
        (later, source, coarse, powers, table),
    )
    far = jnp.zeros_like(block)
    distance = 2 * near
    while distance < n_cell:
        far = far_swap(block, distance)
        distance *= 2
        if distance < n_cell:
            block = block + far
    far, sent = lax.optimization_barrier((far, sent))
    for turn in range(turns):
        sent = from_behind(sent, "tm", 1)
        if turn + 1 < turns:
            sent, = call(
                functools.partial(sweep_kernel, False, False), "sweep", [bundle],
                (initial, sent, source, coarse, powers, table),
            )
    payload, = call(
        gather_kernel, "gather", [shape(near, shard + slices * ROWS, width)], (block, far)
    )
    gathered = exchange(payload, near_groups())
    sums, ends = call(
        functools.partial(sweep_kernel, False, True), "sweep", [vectors, states],
        (initial, sent, source, coarse, powers, table),
    )
    theirs = swap_core(gathered)
    mixing, first, out = call(
        functools.partial(mixing_kernel, everyone, per), "mixing",
        [shape(slices, 2 * width, MATS * width, dtype=BF16), averages, rows4],
        (gathered, theirs, base, powers, table),
        scratch=[pltpu.VMEM((slices * MATS * width, width), F32)],
    )
    pushes1, end = call(
        push_kernel, "push", [vectors, vector],
        (exchange(out), first, mixing, powers, table, coarse),
    )
    nothing = jnp.zeros(vectors.shape, F32)
    moved = end
    for turn in range(turns):
        moved = from_behind(moved, "tm", 1)
        if turn + 1 < turns:
            moved, = call(vectors_kernel, "vectors", [vector], (moved, pushes1, nothing, coarse))
    moved1, base, out = call(
        functools.partial(second_kernel, everyone), "second",
        [vectors, rows8, shape(n_cell, slices * (FINE_MIN + 1), width)],
        (moved, pushes1, coarse, sums, table, powers, ofsource),
    )
    first, out = call(
        functools.partial(first_kernel, everyone, per), "first", [averages, rows4],
        (exchange(out), base, mixing, powers, table),
    )
    pushes2, end = call(
        push_kernel, "push", [vectors, vector],
        (exchange(out), first, mixing, powers, table, coarse, moved1),
    )
    moved = end
    for turn in range(turns):
        moved = from_behind(moved, "tm", 1)
        if turn + 1 < turns:
            moved, = call(vectors_kernel, "vectors", [vector], (moved, pushes2, moved1, coarse))
    out, = call(
        finish_kernel, "finish", [states], (moved, pushes2, moved1, coarse, ends, table)
    )
    return out


def solution(mesh):
    return jax.shard_map(
        body,
        mesh=mesh,
        in_specs=(
            P("cell", None),
            P("tm", "cell", None),
            P(),
            P("tm", "cell", None, None),
            P("tm", "cell", None, None),
            P("cell"),
        ),
        out_specs=P("tm", "cell", None),
        check_vma=False,
    )
```

```python
import functools

import jax
import jax.numpy as jnp
from jax import lax
from jax.experimental import pallas as pl
from jax.experimental.pallas import tpu as pltpu
from jax.sharding import PartitionSpec as P

FINE_MAX = 8
FINE_MIN = 4
CLASSES = FINE_MAX - FINE_MIN + 1
MATS = 7
ROWS = 8
OPENING_FLOPS = 10**9
COUNT_ROW = slice(6, 7)
RATE_ROW = slice(7, 8)
F32 = jnp.float32
BF16 = jnp.bfloat16


def high_low(x):
    high = x.astype(BF16).astype(F32)
    return high, x - high


def stacked(w):
    high, low = high_low(w)
    return jnp.concatenate([high, low], axis=0).astype(BF16)


def mul(x, w):
    rows = x.shape[0]
    high, low = high_low(x)
    left = jnp.concatenate([high, low], axis=0).astype(BF16)
    right = jnp.concatenate([high, jnp.zeros_like(low)], axis=0).astype(BF16)
    out = jnp.dot(jnp.concatenate([left, right], axis=1), w, preferred_element_type=F32)
    return out[:rows] + out[rows:]


def row_is(i, shape):
    return lax.broadcasted_iota(jnp.int32, shape, 0) == i


def leading():
    return lax.axis_index("tm") == 0


def from_behind(block, axis, distance):
    devices = range(lax.axis_size(axis))
    route = [(i - distance, i) for i in devices if i - distance in devices]
    return lax.ppermute(block, axis, route)


def swap_core(block):
    n = lax.axis_size("cell")
    return lax.ppermute(block, "cell", [(i, i ^ 1) for i in range(n)])


def near_size():
    n = lax.axis_size("cell")
    return 4 if n % 8 == 0 else n // 2


def near_groups():
    n, near = lax.axis_size("cell"), near_size()
    return [
        [at + core + 2 * i for i in range(near)]
        for at in range(0, n, 2 * near)
        for core in range(2)
    ]


def far_swap(block, distance):
    n = lax.axis_size("cell")
    return lax.ppermute(block, "cell", [(i, i ^ distance) for i in range(n)])


def exchange(block, groups=None):
    return lax.all_to_all(block, "cell", 0, 0, axis_index_groups=groups)


def call(kernel, name, outs, args, scratch=(), flops=0):
    size = sum(x.size * x.dtype.itemsize for x in args)
    size += sum(x.size * x.dtype.itemsize for x in outs)
    return pl.pallas_call(
        kernel,
        out_shape=outs,
        in_specs=[pl.BlockSpec(memory_space=pltpu.VMEM)] * len(args),
        out_specs=[pl.BlockSpec(memory_space=pltpu.VMEM)] * len(outs),
        scratch_shapes=list(scratch),
        compiler_params=pltpu.CompilerParams(vmem_limit_bytes=24 << 20),
        cost_estimate=pl.CostEstimate(flops=flops, bytes_accessed=size, transcendentals=0),
        name=name,
    )(*args)


def shape(*dims, dtype=F32):
    return jax.ShapeDtypeStruct(dims, dtype)


def group_rows(g, per):
    return slice(g * per, (g + 1) * per)


def block(d, width):
    return slice((d - 1) * width, d * width)


def spread_counts(row):
    per = row.shape[1]
    return jnp.broadcast_to(row.astype(F32), (per, per)).T


def relay_kernel(start, received, source_sums, coarse, end):
    slices, groups, _, _ = coarse.shape
    for g in range(groups):
        V = jnp.where(leading(), start[g], received[g])
        for l in range(slices):
            V = mul(V + source_sums[l, g], stacked(coarse[l, g]))
        end[g] = V


def opening_kernel(out):
    out[...] = jnp.zeros_like(out)


def setup_kernel(everyone, fine, rate, counts, opened, own, other, lows, table):
    slices, groups, width, _ = fine.shape
    per = counts.shape[1]
    half = slices // 2
    core = lax.rem(lax.axis_index("cell"), 2)
    keep = 1.0 - rate[...]
    alive = []
    for g in range(groups):
        k = counts[g:g + 1].astype(F32)
        rows = [
            jnp.sum((k >= q).astype(F32), axis=1, keepdims=True)
            for q in range(FINE_MIN, FINE_MAX + 1)
        ]
        alive.append(rows)
        filled = jnp.zeros((ROWS, width), F32)
        for i, n in enumerate(rows + [None, k, rate[...]]):
            if n is not None:
                filled = jnp.where(row_is(i, filled.shape), n, filled)
        table[g] = filled
    for l in range(slices):
        sums = [0.0] * 4
        e6, e7, e72 = 0.0, 0.0, 0.0
        for g in range(groups):
            w1 = fine[l, g]
            w2 = mul(w1 * keep, stacked(w1))
            first = jnp.concatenate([w1, w2], axis=0)
            w34 = mul(first * keep, stacked(w2))
            w3, w4 = w34[:width], w34[width:]
            lows[l, g, :2 * width] = first
            lows[l, g, 2 * width:] = w34
            sums = [t + w for t, w in zip(sums, (w1, w2, w3, w4))]
            e6 = e6 + alive[g][2] * w1
            e7 = e7 + alive[g][3] * w1
            e72 = e72 + alive[g][3] * w2
        mats = [t * (per / everyone) for t in sums]
        mats += [e6 / everyone, (e6 + e72 - e7) / everyone, e7 / everyone]
        for i, m in enumerate(mats):
            at = slice(((l % half) * MATS + i) * width, ((l % half) * MATS + i + 1) * width)

            @pl.when(core == l // half)
            def _():
                own[at] = m

            @pl.when(core != l // half)
            def _():
                other[at] = m


def extend_kernel(lows, table, powers):
    slices, groups, _, width = lows.shape
    keep = 1.0 - table[0, RATE_ROW]
    for l in range(slices):
        for g in range(groups):
            ws = [lows[l, g, i * width:(i + 1) * width] for i in range(4)]
            w58 = mul(lows[l, g] * keep, stacked(ws[3]))
            ws += [w58[i * width:(i + 1) * width] for i in range(4)]
            ws.append((ws[0] + ws[1]) + (ws[2] + ws[3]))
            for i, w in enumerate(ws):
                powers[l, g, :, block(i + 1, width)] = stacked(w)


def lead_kernel(table, initial, source, coarse, start_sums, source_sums, end):
    slices, groups, _, _ = coarse.shape
    per = initial.shape[0] // groups
    for g in range(groups):
        here = group_rows(g, per)
        k = table[g, COUNT_ROW]
        V = class_sums(initial[here], k)
        start_sums[g] = V
        for l in range(slices):
            S = class_sums(source[l, here], k)
            source_sums[l, g] = S
            V = mul(V + S, stacked(coarse[l, g]))
        end[g] = V


def add_kernel(a, b, out):
    out[...] = a[...] + b[...]


def class_sums(state, k):
    least = (FINE_MIN + lax.broadcasted_iota(jnp.int32, (ROWS, k.shape[1]), 0)).astype(F32)
    mask = (k >= least).astype(F32)
    left = jnp.concatenate([mask, mask], axis=1)
    left = jnp.concatenate([left, jnp.zeros_like(left)], axis=0).astype(BF16)
    return jnp.dot(left, stacked(state), preferred_element_type=F32)[:ROWS]


def picked(products, first, width):
    out = jnp.zeros((ROWS, width), F32)
    for i in range(CLASSES):
        d = first + i
        if 1 <= d <= FINE_MAX:
            out = out + jnp.where(row_is(i, out.shape), products[:, block(d, width)], 0.0)
    return out


def sums_of_state(V, keep, powers, width):
    x = mul(V * keep, powers)
    rows = [V[0:1]] + [x[0:1, block(m, width)] for m in range(1, FINE_MIN + 1)]
    gain = picked(x, FINE_MIN, width) - picked(x, FINE_MIN - 1, width)
    for i in range(1, 4):
        rows.append(rows[-1] + gain[i:i + 1])
    return jnp.concatenate(rows, axis=0)


def sums_of_source(S, powers, width):
    x = mul(S, powers)
    rows = [jnp.zeros((1, width), F32)]
    for m in range(1, FINE_MAX):
        i = max(m - FINE_MIN, 0)
        rows.append(rows[-1] + x[i:i + 1, block(m, width)])
    return jnp.concatenate(rows, axis=0)


def by_count(products, k, first, width):
    out = jnp.zeros(k.shape, F32)
    for i in range(CLASSES):
        d = i * width
        out = jnp.where(k == float(FINE_MIN + i), products[:, d:d + width], out)
    return out


def base_kernel(everyone, sums, received, source_sums, coarse, powers, table, base, ofsource):
    slices, groups, width, _ = coarse.shape
    keep = 1.0 - table[0, RATE_ROW]
    states = [jnp.where(leading(), sums[g], received[g]) for g in range(groups)]
    for l in range(slices):
        rows, rows_source = 0.0, 0.0
        for g in range(groups):
            V, S, w = states[g], source_sums[l, g], powers[l, g, :, :FINE_MAX * width]
            rows = rows + sums_of_state(V, keep, w, width)
            rows_source = rows_source + sums_of_source(S, w, width)
            if l + 1 < slices:
                states[g] = mul(V + S, stacked(coarse[l, g]))
        rows_source = rows_source / everyone
        at = slice(l * ROWS, (l + 1) * ROWS)
        ofsource[at] = rows_source
        base[at] = rows / everyone + rows_source


def sweep_kernel(first, last, *refs):
    if first:
        initial, source, coarse, powers, table, *outs = refs
    else:
        initial, received, source, coarse, powers, table, *outs = refs
    slices, groups, width, _ = coarse.shape
    per = initial.shape[0] // groups
    keep = 1.0 - table[0, RATE_ROW]
    for g in range(groups):
        here = group_rows(g, per)
        n = spread_counts(table[g, COUNT_ROW])
        start = initial[here]
        states = [start] * 3
        if not first:
            states = [jnp.where(leading(), start, received[i, here]) for i in range(3)]
        for l in range(slices):
            s = source[l, here]
            if last:
                outs[0][l, g] = class_sums(states[1], table[g, COUNT_ROW])
            w = powers[l, g, :, FINE_MIN * width:]
            x = mul(s, w)
            total = x[:, FINE_MIN * width:]
            sourced = jnp.where(n == float(FINE_MIN), total, 0.0)
            for i in range(CLASSES - 1):
                total = total + x[:, i * width:(i + 1) * width]
                sourced = jnp.where(n == float(FINE_MIN + 1 + i), total, sourced)
            both = jnp.concatenate(states[:2], axis=0) * keep
            x = mul(both, powers[l, g, :, (FINE_MIN - 1) * width:FINE_MAX * width])
            moved = mul(
                jnp.concatenate(
                    [states[0] + s, states[1] - states[0], states[2] - states[1]], axis=0
                ),
                stacked(coarse[l, g]),
            )
            states = [
                moved[:per],
                sourced + by_count(x[:per], n, FINE_MIN, width) + moved[per:2 * per],
                sourced + by_count(x[per:], n, FINE_MIN, width) + moved[2 * per:],
            ]
            if last:
                outs[1][l, here] = states[2]
        if not last:
            for i in range(3):
                outs[0][i, here] = states[i]


def middle_kernel(parts, base, out):
    n, rows, _ = parts.shape
    total = parts[0]
    for p in range(1, n):
        total = total + parts[p]
    out[:rows] = total
    out[rows:] = base[...]


def gather_kernel(a, b, out):
    total = a[...] + b[...]
    for p in range(out.shape[0]):
        out[p] = total


def wide(row):
    return jnp.broadcast_to(row, (ROWS, row.shape[-1]))


def assembled(known, width):
    out = jnp.zeros((ROWS, width), F32)
    for m, a in enumerate(known):
        out = jnp.where(row_is(m, out.shape), a, out)
    return out


def first_averages(rows, mixing, rate, width):
    known, sent = [], []
    for m in range(FINE_MIN + 1):
        a = wide(rows[m:m + 1])
        for j in range(m):
            a = a + sent[j][:, block(m - j, width)]
        known.append(a)
        if m < FINE_MIN:
            sent.append(mul(a * rate, mixing[:, :(FINE_MIN - m) * width]))
    return assembled(known, width)


def shifted(products, width):
    out = jnp.zeros((2 * ROWS, width), F32)
    empty = jnp.zeros((ROWS, width), F32)
    for d in range(1, FINE_MAX + 1):
        z = jnp.concatenate([products[:, block(d, width)], empty], axis=0)
        out = out + pltpu.roll(z, d, 0)
    return out


def second_rows(everyone, per, a, base, rate, powers, active, l, width):
    groups = powers.shape[1]
    rows = [0.0] * 3
    for g in range(groups):
        h = shifted(mul(a * rate, powers[l, g, :, :FINE_MAX * width]), width)
        total = per * h[4:5]
        for i in range(1, 4):
            total = total + active[g, i:i + 1] * (h[4 + i:5 + i] - h[3 + i:4 + i])
            rows[i - 1] = rows[i - 1] + total
    at = l * ROWS + FINE_MIN + 1
    return [rows[i] / everyone + base[at + i:at + i + 1] for i in range(3)]


def send_rows(everyone, per, a, base, rate, powers, active, out, width):
    slices = powers.shape[0]
    rows = []
    for l in range(slices):
        rows += second_rows(everyone, per, a[l], base, rate, powers, active, l, width)
        rows.append(jnp.zeros((1, width), F32))
    rows = jnp.concatenate(rows, axis=0)
    for p in range(out.shape[0]):
        out[p] = rows


def mixing_kernel(everyone, per, mine, theirs, base, powers, table,
                  mixing, averages, out, held):
    slices, _, _, wider = powers.shape
    width = wider // (FINE_MAX + 1)
    half = slices // 2
    n, rows, _ = mine.shape
    rows -= slices * ROWS
    rate = table[0, RATE_ROW]
    core = lax.rem(lax.axis_index("cell"), 2)
    mixed = 0.0
    for ref, at in ((mine, core), (theirs, 1 - core)):
        for p in range(n):
            place = at * (half * MATS * width) + p * rows
            held[pl.ds(place, rows), :] = ref[p, :rows]
            mixed = mixed + ref[p, rows:]
    a = []
    for l in range(slices):
        for i in range(MATS):
            at = (l * MATS + i) * width
            mixing[l, :, block(i + 1, width)] = stacked(held[at:at + width])
        a.append(first_averages(mixed[l * ROWS:(l + 1) * ROWS], mixing[l], rate, width))
        averages[l] = a[-1]
    send_rows(everyone, per, a, base, rate, powers, table, out, width)


def first_kernel(everyone, per, received, base, mixing, powers, table, averages, out):
    slices, _, _, wider = powers.shape
    width = wider // (FINE_MAX + 1)
    rate = table[0, RATE_ROW]
    total = received[0]
    for p in range(1, received.shape[0]):
        total = total + received[p]
    a = []
    for l in range(slices):
        rows = total[l * (FINE_MIN + 1):(l + 1) * (FINE_MIN + 1)]
        a.append(first_averages(rows, mixing[l], rate, width))
        averages[l] = a[-1]
    send_rows(everyone, per, a, base, rate, powers, table, out, width)


def push_kernel(received, averages, mixing, powers, table, coarse, *refs):
    starts, (pushes, end) = (None, refs) if len(refs) == 2 else (refs[0], refs[1:])
    slices, groups, _, wider = powers.shape
    width = wider // (FINE_MAX + 1)
    r = table[0, RATE_ROW]
    total = received[0]
    for p in range(1, received.shape[0]):
        total = total + received[p]
    x = [jnp.zeros((ROWS, width), F32) for _ in range(groups)]
    for l in range(slices):
        a5 = wide(total[l * 4:l * 4 + 1])
        z = mul(a5 * r, mixing[l, :, 4 * width:6 * width])
        a6 = wide(total[l * 4 + 1:l * 4 + 2]) + z[:, :width]
        a7 = wide(total[l * 4 + 2:l * 4 + 3]) + z[:, width:]
        a7 = a7 + mul(a6 * r, mixing[l, :, 6 * width:])
        a = averages[l]
        for m, row in ((5, a5), (6, a6), (7, a7)):
            a = jnp.where(row_is(m, a.shape), row, a)
        for g in range(groups):
            w = powers[l, g, :, :FINE_MAX * width]
            if starts is None:
                h = shifted(mul(a * r, w), width)[FINE_MIN:FINE_MIN + ROWS]
                old = x[g]
            else:
                both = jnp.concatenate([a * r, starts[l, g] * (1.0 - r)], axis=0)
                z = mul(both, w)
                h = shifted(z[:ROWS], width)[FINE_MIN:FINE_MIN + ROWS]
                h = h + picked(z[ROWS:], FINE_MIN, width)
                old = x[g] - starts[l, g]
            pushes[l, g] = h
            x[g] = h + mul(old, stacked(coarse[l, g]))
    for g in range(groups):
        end[g] = x[g]


def vectors_kernel(received, pushes, starts, coarse, end):
    slices, groups, _, _ = coarse.shape
    for g in range(groups):
        x = jnp.where(leading(), 0.0, received[g])
        for l in range(slices):
            x = pushes[l, g] + mul(x - starts[l, g], stacked(coarse[l, g]))
        end[g] = x


def second_kernel(everyone, received, pushes, coarse, sums, table, powers, ofsource,
                  starts, base, out):
    slices, groups, width, _ = coarse.shape
    keep = 1.0 - table[0, RATE_ROW]
    x = [jnp.where(leading(), 0.0, received[g]) for g in range(groups)]
    sent = []
    for l in range(slices):
        rows = 0.0
        for g in range(groups):
            starts[l, g] = x[g]
            n = table[g]
            exact = n - pltpu.roll(n, ROWS - 1, 0)
            exact = jnp.where(row_is(ROWS - 1, n.shape), 0.0, exact)
            weighted = exact * x[g]
            tail = jnp.zeros((1, width), F32)
            V = sums[l, g]
            for i in reversed(range(CLASSES)):
                tail = tail + weighted[i:i + 1]
                V = jnp.where(row_is(i, V.shape), V + tail, V)
            rows = rows + sums_of_state(V, keep, powers[l, g, :, :FINE_MAX * width], width)
            if l + 1 < slices:
                x[g] = pushes[l, g] + mul(x[g], stacked(coarse[l, g]))
        at = slice(l * ROWS, (l + 1) * ROWS)
        rows = rows / everyone + ofsource[at]
        base[at] = rows
        sent.append(rows[:FINE_MIN + 1])
    sent = jnp.concatenate(sent, axis=0)
    for p in range(out.shape[0]):
        out[p] = sent


def finish_kernel(received, pushes, starts, coarse, ends, table, out):
    slices, groups, width, _ = coarse.shape
    per = ends.shape[1] // groups
    for g in range(groups):
        here = group_rows(g, per)
        n = spread_counts(table[g, COUNT_ROW])
        x = jnp.where(leading(), 0.0, received[g])
        for l in range(slices):
            x = pushes[l, g] + mul(x - starts[l, g], stacked(coarse[l, g]))
            add = jnp.zeros((per, width), F32)
            for i in range(CLASSES):
                add = jnp.where(n == float(FINE_MIN + i), x[i:i + 1], add)
            out[l, here] = ends[l, here] + add


def body(initial, source, mix_rate, fine, coarse, step_counts):
    slices, groups, width, _ = fine.shape
    cells = initial.shape[0]
    per = cells // groups
    n_cell = lax.axis_size("cell")
    turns = lax.axis_size("tm") - 1
    everyone = cells * n_cell
    half = slices // 2
    near = near_size()
    shard = half * MATS * width // near
    rate = mix_rate.reshape(1, width)
    counts = step_counts.reshape(groups, per)
    state = shape(cells, width)
    states = shape(slices, cells, width)
    vectors = shape(slices, groups, ROWS, width)
    vector = shape(groups, ROWS, width)
    rows8 = shape(slices * ROWS, width)
    rows4 = shape(n_cell, slices * 4, width)
    averages = shape(slices, ROWS, width)
    mats = shape(half * MATS * width, width)
    opened, = call(opening_kernel, "opening", [shape(ROWS, width)], (), flops=OPENING_FLOPS)
    own, other, lows, table = call(
        functools.partial(setup_kernel, everyone), "setup",
        [mats, mats, shape(slices, groups, 4 * width, width), vector],
        (fine, rate, counts, opened),
    )
    swapped = swap_core(other)
    powers, = call(
        extend_kernel, "extend",
        [shape(slices, groups, 2 * width, (FINE_MAX + 1) * width, dtype=BF16)], (lows, table),
    )
    swapped, powers = lax.optimization_barrier((swapped, powers))
    sums0, source_sums, moved = call(
        lead_kernel, "lead", [vector, vectors, vector], (table, initial, source, coarse)
    )
    for turn in range(turns):
        moved = from_behind(moved, "tm", 1)
        if turn + 1 < turns:
            moved, = call(relay_kernel, "relay", [vector], (sums0, moved, source_sums, coarse))
    mine, = call(add_kernel, "add", [mats], (own, swapped))
    parts = exchange(mine.reshape(near, shard, width), near_groups())
    base, ofsource = call(
        functools.partial(base_kernel, everyone), "base", [rows8, rows8],
        (sums0, moved, source_sums, coarse, powers, table),
    )
    block, = call(
        middle_kernel, "middle", [shape(shard + slices * ROWS, width)], (parts, base)
    )
    block, later = lax.optimization_barrier((block, initial))
    bundle = shape(3, cells, width)
    sent, = call(
        functools.partial(sweep_kernel, True, False), "sweep", [bundle],
        (later, source, coarse, powers, table),
    )
    far = jnp.zeros_like(block)
    distance = 2 * near
    while distance < n_cell:
        far = far_swap(block, distance)
        distance *= 2
        if distance < n_cell:
            block = block + far
    far, sent = lax.optimization_barrier((far, sent))
    for turn in range(turns):
        sent = from_behind(sent, "tm", 1)
        if turn + 1 < turns:
            sent, = call(
                functools.partial(sweep_kernel, False, False), "sweep", [bundle],
                (initial, sent, source, coarse, powers, table),
            )
    payload, = call(
        gather_kernel, "gather", [shape(near, shard + slices * ROWS, width)], (block, far)
    )
    gathered = exchange(payload, near_groups())
    sums, ends = call(
        functools.partial(sweep_kernel, False, True), "sweep", [vectors, states],
        (initial, sent, source, coarse, powers, table),
    )
    theirs = swap_core(gathered)
    mixing, first, out = call(
        functools.partial(mixing_kernel, everyone, per), "mixing",
        [shape(slices, 2 * width, MATS * width, dtype=BF16), averages, rows4],
        (gathered, theirs, base, powers, table),
        scratch=[pltpu.VMEM((slices * MATS * width, width), F32)],
    )
    pushes1, end = call(
        push_kernel, "push", [vectors, vector],
        (exchange(out), first, mixing, powers, table, coarse),
    )
    nothing = jnp.zeros(vectors.shape, F32)
    moved = end
    for turn in range(turns):
        moved = from_behind(moved, "tm", 1)
        if turn + 1 < turns:
            moved, = call(vectors_kernel, "vectors", [vector], (moved, pushes1, nothing, coarse))
    moved1, base, out = call(
        functools.partial(second_kernel, everyone), "second",
        [vectors, rows8, shape(n_cell, slices * (FINE_MIN + 1), width)],
        (moved, pushes1, coarse, sums, table, powers, ofsource),
    )
    first, out = call(
        functools.partial(first_kernel, everyone, per), "first", [averages, rows4],
        (exchange(out), base, mixing, powers, table),
    )
    pushes2, end = call(
        push_kernel, "push", [vectors, vector],
        (exchange(out), first, mixing, powers, table, coarse, moved1),
    )
    moved = end
    for turn in range(turns):
        moved = from_behind(moved, "tm", 1)
        if turn + 1 < turns:
            moved, = call(vectors_kernel, "vectors", [vector], (moved, pushes2, moved1, coarse))
    out, = call(
        finish_kernel, "finish", [states], (moved, pushes2, moved1, coarse, ends, table)
    )
    return out


def solution(mesh):
    return jax.shard_map(
        body,
        mesh=mesh,
        in_specs=(
            P("cell", None),
            P("tm", "cell", None),
            P(),
            P("tm", "cell", None, None),
            P("tm", "cell", None, None),
            P("cell"),
        ),
        out_specs=P("tm", "cell", None),
        check_vma=False,
    )
```

```python
import functools

import jax
import jax.numpy as jnp
from jax import lax
from jax.experimental import pallas as pl
from jax.experimental.pallas import tpu as pltpu
from jax.sharding import PartitionSpec as P

FINE_MAX = 8
FINE_MIN = 4
CLASSES = FINE_MAX - FINE_MIN + 1
MATS = 7
ROWS = 8
OPENING_FLOPS = 10**9
COUNT_ROW = slice(6, 7)
RATE_ROW = slice(7, 8)
F32 = jnp.float32
BF16 = jnp.bfloat16


def high_low(x):
    high = x.astype(BF16).astype(F32)
    return high, x - high


def stacked(w):
    high, low = high_low(w)
    return jnp.concatenate([high, low], axis=0).astype(BF16)


def mul(x, w):
    rows = x.shape[0]
    high, low = high_low(x)
    left = jnp.concatenate([high, low], axis=0).astype(BF16)
    right = jnp.concatenate([high, jnp.zeros_like(low)], axis=0).astype(BF16)
    out = jnp.dot(jnp.concatenate([left, right], axis=1), w, preferred_element_type=F32)
    return out[:rows] + out[rows:]


def row_is(i, shape):
    return lax.broadcasted_iota(jnp.int32, shape, 0) == i


def leading():
    return lax.axis_index("tm") == 0


def from_behind(block, axis, distance):
    n = lax.axis_size(axis)
    return lax.ppermute(block, axis, [(i, (i + distance) % n) for i in range(n)])


def swap_core(block):
    n = lax.axis_size("cell")
    return lax.ppermute(block, "cell", [(i, i ^ 1) for i in range(n)])


def near_size():
    n = lax.axis_size("cell")
    return 4 if n % 8 == 0 else n // 2


def near_groups():
    n, near = lax.axis_size("cell"), near_size()
    return [
        [at + core + 2 * i for i in range(near)]
        for at in range(0, n, 2 * near)
        for core in range(2)
    ]


def far_swap(block, distance):
    n = lax.axis_size("cell")
    return lax.ppermute(block, "cell", [(i, i ^ distance) for i in range(n)])


def exchange(block, groups=None):
    return lax.all_to_all(block, "cell", 0, 0, axis_index_groups=groups)


def call(kernel, name, outs, args, scratch=(), flops=0):
    size = sum(x.size * x.dtype.itemsize for x in args)
    size += sum(x.size * x.dtype.itemsize for x in outs)
    return pl.pallas_call(
        kernel,
        out_shape=outs,
        in_specs=[pl.BlockSpec(memory_space=pltpu.VMEM)] * len(args),
        out_specs=[pl.BlockSpec(memory_space=pltpu.VMEM)] * len(outs),
        scratch_shapes=list(scratch),
        compiler_params=pltpu.CompilerParams(vmem_limit_bytes=24 << 20),
        cost_estimate=pl.CostEstimate(flops=flops, bytes_accessed=size, transcendentals=0),
        name=name,
    )(*args)


def shape(*dims, dtype=F32):
    return jax.ShapeDtypeStruct(dims, dtype)


def group_rows(g, per):
    return slice(g * per, (g + 1) * per)


def block(d, width):
    return slice((d - 1) * width, d * width)


def spread_counts(row):
    per = row.shape[1]
    return jnp.broadcast_to(row.astype(F32), (per, per)).T


def relay_kernel(start, received, source_sums, coarse, end):
    slices, groups, _, _ = coarse.shape
    for g in range(groups):
        V = jnp.where(leading(), start[g], received[g])
        for l in range(slices):
            V = mul(V + source_sums[l, g], stacked(coarse[l, g]))
        end[g] = V


def opening_kernel(out):
    out[...] = jnp.zeros_like(out)


def setup_kernel(everyone, fine, rate, counts, opened, own, other, lows, table):
    slices, groups, width, _ = fine.shape
    per = counts.shape[1]
    half = slices // 2
    core = lax.rem(lax.axis_index("cell"), 2)
    keep = 1.0 - rate[...]
    alive = []
    for g in range(groups):
        k = counts[g:g + 1].astype(F32)
        rows = [
            jnp.sum((k >= q).astype(F32), axis=1, keepdims=True)
            for q in range(FINE_MIN, FINE_MAX + 1)
        ]
        alive.append(rows)
        filled = jnp.zeros((ROWS, width), F32)
        for i, n in enumerate(rows + [None, k, rate[...]]):
            if n is not None:
                filled = jnp.where(row_is(i, filled.shape), n, filled)
        table[g] = filled
    for l in range(slices):
        sums = [0.0] * 4
        e6, e7, e72 = 0.0, 0.0, 0.0
        for g in range(groups):
            w1 = fine[l, g]
            w2 = mul(w1 * keep, stacked(w1))
            first = jnp.concatenate([w1, w2], axis=0)
            w34 = mul(first * keep, stacked(w2))
            w3, w4 = w34[:width], w34[width:]
            lows[l, g, :2 * width] = first
            lows[l, g, 2 * width:] = w34
            sums = [t + w for t, w in zip(sums, (w1, w2, w3, w4))]
            e6 = e6 + alive[g][2] * w1
            e7 = e7 + alive[g][3] * w1
            e72 = e72 + alive[g][3] * w2
        mats = [t * (per / everyone) for t in sums]
        mats += [e6 / everyone, (e6 + e72 - e7) / everyone, e7 / everyone]
        for i, m in enumerate(mats):
            at = slice(((l % half) * MATS + i) * width, ((l % half) * MATS + i + 1) * width)

            @pl.when(core == l // half)
            def _():
                own[at] = m

            @pl.when(core != l // half)
            def _():
                other[at] = m


def extend_kernel(lows, table, powers):
    slices, groups, _, width = lows.shape
    keep = 1.0 - table[0, RATE_ROW]
    for l in range(slices):
        for g in range(groups):
            ws = [lows[l, g, i * width:(i + 1) * width] for i in range(4)]
            w58 = mul(lows[l, g] * keep, stacked(ws[3]))
            ws += [w58[i * width:(i + 1) * width] for i in range(4)]
            ws.append((ws[0] + ws[1]) + (ws[2] + ws[3]))
            for i, w in enumerate(ws):
                powers[l, g, :, block(i + 1, width)] = stacked(w)


def lead_kernel(counts, initial, source, coarse, opened, start_sums, source_sums, end):
    slices, groups, _, _ = coarse.shape
    per = initial.shape[0] // groups
    for g in range(groups):
        here = group_rows(g, per)
        k = counts[g:g + 1].astype(F32)
        V = class_sums(initial[here], k)
        start_sums[g] = V
        for l in range(slices):
            S = class_sums(source[l, here], k)
            source_sums[l, g] = S
            V = mul(V + S, stacked(coarse[l, g]))
        end[g] = V


def add_kernel(a, b, out):
    out[...] = a[...] + b[...]


def class_sums(state, k):
    least = (FINE_MIN + lax.broadcasted_iota(jnp.int32, (ROWS, k.shape[1]), 0)).astype(F32)
    mask = (k >= least).astype(F32)
    left = jnp.concatenate([mask, mask], axis=1)
    left = jnp.concatenate([left, jnp.zeros_like(left)], axis=0).astype(BF16)
    return jnp.dot(left, stacked(state), preferred_element_type=F32)[:ROWS]


def picked(products, first, width):
    out = jnp.zeros((ROWS, width), F32)
    for i in range(CLASSES):
        d = first + i
        if 1 <= d <= FINE_MAX:
            out = out + jnp.where(row_is(i, out.shape), products[:, block(d, width)], 0.0)
    return out


def sums_of_state(V, keep, powers, width):
    x = mul(V * keep, powers)
    rows = [V[0:1]] + [x[0:1, block(m, width)] for m in range(1, FINE_MIN + 1)]
    gain = picked(x, FINE_MIN, width) - picked(x, FINE_MIN - 1, width)
    for i in range(1, 4):
        rows.append(rows[-1] + gain[i:i + 1])
    return jnp.concatenate(rows, axis=0)


def sums_of_source(S, powers, width):
    x = mul(S, powers)
    rows = [jnp.zeros((1, width), F32)]
    for m in range(1, FINE_MAX):
        i = max(m - FINE_MIN, 0)
        rows.append(rows[-1] + x[i:i + 1, block(m, width)])
    return jnp.concatenate(rows, axis=0)


def by_count(products, k, first, width):
    out = jnp.zeros(k.shape, F32)
    for i in range(CLASSES):
        d = i * width
        out = jnp.where(k == float(FINE_MIN + i), products[:, d:d + width], out)
    return out


def base_kernel(everyone, sums, received, source_sums, coarse, powers, table, base, ofsource):
    slices, groups, width, _ = coarse.shape
    keep = 1.0 - table[0, RATE_ROW]
    states = [jnp.where(leading(), sums[g], received[g]) for g in range(groups)]
    for l in range(slices):
        rows, rows_source = 0.0, 0.0
        for g in range(groups):
            V, S, w = states[g], source_sums[l, g], powers[l, g, :, :FINE_MAX * width]
            rows = rows + sums_of_state(V, keep, w, width)
            rows_source = rows_source + sums_of_source(S, w, width)
            if l + 1 < slices:
                states[g] = mul(V + S, stacked(coarse[l, g]))
        rows_source = rows_source / everyone
        at = slice(l * ROWS, (l + 1) * ROWS)
        ofsource[at] = rows_source
        base[at] = rows / everyone + rows_source


def sweep_kernel(first, last, *refs):
    if first:
        initial, source, coarse, powers, table, *outs = refs
    else:
        initial, received, source, coarse, powers, table, *outs = refs
    slices, groups, width, _ = coarse.shape
    per = initial.shape[0] // groups
    keep = 1.0 - table[0, RATE_ROW]
    for g in range(groups):
        here = group_rows(g, per)
        n = spread_counts(table[g, COUNT_ROW])
        start = initial[here]
        states = [start] * 3
        if not first:
            states = [jnp.where(leading(), start, received[i, here]) for i in range(3)]
        for l in range(slices):
            s = source[l, here]
            if last:
                outs[0][l, g] = class_sums(states[1], table[g, COUNT_ROW])
            w = powers[l, g, :, FINE_MIN * width:]
            x = mul(s, w)
            total = x[:, FINE_MIN * width:]
            sourced = jnp.where(n == float(FINE_MIN), total, 0.0)
            for i in range(CLASSES - 1):
                total = total + x[:, i * width:(i + 1) * width]
                sourced = jnp.where(n == float(FINE_MIN + 1 + i), total, sourced)
            both = jnp.concatenate(states[:2], axis=0) * keep
            x = mul(both, powers[l, g, :, (FINE_MIN - 1) * width:FINE_MAX * width])
            moved = mul(
                jnp.concatenate(
                    [states[0] + s, states[1] - states[0], states[2] - states[1]], axis=0
                ),
                stacked(coarse[l, g]),
            )
            states = [
                moved[:per],
                sourced + by_count(x[:per], n, FINE_MIN, width) + moved[per:2 * per],
                sourced + by_count(x[per:], n, FINE_MIN, width) + moved[2 * per:],
            ]
            if last:
                outs[1][l, here] = states[2]
        if not last:
            for i in range(3):
                outs[0][i, here] = states[i]


def middle_kernel(parts, base, out):
    n, rows, _ = parts.shape
    total = parts[0]
    for p in range(1, n):
        total = total + parts[p]
    out[:rows] = total
    out[rows:] = base[...]


def gather_kernel(a, b, out):
    total = a[...] + b[...]
    for p in range(out.shape[0]):
        out[p] = total


def wide(row):
    return jnp.broadcast_to(row, (ROWS, row.shape[-1]))


def assembled(known, width):
    out = jnp.zeros((ROWS, width), F32)
    for m, a in enumerate(known):
        out = jnp.where(row_is(m, out.shape), a, out)
    return out


def first_averages(rows, mixing, rate, width):
    known, sent = [], []
    for m in range(FINE_MIN + 1):
        a = wide(rows[m:m + 1])
        for j in range(m):
            a = a + sent[j][:, block(m - j, width)]
        known.append(a)
        if m < FINE_MIN:
            sent.append(mul(a * rate, mixing[:, :(FINE_MIN - m) * width]))
    return assembled(known, width)


def shifted(products, width):
    out = jnp.zeros((2 * ROWS, width), F32)
    empty = jnp.zeros((ROWS, width), F32)
    for d in range(1, FINE_MAX + 1):
        z = jnp.concatenate([products[:, block(d, width)], empty], axis=0)
        out = out + pltpu.roll(z, d, 0)
    return out


def second_rows(everyone, per, a, base, rate, powers, active, l, width):
    groups = powers.shape[1]
    rows = [0.0] * 3
    for g in range(groups):
        h = shifted(mul(a * rate, powers[l, g, :, :FINE_MAX * width]), width)
        total = per * h[4:5]
        for i in range(1, 4):
            total = total + active[g, i:i + 1] * (h[4 + i:5 + i] - h[3 + i:4 + i])
            rows[i - 1] = rows[i - 1] + total
    at = l * ROWS + FINE_MIN + 1
    return [rows[i] / everyone + base[at + i:at + i + 1] for i in range(3)]


def send_rows(everyone, per, a, base, rate, powers, active, out, width):
    slices = powers.shape[0]
    rows = []
    for l in range(slices):
        rows += second_rows(everyone, per, a[l], base, rate, powers, active, l, width)
        rows.append(jnp.zeros((1, width), F32))
    rows = jnp.concatenate(rows, axis=0)
    for p in range(out.shape[0]):
        out[p] = rows


def mixing_kernel(everyone, per, mine, theirs, base, powers, table,
                  mixing, averages, out, held):
    slices, _, _, wider = powers.shape
    width = wider // (FINE_MAX + 1)
    half = slices // 2
    n, rows, _ = mine.shape
    rows -= slices * ROWS
    rate = table[0, RATE_ROW]
    core = lax.rem(lax.axis_index("cell"), 2)
    mixed = 0.0
    for ref, at in ((mine, core), (theirs, 1 - core)):
        for p in range(n):
            place = at * (half * MATS * width) + p * rows
            held[pl.ds(place, rows), :] = ref[p, :rows]
            mixed = mixed + ref[p, rows:]
    a = []
    for l in range(slices):
        for i in range(MATS):
            at = (l * MATS + i) * width
            mixing[l, :, block(i + 1, width)] = stacked(held[at:at + width])
        a.append(first_averages(mixed[l * ROWS:(l + 1) * ROWS], mixing[l], rate, width))
        averages[l] = a[-1]
    send_rows(everyone, per, a, base, rate, powers, table, out, width)


def first_kernel(everyone, per, received, base, mixing, powers, table, averages, out):
    slices, _, _, wider = powers.shape
    width = wider // (FINE_MAX + 1)
    rate = table[0, RATE_ROW]
    total = received[0]
    for p in range(1, received.shape[0]):
        total = total + received[p]
    a = []
    for l in range(slices):
        rows = total[l * (FINE_MIN + 1):(l + 1) * (FINE_MIN + 1)]
        a.append(first_averages(rows, mixing[l], rate, width))
        averages[l] = a[-1]
    send_rows(everyone, per, a, base, rate, powers, table, out, width)


def push_kernel(received, averages, mixing, powers, table, coarse, *refs):
    starts, (pushes, end) = (None, refs) if len(refs) == 2 else (refs[0], refs[1:])
    slices, groups, _, wider = powers.shape
    width = wider // (FINE_MAX + 1)
    r = table[0, RATE_ROW]
    total = received[0]
    for p in range(1, received.shape[0]):
        total = total + received[p]
    x = [jnp.zeros((ROWS, width), F32) for _ in range(groups)]
    for l in range(slices):
        a5 = wide(total[l * 4:l * 4 + 1])
        z = mul(a5 * r, mixing[l, :, 4 * width:6 * width])
        a6 = wide(total[l * 4 + 1:l * 4 + 2]) + z[:, :width]
        a7 = wide(total[l * 4 + 2:l * 4 + 3]) + z[:, width:]
        a7 = a7 + mul(a6 * r, mixing[l, :, 6 * width:])
        a = averages[l]
        for m, row in ((5, a5), (6, a6), (7, a7)):
            a = jnp.where(row_is(m, a.shape), row, a)
        for g in range(groups):
            w = powers[l, g, :, :FINE_MAX * width]
            if starts is None:
                h = shifted(mul(a * r, w), width)[FINE_MIN:FINE_MIN + ROWS]
                old = x[g]
            else:
                both = jnp.concatenate([a * r, starts[l, g] * (1.0 - r)], axis=0)
                z = mul(both, w)
                h = shifted(z[:ROWS], width)[FINE_MIN:FINE_MIN + ROWS]
                h = h + picked(z[ROWS:], FINE_MIN, width)
                old = x[g] - starts[l, g]
            pushes[l, g] = h
            x[g] = h + mul(old, stacked(coarse[l, g]))
    for g in range(groups):
        end[g] = x[g]


def vectors_kernel(received, pushes, starts, coarse, end):
    slices, groups, _, _ = coarse.shape
    for g in range(groups):
        x = jnp.where(leading(), 0.0, received[g])
        for l in range(slices):
            x = pushes[l, g] + mul(x - starts[l, g], stacked(coarse[l, g]))
        end[g] = x


def second_kernel(everyone, received, pushes, coarse, sums, table, powers, ofsource,
                  starts, base, out):
    slices, groups, width, _ = coarse.shape
    keep = 1.0 - table[0, RATE_ROW]
    x = [jnp.where(leading(), 0.0, received[g]) for g in range(groups)]
    sent = []
    for l in range(slices):
        rows = 0.0
        for g in range(groups):
            starts[l, g] = x[g]
            n = table[g]
            exact = n - pltpu.roll(n, ROWS - 1, 0)
            exact = jnp.where(row_is(ROWS - 1, n.shape), 0.0, exact)
            weighted = exact * x[g]
            tail = jnp.zeros((1, width), F32)
            V = sums[l, g]
            for i in reversed(range(CLASSES)):
                tail = tail + weighted[i:i + 1]
                V = jnp.where(row_is(i, V.shape), V + tail, V)
            rows = rows + sums_of_state(V, keep, powers[l, g, :, :FINE_MAX * width], width)
            if l + 1 < slices:
                x[g] = pushes[l, g] + mul(x[g], stacked(coarse[l, g]))
        at = slice(l * ROWS, (l + 1) * ROWS)
        rows = rows / everyone + ofsource[at]
        base[at] = rows
        sent.append(rows[:FINE_MIN + 1])
    sent = jnp.concatenate(sent, axis=0)
    for p in range(out.shape[0]):
        out[p] = sent


def finish_kernel(received, pushes, starts, coarse, ends, table, out):
    slices, groups, width, _ = coarse.shape
    per = ends.shape[1] // groups
    for g in range(groups):
        here = group_rows(g, per)
        n = spread_counts(table[g, COUNT_ROW])
        x = jnp.where(leading(), 0.0, received[g])
        for l in range(slices):
            x = pushes[l, g] + mul(x - starts[l, g], stacked(coarse[l, g]))
            add = jnp.zeros((per, width), F32)
            for i in range(CLASSES):
                add = jnp.where(n == float(FINE_MIN + i), x[i:i + 1], add)
            out[l, here] = ends[l, here] + add


def body(initial, source, mix_rate, fine, coarse, step_counts):
    slices, groups, width, _ = fine.shape
    cells = initial.shape[0]
    per = cells // groups
    n_cell = lax.axis_size("cell")
    turns = lax.axis_size("tm") - 1
    everyone = cells * n_cell
    half = slices // 2
    near = near_size()
    shard = half * MATS * width // near
    rate = mix_rate.reshape(1, width)
    counts = step_counts.reshape(groups, per)
    state = shape(cells, width)
    states = shape(slices, cells, width)
    vectors = shape(slices, groups, ROWS, width)
    vector = shape(groups, ROWS, width)
    rows8 = shape(slices * ROWS, width)
    rows4 = shape(n_cell, slices * 4, width)
    averages = shape(slices, ROWS, width)
    mats = shape(half * MATS * width, width)
    opened, = call(opening_kernel, "opening", [shape(ROWS, width)], (), flops=OPENING_FLOPS)
    sums0, source_sums, moved = call(
        lead_kernel, "lead", [vector, vectors, vector], (counts, initial, source, coarse, opened)
    )
    for turn in range(turns):
        moved = from_behind(moved, "tm", 1)
        if turn + 1 < turns:
            moved, = call(relay_kernel, "relay", [vector], (sums0, moved, source_sums, coarse))
    fine, sums0 = lax.optimization_barrier((fine, sums0))
    own, other, lows, table = call(
        functools.partial(setup_kernel, everyone), "setup",
        [mats, mats, shape(slices, groups, 4 * width, width), vector],
        (fine, rate, counts, opened),
    )
    swapped = swap_core(other)
    powers, = call(
        extend_kernel, "extend",
        [shape(slices, groups, 2 * width, (FINE_MAX + 1) * width, dtype=BF16)], (lows, table),
    )
    base, ofsource = call(
        functools.partial(base_kernel, everyone), "base", [rows8, rows8],
        (sums0, moved, source_sums, coarse, powers, table),
    )
    swapped, base = lax.optimization_barrier((swapped, base))
    mine, = call(add_kernel, "add", [mats], (own, swapped))
    parts = exchange(mine.reshape(near, shard, width), near_groups())
    block, = call(
        middle_kernel, "middle", [shape(shard + slices * ROWS, width)], (parts, base)
    )
    block, later = lax.optimization_barrier((block, initial))
    bundle = shape(3, cells, width)
    sent, = call(
        functools.partial(sweep_kernel, True, False), "sweep", [bundle],
        (later, source, coarse, powers, table),
    )
    far = jnp.zeros_like(block)
    distance = 2 * near
    while distance < n_cell:
        far = far_swap(block, distance)
        distance *= 2
        if distance < n_cell:
            block = block + far
    far, sent = lax.optimization_barrier((far, sent))
    for turn in range(turns):
        sent = from_behind(sent, "tm", 1)
        if turn + 1 < turns:
            sent, = call(
                functools.partial(sweep_kernel, False, False), "sweep", [bundle],
                (initial, sent, source, coarse, powers, table),
            )
    payload, = call(
        gather_kernel, "gather", [shape(near, shard + slices * ROWS, width)], (block, far)
    )
    gathered = exchange(payload, near_groups())
    sums, ends = call(
        functools.partial(sweep_kernel, False, True), "sweep", [vectors, states],
        (initial, sent, source, coarse, powers, table),
    )
    theirs = swap_core(gathered)
    mixing, first, out = call(
        functools.partial(mixing_kernel, everyone, per), "mixing",
        [shape(slices, 2 * width, MATS * width, dtype=BF16), averages, rows4],
        (gathered, theirs, base, powers, table),
        scratch=[pltpu.VMEM((slices * MATS * width, width), F32)],
    )
    pushes1, end = call(
        push_kernel, "push", [vectors, vector],
        (exchange(out), first, mixing, powers, table, coarse),
    )
    nothing = jnp.zeros(vectors.shape, F32)
    moved = end
    for turn in range(turns):
        moved = from_behind(moved, "tm", 1)
        if turn + 1 < turns:
            moved, = call(vectors_kernel, "vectors", [vector], (moved, pushes1, nothing, coarse))
    moved1, base, out = call(
        functools.partial(second_kernel, everyone), "second",
        [vectors, rows8, shape(n_cell, slices * (FINE_MIN + 1), width)],
        (moved, pushes1, coarse, sums, table, powers, ofsource),
    )
    first, out = call(
        functools.partial(first_kernel, everyone, per), "first", [averages, rows4],
        (exchange(out), base, mixing, powers, table),
    )
    pushes2, end = call(
        push_kernel, "push", [vectors, vector],
        (exchange(out), first, mixing, powers, table, coarse, moved1),
    )
    moved = end
    for turn in range(turns):
        moved = from_behind(moved, "tm", 1)
        if turn + 1 < turns:
            moved, = call(vectors_kernel, "vectors", [vector], (moved, pushes2, moved1, coarse))
    out, = call(
        finish_kernel, "finish", [states], (moved, pushes2, moved1, coarse, ends, table)
    )
    return out


def solution(mesh):
    return jax.shard_map(
        body,
        mesh=mesh,
        in_specs=(
            P("cell", None),
            P("tm", "cell", None),
            P(),
            P("tm", "cell", None, None),
            P("tm", "cell", None, None),
            P("cell"),
        ),
        out_specs=P("tm", "cell", None),
        check_vma=False,
    )
```

```python
import functools

import jax
import jax.numpy as jnp
from jax import lax
from jax.experimental import pallas as pl
from jax.experimental.pallas import tpu as pltpu
from jax.sharding import PartitionSpec as P

FINE_MAX = 8
FINE_MIN = 4
CLASSES = FINE_MAX - FINE_MIN + 1
MATS = 7
ROWS = 8
OPENING_FLOPS = 10**9
COUNT_ROW = slice(6, 7)
RATE_ROW = slice(7, 8)
F32 = jnp.float32
BF16 = jnp.bfloat16


def high_low(x):
    high = x.astype(BF16).astype(F32)
    return high, x - high


def stacked(w):
    high, low = high_low(w)
    return jnp.concatenate([high, low], axis=0).astype(BF16)


def mul(x, w):
    rows = x.shape[0]
    high, low = high_low(x)
    left = jnp.concatenate([high, low], axis=0).astype(BF16)
    right = jnp.concatenate([high, jnp.zeros_like(low)], axis=0).astype(BF16)
    out = jnp.dot(jnp.concatenate([left, right], axis=1), w, preferred_element_type=F32)
    return out[:rows] + out[rows:]


def row_is(i, shape):
    return lax.broadcasted_iota(jnp.int32, shape, 0) == i


def leading():
    return lax.axis_index("tm") == 0


def from_behind(block, axis, distance):
    n = lax.axis_size(axis)
    return lax.ppermute(block, axis, [(i, (i + distance) % n) for i in range(n)])


def swap_core(block):
    n = lax.axis_size("cell")
    return lax.ppermute(block, "cell", [(i, i ^ 1) for i in range(n)])


def near_size():
    n = lax.axis_size("cell")
    return 4 if n % 8 == 0 else n // 2


def near_groups():
    n, near = lax.axis_size("cell"), near_size()
    return [
        [at + core + 2 * i for i in range(near)]
        for at in range(0, n, 2 * near)
        for core in range(2)
    ]


def far_swap(block, distance):
    n = lax.axis_size("cell")
    return lax.ppermute(block, "cell", [(i, i ^ distance) for i in range(n)])


def exchange(block, groups=None):
    return lax.all_to_all(block, "cell", 0, 0, axis_index_groups=groups)


def call(kernel, name, outs, args, scratch=(), flops=0):
    size = sum(x.size * x.dtype.itemsize for x in args)
    size += sum(x.size * x.dtype.itemsize for x in outs)
    return pl.pallas_call(
        kernel,
        out_shape=outs,
        in_specs=[pl.BlockSpec(memory_space=pltpu.VMEM)] * len(args),
        out_specs=[pl.BlockSpec(memory_space=pltpu.VMEM)] * len(outs),
        scratch_shapes=list(scratch),
        compiler_params=pltpu.CompilerParams(vmem_limit_bytes=24 << 20),
        cost_estimate=pl.CostEstimate(flops=flops, bytes_accessed=size, transcendentals=0),
        name=name,
    )(*args)


def shape(*dims, dtype=F32):
    return jax.ShapeDtypeStruct(dims, dtype)


def group_rows(g, per):
    return slice(g * per, (g + 1) * per)


def block(d, width):
    return slice((d - 1) * width, d * width)


def spread_counts(row):
    per = row.shape[1]
    return jnp.broadcast_to(row.astype(F32), (per, per)).T


def relay_kernel(start, received, source_sums, coarse, end):
    slices, groups, _, _ = coarse.shape
    for g in range(groups):
        V = jnp.where(leading(), start[g], received[g])
        for l in range(slices):
            V = mul(V + source_sums[l, g], stacked(coarse[l, g]))
        end[g] = V


def opening_kernel(out):
    out[...] = jnp.zeros_like(out)


def setup_kernel(everyone, fine, rate, counts, opened, own, other, lows, table):
    slices, groups, width, _ = fine.shape
    per = counts.shape[1]
    half = slices // 2
    core = lax.rem(lax.axis_index("cell"), 2)
    keep = 1.0 - rate[...]
    alive = []
    for g in range(groups):
        k = counts[g:g + 1].astype(F32)
        rows = [
            jnp.sum((k >= q).astype(F32), axis=1, keepdims=True)
            for q in range(FINE_MIN, FINE_MAX + 1)
        ]
        alive.append(rows)
        filled = jnp.zeros((ROWS, width), F32)
        for i, n in enumerate(rows + [None, k, rate[...]]):
            if n is not None:
                filled = jnp.where(row_is(i, filled.shape), n, filled)
        table[g] = filled
    for l in range(slices):
        sums = [0.0] * 4
        e6, e7, e72 = 0.0, 0.0, 0.0
        for g in range(groups):
            w1 = fine[l, g]
            w2 = mul(w1 * keep, stacked(w1))
            first = jnp.concatenate([w1, w2], axis=0)
            w34 = mul(first * keep, stacked(w2))
            w3, w4 = w34[:width], w34[width:]
            lows[l, g, :2 * width] = first
            lows[l, g, 2 * width:] = w34
            sums = [t + w for t, w in zip(sums, (w1, w2, w3, w4))]
            e6 = e6 + alive[g][2] * w1
            e7 = e7 + alive[g][3] * w1
            e72 = e72 + alive[g][3] * w2
        mats = [t * (per / everyone) for t in sums]
        mats += [e6 / everyone, (e6 + e72 - e7) / everyone, e7 / everyone]
        for i, m in enumerate(mats):
            at = slice(((l % half) * MATS + i) * width, ((l % half) * MATS + i + 1) * width)

            @pl.when(core == l // half)
            def _():
                own[at] = m

            @pl.when(core != l // half)
            def _():
                other[at] = m


def extend_kernel(lows, table, powers):
    slices, groups, _, width = lows.shape
    keep = 1.0 - table[0, RATE_ROW]
    for l in range(slices):
        for g in range(groups):
            ws = [lows[l, g, i * width:(i + 1) * width] for i in range(4)]
            w58 = mul(lows[l, g] * keep, stacked(ws[3]))
            ws += [w58[i * width:(i + 1) * width] for i in range(4)]
            ws.append((ws[0] + ws[1]) + (ws[2] + ws[3]))
            for i, w in enumerate(ws):
                powers[l, g, :, block(i + 1, width)] = stacked(w)


def lead_kernel(counts, initial, source, coarse, opened, start_sums, source_sums, end):
    slices, groups, _, _ = coarse.shape
    per = initial.shape[0] // groups
    for g in range(groups):
        here = group_rows(g, per)
        k = counts[g:g + 1].astype(F32)
        V = class_sums(initial[here], k)
        start_sums[g] = V
        for l in range(slices):
            S = class_sums(source[l, here], k)
            source_sums[l, g] = S
            V = mul(V + S, stacked(coarse[l, g]))
        end[g] = V


def add_kernel(a, b, out):
    out[...] = a[...] + b[...]


def class_sums(state, k):
    least = (FINE_MIN + lax.broadcasted_iota(jnp.int32, (ROWS, k.shape[1]), 0)).astype(F32)
    mask = (k >= least).astype(F32)
    left = jnp.concatenate([mask, mask], axis=1)
    left = jnp.concatenate([left, jnp.zeros_like(left)], axis=0).astype(BF16)
    return jnp.dot(left, stacked(state), preferred_element_type=F32)[:ROWS]


def picked(products, first, width):
    out = jnp.zeros((ROWS, width), F32)
    for i in range(CLASSES):
        d = first + i
        if 1 <= d <= FINE_MAX:
            out = out + jnp.where(row_is(i, out.shape), products[:, block(d, width)], 0.0)
    return out


def sums_of_state(V, keep, powers, width):
    x = mul(V * keep, powers)
    rows = [V[0:1]] + [x[0:1, block(m, width)] for m in range(1, FINE_MIN + 1)]
    gain = picked(x, FINE_MIN, width) - picked(x, FINE_MIN - 1, width)
    for i in range(1, 4):
        rows.append(rows[-1] + gain[i:i + 1])
    return jnp.concatenate(rows, axis=0)


def sums_of_source(S, powers, width):
    x = mul(S, powers)
    rows = [jnp.zeros((1, width), F32)]
    for m in range(1, FINE_MAX):
        i = max(m - FINE_MIN, 0)
        rows.append(rows[-1] + x[i:i + 1, block(m, width)])
    return jnp.concatenate(rows, axis=0)


def by_count(products, k, first, width):
    out = jnp.zeros(k.shape, F32)
    for i in range(CLASSES):
        d = i * width
        out = jnp.where(k == float(FINE_MIN + i), products[:, d:d + width], out)
    return out


def base_kernel(everyone, sums, received, source_sums, coarse, powers, table, base, ofsource):
    slices, groups, width, _ = coarse.shape
    keep = 1.0 - table[0, RATE_ROW]
    states = [jnp.where(leading(), sums[g], received[g]) for g in range(groups)]
    for l in range(slices):
        rows, rows_source = 0.0, 0.0
        for g in range(groups):
            V, S, w = states[g], source_sums[l, g], powers[l, g, :, :FINE_MAX * width]
            rows = rows + sums_of_state(V, keep, w, width)
            rows_source = rows_source + sums_of_source(S, w, width)
            if l + 1 < slices:
                states[g] = mul(V + S, stacked(coarse[l, g]))
        rows_source = rows_source / everyone
        at = slice(l * ROWS, (l + 1) * ROWS)
        ofsource[at] = rows_source
        base[at] = rows / everyone + rows_source


def sweep_kernel(first, last, *refs):
    if first:
        initial, source, coarse, powers, table, *outs = refs
    else:
        initial, received, source, coarse, powers, table, *outs = refs
    slices, groups, width, _ = coarse.shape
    per = initial.shape[0] // groups
    keep = 1.0 - table[0, RATE_ROW]
    for g in range(groups):
        here = group_rows(g, per)
        n = spread_counts(table[g, COUNT_ROW])
        start = initial[here]
        states = [start] * 3
        if not first:
            states = [jnp.where(leading(), start, received[i, here]) for i in range(3)]
        for l in range(slices):
            s = source[l, here]
            if last:
                outs[0][l, g] = class_sums(states[1], table[g, COUNT_ROW])
            w = powers[l, g, :, FINE_MIN * width:]
            x = mul(s, w)
            total = x[:, FINE_MIN * width:]
            sourced = jnp.where(n == float(FINE_MIN), total, 0.0)
            for i in range(CLASSES - 1):
                total = total + x[:, i * width:(i + 1) * width]
                sourced = jnp.where(n == float(FINE_MIN + 1 + i), total, sourced)
            both = jnp.concatenate(states[:2], axis=0) * keep
            x = mul(both, powers[l, g, :, (FINE_MIN - 1) * width:FINE_MAX * width])
            moved = mul(
                jnp.concatenate(
                    [states[0] + s, states[1] - states[0], states[2] - states[1]], axis=0
                ),
                stacked(coarse[l, g]),
            )
            states = [
                moved[:per],
                sourced + by_count(x[:per], n, FINE_MIN, width) + moved[per:2 * per],
                sourced + by_count(x[per:], n, FINE_MIN, width) + moved[2 * per:],
            ]
            if last:
                outs[1][l, here] = states[2]
        if not last:
            for i in range(3):
                outs[0][i, here] = states[i]


def middle_kernel(parts, base, out):
    n, rows, _ = parts.shape
    total = parts[0]
    for p in range(1, n):
        total = total + parts[p]
    out[:rows] = total
    out[rows:] = base[...]


def gather_kernel(a, b, out):
    total = a[...] + b[...]
    for p in range(out.shape[0]):
        out[p] = total


def wide(row):
    return jnp.broadcast_to(row, (ROWS, row.shape[-1]))


def assembled(known, width):
    out = jnp.zeros((ROWS, width), F32)
    for m, a in enumerate(known):
        out = jnp.where(row_is(m, out.shape), a, out)
    return out


def first_averages(rows, mixing, rate, width):
    known, sent = [], []
    for m in range(FINE_MIN + 1):
        a = wide(rows[m])
        for j in range(m):
            a = a + sent[j][:, block(m - j, width)]
        known.append(a)
        if m < FINE_MIN:
            sent.append(mul(a * rate, mixing[:, :(FINE_MIN - m) * width]))
    return assembled(known, width)


def shifted(products, width):
    out = jnp.zeros((2 * ROWS, width), F32)
    empty = jnp.zeros((ROWS, width), F32)
    for d in range(1, products.shape[1] // width + 1):
        z = jnp.concatenate([products[:, block(d, width)], empty], axis=0)
        out = out + pltpu.roll(z, d, 0)
    return out


def second_rows(everyone, per, a, base, rate, powers, table, partial, l, width):
    groups = powers.shape[1]
    rows = [0.0] * 3
    for g in range(groups):
        h = shifted(mul(a * rate, powers[l, g, :, :FINE_MAX * width]), width)
        partial[l, g] = h
        total = per * h[4:5]
        for i in range(1, 4):
            total = total + table[g, i:i + 1] * (h[4 + i:5 + i] - h[3 + i:4 + i])
            rows[i - 1] = rows[i - 1] + total
    at = l * ROWS + FINE_MIN + 1
    return [rows[i] / everyone + base[at + i:at + i + 1] for i in range(3)]


def send_line(rows, out):
    line = jnp.concatenate(rows, axis=1)
    for p in range(out.shape[0]):
        out[p] = line


def received_rows(received, width):
    total = received[0]
    for p in range(1, received.shape[0]):
        total = total + received[p]
    return [total[:, i:i + width] for i in range(0, total.shape[1], width)]


def send_rows(everyone, per, a, base, rate, powers, table, partial, out, width):
    rows = []
    for l in range(powers.shape[0]):
        rows += second_rows(everyone, per, a[l], base, rate, powers, table, partial, l, width)
    send_line(rows, out)


def mixing_kernel(everyone, per, mine, theirs, base, powers, table,
                  mixing, partial, out, held):
    slices, _, _, wider = powers.shape
    width = wider // (FINE_MAX + 1)
    half = slices // 2
    n, rows, _ = mine.shape
    rows -= slices * ROWS
    rate = table[0, RATE_ROW]
    core = lax.rem(lax.axis_index("cell"), 2)
    mixed = 0.0
    for ref, at in ((mine, core), (theirs, 1 - core)):
        for p in range(n):
            place = at * (half * MATS * width) + p * rows
            held[pl.ds(place, rows), :] = ref[p, :rows]
            mixed = mixed + ref[p, rows:]
    a = []
    for l in range(slices):
        for i in range(MATS):
            at = (l * MATS + i) * width
            mixing[l, :, block(i + 1, width)] = stacked(held[at:at + width])
        rows = [mixed[l * ROWS + m:l * ROWS + m + 1] for m in range(FINE_MIN + 1)]
        a.append(first_averages(rows, mixing[l], rate, width))
    send_rows(everyone, per, a, base, rate, powers, table, partial, out, width)


def first_kernel(everyone, per, received, base, mixing, powers, table, partial, out):
    slices, _, _, wider = powers.shape
    width = wider // (FINE_MAX + 1)
    rate = table[0, RATE_ROW]
    rows = received_rows(received, width)
    known = FINE_MIN + 1
    a = [
        first_averages(rows[l * known:(l + 1) * known], mixing[l], rate, width)
        for l in range(slices)
    ]
    send_rows(everyone, per, a, base, rate, powers, table, partial, out, width)


def push_kernel(received, partial, mixing, powers, table, coarse, *refs):
    starts, (pushes, end) = (None, refs) if len(refs) == 2 else (refs[0], refs[1:])
    slices, groups, _, wider = powers.shape
    width = wider // (FINE_MAX + 1)
    r = table[0, RATE_ROW]
    rows = received_rows(received, width)
    x = [jnp.zeros((ROWS, width), F32) for _ in range(groups)]
    for l in range(slices):
        a5, a6, a7 = (wide(row) for row in rows[3 * l:3 * l + 3])
        z = mul(a5 * r, mixing[l, :, 4 * width:6 * width])
        a6 = a6 + z[:, :width]
        a7 = a7 + z[:, width:] + mul(a6 * r, mixing[l, :, 6 * width:])
        a = jnp.zeros((ROWS, width), F32)
        for m, row in ((5, a5), (6, a6), (7, a7)):
            a = jnp.where(row_is(m, a.shape), row, a)
        for g in range(groups):
            z = mul(a * r, powers[l, g, :, :3 * width])
            h = (partial[l, g] + shifted(z, width))[FINE_MIN:FINE_MIN + ROWS]
            old = x[g]
            if starts is not None:
                w = powers[l, g, :, (FINE_MIN - 1) * width:FINE_MAX * width]
                h = h + picked(mul(starts[l, g] * (1.0 - r), w), 1, width)
                old = x[g] - starts[l, g]
            pushes[l, g] = h
            x[g] = h + mul(old, stacked(coarse[l, g]))
    for g in range(groups):
        end[g] = x[g]


def vectors_kernel(received, pushes, starts, coarse, end):
    slices, groups, _, _ = coarse.shape
    for g in range(groups):
        x = jnp.where(leading(), 0.0, received[g])
        for l in range(slices):
            x = pushes[l, g] + mul(x - starts[l, g], stacked(coarse[l, g]))
        end[g] = x


def second_kernel(everyone, received, pushes, coarse, sums, table, powers, ofsource,
                  starts, base, out):
    slices, groups, width, _ = coarse.shape
    keep = 1.0 - table[0, RATE_ROW]
    x = [jnp.where(leading(), 0.0, received[g]) for g in range(groups)]
    sent = []
    for l in range(slices):
        rows = 0.0
        for g in range(groups):
            starts[l, g] = x[g]
            n = table[g]
            exact = n - pltpu.roll(n, ROWS - 1, 0)
            exact = jnp.where(row_is(ROWS - 1, n.shape), 0.0, exact)
            weighted = exact * x[g]
            tail = jnp.zeros((1, width), F32)
            V = sums[l, g]
            for i in reversed(range(CLASSES)):
                tail = tail + weighted[i:i + 1]
                V = jnp.where(row_is(i, V.shape), V + tail, V)
            rows = rows + sums_of_state(V, keep, powers[l, g, :, :FINE_MAX * width], width)
            if l + 1 < slices:
                x[g] = pushes[l, g] + mul(x[g], stacked(coarse[l, g]))
        at = slice(l * ROWS, (l + 1) * ROWS)
        rows = rows / everyone + ofsource[at]
        base[at] = rows
        sent += [rows[m:m + 1] for m in range(FINE_MIN + 1)]
    send_line(sent, out)


def finish_kernel(received, pushes, starts, coarse, ends, table, out):
    slices, groups, width, _ = coarse.shape
    per = ends.shape[1] // groups
    for g in range(groups):
        here = group_rows(g, per)
        n = spread_counts(table[g, COUNT_ROW])
        x = jnp.where(leading(), 0.0, received[g])
        for l in range(slices):
            x = pushes[l, g] + mul(x - starts[l, g], stacked(coarse[l, g]))
            add = jnp.zeros((per, width), F32)
            for i in range(CLASSES):
                add = jnp.where(n == float(FINE_MIN + i), x[i:i + 1], add)
            out[l, here] = ends[l, here] + add


def body(initial, source, mix_rate, fine, coarse, step_counts):
    slices, groups, width, _ = fine.shape
    cells = initial.shape[0]
    per = cells // groups
    n_cell = lax.axis_size("cell")
    turns = lax.axis_size("tm") - 1
    everyone = cells * n_cell
    half = slices // 2
    near = near_size()
    shard = half * MATS * width // near
    rate = mix_rate.reshape(1, width)
    counts = step_counts.reshape(groups, per)
    state = shape(cells, width)
    states = shape(slices, cells, width)
    vectors = shape(slices, groups, ROWS, width)
    vector = shape(groups, ROWS, width)
    rows8 = shape(slices * ROWS, width)
    line3 = shape(n_cell, 1, slices * 3 * width)
    line5 = shape(n_cell, 1, slices * (FINE_MIN + 1) * width)
    partial = shape(slices, groups, 2 * ROWS, width)
    mats = shape(half * MATS * width, width)
    opened, = call(opening_kernel, "opening", [shape(ROWS, width)], (), flops=OPENING_FLOPS)
    sums0, source_sums, moved = call(
        lead_kernel, "lead", [vector, vectors, vector], (counts, initial, source, coarse, opened)
    )
    for turn in range(turns):
        moved = from_behind(moved, "tm", 1)
        if turn + 1 < turns:
            moved, = call(relay_kernel, "relay", [vector], (sums0, moved, source_sums, coarse))
    fine, sums0 = lax.optimization_barrier((fine, sums0))
    own, other, lows, table = call(
        functools.partial(setup_kernel, everyone), "setup",
        [mats, mats, shape(slices, groups, 4 * width, width), vector],
        (fine, rate, counts, opened),
    )
    swapped = swap_core(other)
    powers, = call(
        extend_kernel, "extend",
        [shape(slices, groups, 2 * width, (FINE_MAX + 1) * width, dtype=BF16)], (lows, table),
    )
    base, ofsource = call(
        functools.partial(base_kernel, everyone), "base", [rows8, rows8],
        (sums0, moved, source_sums, coarse, powers, table),
    )
    swapped, base = lax.optimization_barrier((swapped, base))
    mine, = call(add_kernel, "add", [mats], (own, swapped))
    parts = exchange(mine.reshape(near, shard, width), near_groups())
    block, = call(
        middle_kernel, "middle", [shape(shard + slices * ROWS, width)], (parts, base)
    )
    block, later = lax.optimization_barrier((block, initial))
    bundle = shape(3, cells, width)
    sent, = call(
        functools.partial(sweep_kernel, True, False), "sweep", [bundle],
        (later, source, coarse, powers, table),
    )
    far = jnp.zeros_like(block)
    distance = 2 * near
    while distance < n_cell:
        far = far_swap(block, distance)
        distance *= 2
        if distance < n_cell:
            block = block + far
    far, sent = lax.optimization_barrier((far, sent))
    for turn in range(turns):
        sent = from_behind(sent, "tm", 1)
        if turn + 1 < turns:
            sent, = call(
                functools.partial(sweep_kernel, False, False), "sweep", [bundle],
                (initial, sent, source, coarse, powers, table),
            )
    payload, = call(
        gather_kernel, "gather", [shape(near, shard + slices * ROWS, width)], (block, far)
    )
    gathered = exchange(payload, near_groups())
    sums, ends = call(
        functools.partial(sweep_kernel, False, True), "sweep", [vectors, states],
        (initial, sent, source, coarse, powers, table),
    )
    theirs = swap_core(gathered)
    mixing, first, out = call(
        functools.partial(mixing_kernel, everyone, per), "mixing",
        [shape(slices, 2 * width, MATS * width, dtype=BF16), partial, line3],
        (gathered, theirs, base, powers, table),
        scratch=[pltpu.VMEM((slices * MATS * width, width), F32)],
    )
    pushes1, end = call(
        push_kernel, "push", [vectors, vector],
        (exchange(out), first, mixing, powers, table, coarse),
    )
    nothing = jnp.zeros(vectors.shape, F32)
    moved = end
    for turn in range(turns):
        moved = from_behind(moved, "tm", 1)
        if turn + 1 < turns:
            moved, = call(vectors_kernel, "vectors", [vector], (moved, pushes1, nothing, coarse))
    moved1, base, out = call(
        functools.partial(second_kernel, everyone), "second",
        [vectors, rows8, line5],
        (moved, pushes1, coarse, sums, table, powers, ofsource),
    )
    first, out = call(
        functools.partial(first_kernel, everyone, per), "first", [partial, line3],
        (exchange(out), base, mixing, powers, table),
    )
    pushes2, end = call(
        push_kernel, "push", [vectors, vector],
        (exchange(out), first, mixing, powers, table, coarse, moved1),
    )
    moved = end
    for turn in range(turns):
        moved = from_behind(moved, "tm", 1)
        if turn + 1 < turns:
            moved, = call(vectors_kernel, "vectors", [vector], (moved, pushes2, moved1, coarse))
    out, = call(
        finish_kernel, "finish", [states], (moved, pushes2, moved1, coarse, ends, table)
    )
    return out


def solution(mesh):
    return jax.shard_map(
        body,
        mesh=mesh,
        in_specs=(
            P("cell", None),
            P("tm", "cell", None),
            P(),
            P("tm", "cell", None, None),
            P("tm", "cell", None, None),
            P("cell"),
        ),
        out_specs=P("tm", "cell", None),
        check_vma=False,
    )
```

```python
import functools

import jax
import jax.numpy as jnp
from jax import lax
from jax.experimental import pallas as pl
from jax.experimental.pallas import tpu as pltpu
from jax.sharding import PartitionSpec as P

FINE_MAX = 8
FINE_MIN = 4
CLASSES = FINE_MAX - FINE_MIN + 1
MATS = 7
ROWS = 8
OPENING_FLOPS = 10**9
COUNT_ROW = slice(6, 7)
RATE_ROW = slice(7, 8)
F32 = jnp.float32
BF16 = jnp.bfloat16


def high_low(x):
    high = x.astype(BF16).astype(F32)
    return high, x - high


def stacked(w):
    high, low = high_low(w)
    return jnp.concatenate([high, low], axis=0).astype(BF16)


def mul(x, w):
    rows = x.shape[0]
    high, low = high_low(x)
    left = jnp.concatenate([high, low], axis=0).astype(BF16)
    right = jnp.concatenate([high, jnp.zeros_like(low)], axis=0).astype(BF16)
    out = jnp.dot(jnp.concatenate([left, right], axis=1), w, preferred_element_type=F32)
    return out[:rows] + out[rows:]


def row_is(i, shape):
    return lax.broadcasted_iota(jnp.int32, shape, 0) == i


def leading():
    return lax.axis_index("tm") == 0


def from_behind(block, axis, distance):
    n = lax.axis_size(axis)
    return lax.ppermute(block, axis, [(i, (i + distance) % n) for i in range(n)])


def swap_core(block):
    n = lax.axis_size("cell")
    return lax.ppermute(block, "cell", [(i, i ^ 1) for i in range(n)])


def near_size():
    n = lax.axis_size("cell")
    return 4 if n % 8 == 0 else n // 2


def near_groups():
    n, near = lax.axis_size("cell"), near_size()
    return [
        [at + core + 2 * i for i in range(near)]
        for at in range(0, n, 2 * near)
        for core in range(2)
    ]


def far_swap(block, distance):
    n = lax.axis_size("cell")
    return lax.ppermute(block, "cell", [(i, i ^ distance) for i in range(n)])


def exchange(block, groups=None):
    return lax.all_to_all(block, "cell", 0, 0, axis_index_groups=groups)


def call(kernel, name, outs, args, scratch=(), flops=0):
    size = sum(x.size * x.dtype.itemsize for x in args)
    size += sum(x.size * x.dtype.itemsize for x in outs)
    return pl.pallas_call(
        kernel,
        out_shape=outs,
        in_specs=[pl.BlockSpec(memory_space=pltpu.VMEM)] * len(args),
        out_specs=[pl.BlockSpec(memory_space=pltpu.VMEM)] * len(outs),
        scratch_shapes=list(scratch),
        compiler_params=pltpu.CompilerParams(vmem_limit_bytes=24 << 20),
        cost_estimate=pl.CostEstimate(flops=flops, bytes_accessed=size, transcendentals=0),
        name=name,
    )(*args)


def shape(*dims, dtype=F32):
    return jax.ShapeDtypeStruct(dims, dtype)


def group_rows(g, per):
    return slice(g * per, (g + 1) * per)


def block(d, width):
    return slice((d - 1) * width, d * width)


def spread_counts(row):
    per = row.shape[1]
    return jnp.broadcast_to(row.astype(F32), (per, per)).T


def relay_kernel(start, received, source_sums, coarse, end):
    slices, groups, _, _ = coarse.shape
    for g in range(groups):
        V = jnp.where(leading(), start[g], received[g])
        for l in range(slices):
            V = mul(V + source_sums[l, g], stacked(coarse[l, g]))
        end[g] = V


def opening_kernel(out):
    out[...] = jnp.zeros_like(out)


def setup_kernel(everyone, fine, rate, counts, initial, source, coarse, opened,
                 own, other, lows, table, start_sums, source_sums, end):
    slices, groups, width, _ = fine.shape
    per = counts.shape[1]
    half = slices // 2
    core = lax.rem(lax.axis_index("cell"), 2)
    keep = 1.0 - rate[...]
    alive = []
    for g in range(groups):
        k = counts[g:g + 1].astype(F32)
        rows = [
            jnp.sum((k >= q).astype(F32), axis=1, keepdims=True)
            for q in range(FINE_MIN, FINE_MAX + 1)
        ]
        alive.append(rows)
        filled = jnp.zeros((ROWS, width), F32)
        for i, n in enumerate(rows + [None, k, rate[...]]):
            if n is not None:
                filled = jnp.where(row_is(i, filled.shape), n, filled)
        table[g] = filled
    for g in range(groups):
        here = group_rows(g, per)
        k = counts[g:g + 1].astype(F32)
        V = class_sums(initial[here], k)
        start_sums[g] = V
        for l in range(slices):
            S = class_sums(source[l, here], k)
            source_sums[l, g] = S
            V = mul(V + S, stacked(coarse[l, g]))
        end[g] = V
    made = []
    for l in range(slices):
        sums = [0.0] * 4
        e6, e7, e72 = 0.0, 0.0, 0.0
        for g in range(groups):
            w1 = fine[l, g]
            w2 = mul(w1 * keep, stacked(w1))
            first = jnp.concatenate([w1, w2], axis=0)
            w34 = mul(first * keep, stacked(w2))
            w3, w4 = w34[:width], w34[width:]
            lows[l, g, :2 * width] = first
            lows[l, g, 2 * width:] = w34
            sums = [t + w for t, w in zip(sums, (w1, w2, w3, w4))]
            e6 = e6 + alive[g][2] * w1
            e7 = e7 + alive[g][3] * w1
            e72 = e72 + alive[g][3] * w2
        mats = [t * (per / everyone) for t in sums]
        mats += [e6 / everyone, (e6 + e72 - e7) / everyone, e7 / everyone]
        made.append(jnp.concatenate(mats, axis=0))
    first = core == 0
    own[...] = jnp.where(first, jnp.concatenate(made[:half]), jnp.concatenate(made[half:]))
    other[...] = jnp.where(first, jnp.concatenate(made[half:]), jnp.concatenate(made[:half]))


def extend_kernel(everyone, lows, table, source_sums, powers, ofsource):
    slices, groups, _, width = lows.shape
    keep = 1.0 - table[0, RATE_ROW]
    for l in range(slices):
        for g in range(groups):
            ws = [lows[l, g, i * width:(i + 1) * width] for i in range(4)]
            w58 = mul(lows[l, g] * keep, stacked(ws[3]))
            ws += [w58[i * width:(i + 1) * width] for i in range(4)]
            ws.append((ws[0] + ws[1]) + (ws[2] + ws[3]))
            for i, w in enumerate(ws):
                powers[l, g, :, block(i + 1, width)] = stacked(w)
    for l in range(slices):
        rows = 0.0
        for g in range(groups):
            w = powers[l, g, :, :FINE_MAX * width]
            rows = rows + sums_of_source(source_sums[l, g], w, width)
        ofsource[l * ROWS:(l + 1) * ROWS] = rows / everyone


def add_kernel(a, b, out):
    out[...] = a[...] + b[...]


def class_sums(state, k):
    least = (FINE_MIN + lax.broadcasted_iota(jnp.int32, (ROWS, k.shape[1]), 0)).astype(F32)
    mask = (k >= least).astype(F32)
    left = jnp.concatenate([mask, mask], axis=1)
    left = jnp.concatenate([left, jnp.zeros_like(left)], axis=0).astype(BF16)
    return jnp.dot(left, stacked(state), preferred_element_type=F32)[:ROWS]


def picked(products, first, width):
    out = jnp.zeros((ROWS, width), F32)
    for i in range(CLASSES):
        d = first + i
        if 1 <= d <= FINE_MAX:
            out = out + jnp.where(row_is(i, out.shape), products[:, block(d, width)], 0.0)
    return out


def sums_of_state(V, keep, powers, width):
    x = mul(V * keep, powers)
    rows = [V[0:1]] + [x[0:1, block(m, width)] for m in range(1, FINE_MIN + 1)]
    gain = picked(x, FINE_MIN, width) - picked(x, FINE_MIN - 1, width)
    for i in range(1, 4):
        rows.append(rows[-1] + gain[i:i + 1])
    return jnp.concatenate(rows, axis=0)


def sums_of_source(S, powers, width):
    x = mul(S, powers)
    rows = [jnp.zeros((1, width), F32)]
    for m in range(1, FINE_MAX):
        i = max(m - FINE_MIN, 0)
        rows.append(rows[-1] + x[i:i + 1, block(m, width)])
    return jnp.concatenate(rows, axis=0)


def by_count(products, k, first, width):
    out = jnp.zeros(k.shape, F32)
    for i in range(CLASSES):
        d = i * width
        out = jnp.where(k == float(FINE_MIN + i), products[:, d:d + width], out)
    return out


def base_kernel(everyone, sums, received, source_sums, coarse, powers, table, ofsource, base):
    slices, groups, width, _ = coarse.shape
    keep = 1.0 - table[0, RATE_ROW]
    states = [jnp.where(leading(), sums[g], received[g]) for g in range(groups)]
    for l in range(slices):
        rows = 0.0
        for g in range(groups):
            V = states[g]
            rows = rows + sums_of_state(V, keep, powers[l, g, :, :FINE_MAX * width], width)
            if l + 1 < slices:
                states[g] = mul(V + source_sums[l, g], stacked(coarse[l, g]))
        at = slice(l * ROWS, (l + 1) * ROWS)
        base[at] = rows / everyone + ofsource[at]


def sweep_kernel(first, last, *refs):
    if first:
        initial, source, coarse, powers, table, *outs = refs
    else:
        initial, received, source, coarse, powers, table, *outs = refs
    slices, groups, width, _ = coarse.shape
    per = initial.shape[0] // groups
    keep = 1.0 - table[0, RATE_ROW]
    counts = [spread_counts(table[g, COUNT_ROW]) for g in range(groups)]
    held = []
    for g in range(groups):
        here = group_rows(g, per)
        start = initial[here]
        states = [start] * 3
        if not first:
            states = [jnp.where(leading(), start, received[i, here]) for i in range(3)]
        held.append(states)
    for l in range(slices):
        for g in range(groups):
            here = group_rows(g, per)
            states, n, s = held[g], counts[g], source[l, here]
            if last:
                outs[0][l, g] = class_sums(states[1], table[g, COUNT_ROW])
            w = powers[l, g, :, FINE_MIN * width:]
            x = mul(s, w)
            total = x[:, FINE_MIN * width:]
            sourced = jnp.where(n == float(FINE_MIN), total, 0.0)
            for i in range(CLASSES - 1):
                total = total + x[:, i * width:(i + 1) * width]
                sourced = jnp.where(n == float(FINE_MIN + 1 + i), total, sourced)
            both = jnp.concatenate(states[:2], axis=0) * keep
            x = mul(both, powers[l, g, :, (FINE_MIN - 1) * width:FINE_MAX * width])
            moved = mul(
                jnp.concatenate(
                    [states[0] + s, states[1] - states[0], states[2] - states[1]], axis=0
                ),
                stacked(coarse[l, g]),
            )
            held[g] = [
                moved[:per],
                sourced + by_count(x[:per], n, FINE_MIN, width) + moved[per:2 * per],
                sourced + by_count(x[per:], n, FINE_MIN, width) + moved[2 * per:],
            ]
            if last:
                outs[1][l, here] = held[g][2]
    if not last:
        for g in range(groups):
            for i in range(3):
                outs[0][i, group_rows(g, per)] = held[g][i]


def middle_kernel(parts, base, out):
    n, rows, _ = parts.shape
    total = parts[0]
    for p in range(1, n):
        total = total + parts[p]
    out[:rows] = total
    out[rows:] = base[...]


def gather_kernel(a, b, out):
    total = a[...] + b[...]
    for p in range(out.shape[0]):
        out[p] = total


def wide(row):
    return jnp.broadcast_to(row, (ROWS, row.shape[-1]))


def assembled(known, width):
    out = jnp.zeros((ROWS, width), F32)
    for m, a in enumerate(known):
        out = jnp.where(row_is(m, out.shape), a, out)
    return out


def first_averages(rows, mixing, rate, width):
    slices = len(rows)
    known = [[] for _ in range(slices)]
    sent = [[] for _ in range(slices)]
    for m in range(FINE_MIN + 1):
        for l in range(slices):
            a = wide(rows[l][m])
            for j in range(m):
                a = a + sent[l][j][:, block(m - j, width)]
            known[l].append(a)
            if m < FINE_MIN:
                sent[l].append(mul(a * rate, mixing[l, :, :(FINE_MIN - m) * width]))
    return [assembled(a, width) for a in known]


def shifted(products, width):
    out = jnp.zeros((2 * ROWS, width), F32)
    empty = jnp.zeros((ROWS, width), F32)
    for d in range(1, products.shape[1] // width + 1):
        z = jnp.concatenate([products[:, block(d, width)], empty], axis=0)
        out = out + pltpu.roll(z, d, 0)
    return out


def second_rows(everyone, per, a, base, rate, powers, table, partial, l, width):
    groups = powers.shape[1]
    rows = [0.0] * 3
    for g in range(groups):
        h = shifted(mul(a * rate, powers[l, g, :, :FINE_MAX * width]), width)
        partial[l, g] = h
        total = per * h[4:5]
        for i in range(1, 4):
            total = total + table[g, i:i + 1] * (h[4 + i:5 + i] - h[3 + i:4 + i])
            rows[i - 1] = rows[i - 1] + total
    at = l * ROWS + FINE_MIN + 1
    return [rows[i] / everyone + base[at + i:at + i + 1] for i in range(3)]


def send_line(rows, out):
    line = jnp.concatenate(rows, axis=1)
    for p in range(out.shape[0]):
        out[p] = line


def received_rows(received, width):
    total = received[0]
    for p in range(1, received.shape[0]):
        total = total + received[p]
    return [total[:, i:i + width] for i in range(0, total.shape[1], width)]


def send_rows(everyone, per, a, base, rate, powers, table, partial, out, width):
    rows = []
    for l in range(powers.shape[0]):
        rows += second_rows(everyone, per, a[l], base, rate, powers, table, partial, l, width)
    send_line(rows, out)


def mixing_kernel(everyone, per, mine, theirs, base, powers, table,
                  mixing, partial, out, held):
    slices, _, _, wider = powers.shape
    width = wider // (FINE_MAX + 1)
    half = slices // 2
    n, rows, _ = mine.shape
    rows -= slices * ROWS
    rate = table[0, RATE_ROW]
    core = lax.rem(lax.axis_index("cell"), 2)
    mixed = 0.0
    for ref, at in ((mine, core), (theirs, 1 - core)):
        for p in range(n):
            place = at * (half * MATS * width) + p * rows
            held[pl.ds(place, rows), :] = ref[p, :rows]
            mixed = mixed + ref[p, rows:]
    def place(l, i):
        at = (l * MATS + i) * width
        mixing[l, :, block(i + 1, width)] = stacked(held[at:at + width])

    for l in range(slices):
        for i in range(FINE_MIN):
            place(l, i)
    rows = [
        [mixed[l * ROWS + m:l * ROWS + m + 1] for m in range(FINE_MIN + 1)]
        for l in range(slices)
    ]
    a = first_averages(rows, mixing, rate, width)
    for l in range(slices):
        for i in range(FINE_MIN, MATS):
            place(l, i)
    send_rows(everyone, per, a, base, rate, powers, table, partial, out, width)


def first_kernel(everyone, per, received, base, mixing, powers, table, partial, out):
    slices, _, _, wider = powers.shape
    width = wider // (FINE_MAX + 1)
    rate = table[0, RATE_ROW]
    rows = received_rows(received, width)
    known = FINE_MIN + 1
    rows = [rows[l * known:(l + 1) * known] for l in range(slices)]
    a = first_averages(rows, mixing, rate, width)
    send_rows(everyone, per, a, base, rate, powers, table, partial, out, width)


def push_kernel(received, partial, mixing, powers, table, coarse, *refs):
    starts, (pushes, end) = (None, refs) if len(refs) == 2 else (refs[0], refs[1:])
    slices, groups, _, wider = powers.shape
    width = wider // (FINE_MAX + 1)
    r = table[0, RATE_ROW]
    rows = received_rows(received, width)
    fives = [wide(rows[3 * l]) for l in range(slices)]
    fed = [mul(fives[l] * r, mixing[l, :, 4 * width:6 * width]) for l in range(slices)]
    sixes = [wide(rows[3 * l + 1]) + fed[l][:, :width] for l in range(slices)]
    late = [mul(sixes[l] * r, mixing[l, :, 6 * width:]) for l in range(slices)]
    h = [[None] * groups for _ in range(slices)]
    for l in range(slices):
        a = jnp.zeros((ROWS, width), F32)
        seven = wide(rows[3 * l + 2]) + fed[l][:, width:] + late[l]
        for m, row in ((5, fives[l]), (6, sixes[l]), (7, seven)):
            a = jnp.where(row_is(m, a.shape), row, a)
        for g in range(groups):
            z = mul(a * r, powers[l, g, :, :3 * width])
            h[l][g] = (partial[l, g] + shifted(z, width))[FINE_MIN:FINE_MIN + ROWS]
            if starts is not None:
                w = powers[l, g, :, (FINE_MIN - 1) * width:FINE_MAX * width]
                h[l][g] = h[l][g] + picked(mul(starts[l, g] * (1.0 - r), w), 1, width)
    x = [jnp.zeros((ROWS, width), F32) for _ in range(groups)]
    for l in range(slices):
        for g in range(groups):
            old = x[g] if starts is None else x[g] - starts[l, g]
            x[g] = h[l][g] + mul(old, stacked(coarse[l, g]))
            pushes[l, g] = h[l][g]
    for g in range(groups):
        end[g] = x[g]


def vectors_kernel(received, pushes, starts, coarse, end):
    slices, groups, _, _ = coarse.shape
    for g in range(groups):
        x = jnp.where(leading(), 0.0, received[g])
        for l in range(slices):
            x = pushes[l, g] + mul(x - starts[l, g], stacked(coarse[l, g]))
        end[g] = x


def second_kernel(everyone, received, pushes, coarse, sums, table, powers, ofsource,
                  starts, base, out):
    slices, groups, width, _ = coarse.shape
    keep = 1.0 - table[0, RATE_ROW]
    x = [jnp.where(leading(), 0.0, received[g]) for g in range(groups)]
    sent = []
    for l in range(slices):
        rows = 0.0
        for g in range(groups):
            starts[l, g] = x[g]
            n = table[g]
            exact = n - pltpu.roll(n, ROWS - 1, 0)
            exact = jnp.where(row_is(ROWS - 1, n.shape), 0.0, exact)
            weighted = exact * x[g]
            tail = jnp.zeros((1, width), F32)
            V = sums[l, g]
            for i in reversed(range(CLASSES)):
                tail = tail + weighted[i:i + 1]
                V = jnp.where(row_is(i, V.shape), V + tail, V)
            rows = rows + sums_of_state(V, keep, powers[l, g, :, :FINE_MAX * width], width)
            if l + 1 < slices:
                x[g] = pushes[l, g] + mul(x[g], stacked(coarse[l, g]))
        at = slice(l * ROWS, (l + 1) * ROWS)
        rows = rows / everyone + ofsource[at]
        base[at] = rows
        sent += [rows[m:m + 1] for m in range(FINE_MIN + 1)]
    send_line(sent, out)


def finish_kernel(received, pushes, starts, coarse, ends, table, out):
    slices, groups, width, _ = coarse.shape
    per = ends.shape[1] // groups
    counts = [spread_counts(table[g, COUNT_ROW]) for g in range(groups)]
    x = [jnp.where(leading(), 0.0, received[g]) for g in range(groups)]
    for l in range(slices):
        for g in range(groups):
            here = group_rows(g, per)
            x[g] = pushes[l, g] + mul(x[g] - starts[l, g], stacked(coarse[l, g]))
            add = jnp.zeros((per, width), F32)
            for i in range(CLASSES):
                add = jnp.where(counts[g] == float(FINE_MIN + i), x[g][i:i + 1], add)
            out[l, here] = ends[l, here] + add


def body(initial, source, mix_rate, fine, coarse, step_counts):
    slices, groups, width, _ = fine.shape
    cells = initial.shape[0]
    per = cells // groups
    n_cell = lax.axis_size("cell")
    turns = lax.axis_size("tm") - 1
    everyone = cells * n_cell
    half = slices // 2
    near = near_size()
    shard = half * MATS * width // near
    rate = mix_rate.reshape(1, width)
    counts = step_counts.reshape(groups, per)
    state = shape(cells, width)
    states = shape(slices, cells, width)
    vectors = shape(slices, groups, ROWS, width)
    vector = shape(groups, ROWS, width)
    rows8 = shape(slices * ROWS, width)
    line3 = shape(n_cell, 1, slices * 3 * width)
    line5 = shape(n_cell, 1, slices * (FINE_MIN + 1) * width)
    partial = shape(slices, groups, 2 * ROWS, width)
    mats = shape(half * MATS * width, width)
    opened, = call(opening_kernel, "opening", [shape(ROWS, width)], (), flops=OPENING_FLOPS)
    own, other, lows, table, sums0, source_sums, moved = call(
        functools.partial(setup_kernel, everyone), "setup",
        [mats, mats, shape(slices, groups, 4 * width, width), vector, vector, vectors, vector],
        (fine, rate, counts, initial, source, coarse, opened),
    )
    for turn in range(turns):
        moved = from_behind(moved, "tm", 1)
        if turn + 1 < turns:
            moved, = call(relay_kernel, "relay", [vector], (sums0, moved, source_sums, coarse))
    swapped = swap_core(other)
    powers, ofsource = call(
        functools.partial(extend_kernel, everyone), "extend",
        [shape(slices, groups, 2 * width, (FINE_MAX + 1) * width, dtype=BF16), rows8],
        (lows, table, source_sums),
    )
    base, = call(
        functools.partial(base_kernel, everyone), "base", [rows8],
        (sums0, moved, source_sums, coarse, powers, table, ofsource),
    )
    swapped, base = lax.optimization_barrier((swapped, base))
    mine, = call(add_kernel, "add", [mats], (own, swapped))
    parts = exchange(mine.reshape(near, shard, width), near_groups())
    block, = call(
        middle_kernel, "middle", [shape(shard + slices * ROWS, width)], (parts, base)
    )
    block, later = lax.optimization_barrier((block, initial))
    bundle = shape(3, cells, width)
    sent, = call(
        functools.partial(sweep_kernel, True, False), "sweep", [bundle],
        (later, source, coarse, powers, table),
    )
    far = jnp.zeros_like(block)
    distance = 2 * near
    while distance < n_cell:
        far = far_swap(block, distance)
        distance *= 2
        if distance < n_cell:
            block = block + far
    far, sent = lax.optimization_barrier((far, sent))
    for turn in range(turns):
        sent = from_behind(sent, "tm", 1)
        if turn + 1 < turns:
            sent, = call(
                functools.partial(sweep_kernel, False, False), "sweep", [bundle],
                (initial, sent, source, coarse, powers, table),
            )
    payload, = call(
        gather_kernel, "gather", [shape(near, shard + slices * ROWS, width)], (block, far)
    )
    gathered = exchange(payload, near_groups())
    sums, ends = call(
        functools.partial(sweep_kernel, False, True), "sweep", [vectors, states],
        (initial, sent, source, coarse, powers, table),
    )
    theirs = swap_core(gathered)
    mixing, first, out = call(
        functools.partial(mixing_kernel, everyone, per), "mixing",
        [shape(slices, 2 * width, MATS * width, dtype=BF16), partial, line3],
        (gathered, theirs, base, powers, table),
        scratch=[pltpu.VMEM((slices * MATS * width, width), F32)],
    )
    pushes1, end = call(
        push_kernel, "push", [vectors, vector],
        (exchange(out), first, mixing, powers, table, coarse),
    )
    nothing = jnp.zeros(vectors.shape, F32)
    moved = end
    for turn in range(turns):
        moved = from_behind(moved, "tm", 1)
        if turn + 1 < turns:
            moved, = call(vectors_kernel, "vectors", [vector], (moved, pushes1, nothing, coarse))
    moved1, base, out = call(
        functools.partial(second_kernel, everyone), "second",
        [vectors, rows8, line5],
        (moved, pushes1, coarse, sums, table, powers, ofsource),
    )
    first, out = call(
        functools.partial(first_kernel, everyone, per), "first", [partial, line3],
        (exchange(out), base, mixing, powers, table),
    )
    pushes2, end = call(
        push_kernel, "push", [vectors, vector],
        (exchange(out), first, mixing, powers, table, coarse, moved1),
    )
    moved = end
    for turn in range(turns):
        moved = from_behind(moved, "tm", 1)
        if turn + 1 < turns:
            moved, = call(vectors_kernel, "vectors", [vector], (moved, pushes2, moved1, coarse))
    out, = call(
        finish_kernel, "finish", [states], (moved, pushes2, moved1, coarse, ends, table)
    )
    return out


def solution(mesh):
    return jax.shard_map(
        body,
        mesh=mesh,
        in_specs=(
            P("cell", None),
            P("tm", "cell", None),
            P(),
            P("tm", "cell", None, None),
            P("tm", "cell", None, None),
            P("cell"),
        ),
        out_specs=P("tm", "cell", None),
        check_vma=False,
    )
```

```python
import functools

import jax
import jax.numpy as jnp
from jax import lax
from jax.experimental import pallas as pl
from jax.experimental.pallas import tpu as pltpu
from jax.sharding import PartitionSpec as P

FINE_MAX = 8
FINE_MIN = 4
CLASSES = FINE_MAX - FINE_MIN + 1
MATS = 7
ROWS = 8
OPENING_FLOPS = 10**9
COUNT_ROW = slice(6, 7)
RATE_ROW = slice(7, 8)
F32 = jnp.float32
BF16 = jnp.bfloat16


def high_low(x):
    high = x.astype(BF16).astype(F32)
    return high, x - high


def stacked(w):
    high, low = high_low(w)
    return jnp.concatenate([high, low], axis=0).astype(BF16)


def mul(x, w):
    rows = x.shape[0]
    high, low = high_low(x)
    left = jnp.concatenate([high, low], axis=0).astype(BF16)
    right = jnp.concatenate([high, jnp.zeros_like(low)], axis=0).astype(BF16)
    out = jnp.dot(jnp.concatenate([left, right], axis=1), w, preferred_element_type=F32)
    return out[:rows] + out[rows:]


def row_is(i, shape):
    return lax.broadcasted_iota(jnp.int32, shape, 0) == i


def leading():
    return lax.axis_index("tm") == 0


def from_behind(block, axis, distance):
    n = lax.axis_size(axis)
    return lax.ppermute(block, axis, [(i, (i + distance) % n) for i in range(n)])


def swap_core(block):
    n = lax.axis_size("cell")
    return lax.ppermute(block, "cell", [(i, i ^ 1) for i in range(n)])


def near_size():
    n = lax.axis_size("cell")
    return 4 if n % 8 == 0 else n // 2


def near_groups():
    n, near = lax.axis_size("cell"), near_size()
    return [
        [at + core + 2 * i for i in range(near)]
        for at in range(0, n, 2 * near)
        for core in range(2)
    ]


def far_swap(block, distance):
    n = lax.axis_size("cell")
    return lax.ppermute(block, "cell", [(i, i ^ distance) for i in range(n)])


def exchange(block, groups=None):
    return lax.all_to_all(block, "cell", 0, 0, axis_index_groups=groups)


def call(kernel, name, outs, args, scratch=(), flops=0, space=pltpu.VMEM):
    size = sum(x.size * x.dtype.itemsize for x in args)
    size += sum(x.size * x.dtype.itemsize for x in outs)
    return pl.pallas_call(
        kernel,
        out_shape=outs,
        in_specs=[pl.BlockSpec(memory_space=pltpu.VMEM)] * len(args),
        out_specs=[pl.BlockSpec(memory_space=space)] * len(outs),
        scratch_shapes=list(scratch),
        compiler_params=pltpu.CompilerParams(vmem_limit_bytes=24 << 20),
        cost_estimate=pl.CostEstimate(flops=flops, bytes_accessed=size, transcendentals=0),
        name=name,
    )(*args)


def shape(*dims, dtype=F32):
    return jax.ShapeDtypeStruct(dims, dtype)


def group_rows(g, per):
    return slice(g * per, (g + 1) * per)


def block(d, width):
    return slice((d - 1) * width, d * width)


def spread_counts(row):
    per = row.shape[1]
    return jnp.broadcast_to(row.astype(F32), (per, per)).T


def relay_kernel(start, received, source_sums, coarse, end):
    slices, groups, _, _ = coarse.shape
    for g in range(groups):
        V = jnp.where(leading(), start[g], received[g])
        for l in range(slices):
            V = mul(V + source_sums[l, g], stacked(coarse[l, g]))
        end[g] = V


def opening_kernel(out):
    out[...] = jnp.zeros_like(out)


def setup_kernel(everyone, fine, rate, counts, initial, source, coarse, opened,
                 own, other, lows, table, start_sums, source_sums, end):
    slices, groups, width, _ = fine.shape
    per = counts.shape[1]
    half = slices // 2
    core = lax.rem(lax.axis_index("cell"), 2)
    keep = 1.0 - rate[...]
    alive = []
    for g in range(groups):
        k = counts[g:g + 1].astype(F32)
        rows = [
            jnp.sum((k >= q).astype(F32), axis=1, keepdims=True)
            for q in range(FINE_MIN, FINE_MAX + 1)
        ]
        alive.append(rows)
        filled = jnp.zeros((ROWS, width), F32)
        for i, n in enumerate(rows + [None, k, rate[...]]):
            if n is not None:
                filled = jnp.where(row_is(i, filled.shape), n, filled)
        table[g] = filled
    for g in range(groups):
        here = group_rows(g, per)
        k = counts[g:g + 1].astype(F32)
        V = class_sums(initial[here], k)
        start_sums[g] = V
        for l in range(slices):
            S = class_sums(source[l, here], k)
            source_sums[l, g] = S
            V = mul(V + S, stacked(coarse[l, g]))
        end[g] = V
    made = []
    for l in range(slices):
        sums = [0.0] * 4
        e6, e7, e72 = 0.0, 0.0, 0.0
        for g in range(groups):
            w1 = fine[l, g]
            w2 = mul(w1 * keep, stacked(w1))
            first = jnp.concatenate([w1, w2], axis=0)
            w34 = mul(first * keep, stacked(w2))
            w3, w4 = w34[:width], w34[width:]
            lows[l, g, :2 * width] = first
            lows[l, g, 2 * width:] = w34
            sums = [t + w for t, w in zip(sums, (w1, w2, w3, w4))]
            e6 = e6 + alive[g][2] * w1
            e7 = e7 + alive[g][3] * w1
            e72 = e72 + alive[g][3] * w2
        mats = [t * (per / everyone) for t in sums]
        mats += [e6 / everyone, (e6 + e72 - e7) / everyone, e7 / everyone]
        made.append(jnp.concatenate(mats, axis=0))
    first = core == 0
    own[...] = jnp.where(first, jnp.concatenate(made[:half]), jnp.concatenate(made[half:]))
    other[...] = jnp.where(first, jnp.concatenate(made[half:]), jnp.concatenate(made[:half]))


def extend_kernel(everyone, lows, table, source_sums, powers, ofsource):
    slices, groups, _, width = lows.shape
    keep = 1.0 - table[0, RATE_ROW]
    for l in range(slices):
        for g in range(groups):
            ws = [lows[l, g, i * width:(i + 1) * width] for i in range(4)]
            w58 = mul(lows[l, g] * keep, stacked(ws[3]))
            ws += [w58[i * width:(i + 1) * width] for i in range(4)]
            ws.append((ws[0] + ws[1]) + (ws[2] + ws[3]))
            for i, w in enumerate(ws):
                powers[l, g, :, block(i + 1, width)] = stacked(w)
    for l in range(slices):
        rows = 0.0
        for g in range(groups):
            w = powers[l, g, :, :FINE_MAX * width]
            rows = rows + sums_of_source(source_sums[l, g], w, width)
        ofsource[l * ROWS:(l + 1) * ROWS] = rows / everyone


def add_kernel(a, b, out):
    out[...] = a[...] + b[...]


def class_sums(state, k):
    least = (FINE_MIN + lax.broadcasted_iota(jnp.int32, (ROWS, k.shape[1]), 0)).astype(F32)
    mask = (k >= least).astype(F32)
    left = jnp.concatenate([mask, mask], axis=1)
    left = jnp.concatenate([left, jnp.zeros_like(left)], axis=0).astype(BF16)
    return jnp.dot(left, stacked(state), preferred_element_type=F32)[:ROWS]


def picked(products, first, width):
    out = jnp.zeros((ROWS, width), F32)
    for i in range(CLASSES):
        d = first + i
        if 1 <= d <= FINE_MAX:
            out = out + jnp.where(row_is(i, out.shape), products[:, block(d, width)], 0.0)
    return out


def sums_of_state(V, keep, powers, width):
    x = mul(V * keep, powers)
    rows = [V[0:1]] + [x[0:1, block(m, width)] for m in range(1, FINE_MIN + 1)]
    gain = picked(x, FINE_MIN, width) - picked(x, FINE_MIN - 1, width)
    for i in range(1, 4):
        rows.append(rows[-1] + gain[i:i + 1])
    return jnp.concatenate(rows, axis=0)


def sums_of_source(S, powers, width):
    x = mul(S, powers)
    rows = [jnp.zeros((1, width), F32)]
    for m in range(1, FINE_MAX):
        i = max(m - FINE_MIN, 0)
        rows.append(rows[-1] + x[i:i + 1, block(m, width)])
    return jnp.concatenate(rows, axis=0)


def by_count(products, k, first, width):
    out = jnp.zeros(k.shape, F32)
    for i in range(CLASSES):
        d = i * width
        out = jnp.where(k == float(FINE_MIN + i), products[:, d:d + width], out)
    return out


def base_kernel(everyone, sums, received, source_sums, coarse, powers, table, ofsource, base):
    slices, groups, width, _ = coarse.shape
    keep = 1.0 - table[0, RATE_ROW]
    states = [jnp.where(leading(), sums[g], received[g]) for g in range(groups)]
    for l in range(slices):
        rows = 0.0
        for g in range(groups):
            V = states[g]
            rows = rows + sums_of_state(V, keep, powers[l, g, :, :FINE_MAX * width], width)
            if l + 1 < slices:
                states[g] = mul(V + source_sums[l, g], stacked(coarse[l, g]))
        at = slice(l * ROWS, (l + 1) * ROWS)
        base[at] = rows / everyone + ofsource[at]


def sweep_kernel(first, last, *refs):
    if first:
        initial, source, coarse, powers, table, *outs = refs
    else:
        initial, received, source, coarse, powers, table, *outs = refs
    slices, groups, width, _ = coarse.shape
    per = initial.shape[0] // groups
    keep = 1.0 - table[0, RATE_ROW]
    counts = [spread_counts(table[g, COUNT_ROW]) for g in range(groups)]
    held = []
    for g in range(groups):
        here = group_rows(g, per)
        start = initial[here]
        states = [start] * 3
        if not first:
            states = [jnp.where(leading(), start, received[i, here]) for i in range(3)]
        held.append(states)
    for l in range(slices):
        for g in range(groups):
            here = group_rows(g, per)
            states, n, s = held[g], counts[g], source[l, here]
            if last:
                outs[0][l, g] = class_sums(states[1], table[g, COUNT_ROW])
            w = powers[l, g, :, FINE_MIN * width:]
            x = mul(s, w)
            total = x[:, FINE_MIN * width:]
            sourced = jnp.where(n == float(FINE_MIN), total, 0.0)
            for i in range(CLASSES - 1):
                total = total + x[:, i * width:(i + 1) * width]
                sourced = jnp.where(n == float(FINE_MIN + 1 + i), total, sourced)
            both = jnp.concatenate(states[:2], axis=0) * keep
            x = mul(both, powers[l, g, :, (FINE_MIN - 1) * width:FINE_MAX * width])
            moved = mul(
                jnp.concatenate(
                    [states[0] + s, states[1] - states[0], states[2] - states[1]], axis=0
                ),
                stacked(coarse[l, g]),
            )
            held[g] = [
                moved[:per],
                sourced + by_count(x[:per], n, FINE_MIN, width) + moved[per:2 * per],
                sourced + by_count(x[per:], n, FINE_MIN, width) + moved[2 * per:],
            ]
            if last:
                outs[1][l, here] = held[g][2]
    if not last:
        for g in range(groups):
            for i in range(3):
                outs[0][i, group_rows(g, per)] = held[g][i]


def middle_kernel(parts, base, out):
    n, rows, _ = parts.shape
    total = parts[0]
    for p in range(1, n):
        total = total + parts[p]
    out[:rows] = total
    out[rows:] = base[...]


def gather_kernel(a, b, out):
    total = a[...] + b[...]
    for p in range(out.shape[0]):
        out[p] = total


def wide(row):
    return jnp.broadcast_to(row, (ROWS, row.shape[-1]))


def assembled(known, width):
    out = jnp.zeros((ROWS, width), F32)
    for m, a in enumerate(known):
        out = jnp.where(row_is(m, out.shape), a, out)
    return out


def first_averages(rows, mixing, rate, width):
    slices = len(rows)
    known = [[] for _ in range(slices)]
    sent = [[] for _ in range(slices)]
    for m in range(FINE_MIN + 1):
        for l in range(slices):
            a = wide(rows[l][m])
            for j in range(m):
                a = a + sent[l][j][:, block(m - j, width)]
            known[l].append(a)
            if m < FINE_MIN:
                sent[l].append(mul(a * rate, mixing[l, :, :(FINE_MIN - m) * width]))
    return [assembled(a, width) for a in known]


def shifted(products, width):
    out = jnp.zeros((2 * ROWS, width), F32)
    empty = jnp.zeros((ROWS, width), F32)
    for d in range(1, products.shape[1] // width + 1):
        z = jnp.concatenate([products[:, block(d, width)], empty], axis=0)
        out = out + pltpu.roll(z, d, 0)
    return out


def second_rows(everyone, per, a, base, rate, powers, table, partial, l, width):
    groups = powers.shape[1]
    rows = [0.0] * 3
    for g in range(groups):
        h = shifted(mul(a * rate, powers[l, g, :, :FINE_MAX * width]), width)
        partial[l, g] = h
        total = per * h[4:5]
        for i in range(1, 4):
            total = total + table[g, i:i + 1] * (h[4 + i:5 + i] - h[3 + i:4 + i])
            rows[i - 1] = rows[i - 1] + total
    at = l * ROWS + FINE_MIN + 1
    return [rows[i] / everyone + base[at + i:at + i + 1] for i in range(3)]


def send_line(rows, out):
    line = jnp.concatenate(rows, axis=1)
    for p in range(out.shape[0]):
        out[p] = line


def received_rows(received, width):
    total = received[0]
    for p in range(1, received.shape[0]):
        total = total + received[p]
    return [total[:, i:i + width] for i in range(0, total.shape[1], width)]


def send_rows(everyone, per, a, base, rate, powers, table, partial, out, width):
    rows = []
    for l in range(powers.shape[0]):
        rows += second_rows(everyone, per, a[l], base, rate, powers, table, partial, l, width)
    send_line(rows, out)


def unpacked(parts, kept, held):
    n, rows, _ = parts.shape
    rows -= kept
    mixed = parts[0, rows:]
    for p in range(n):
        held[p * rows:(p + 1) * rows] = parts[p, :rows]
        if p:
            mixed = mixed + parts[p, rows:]
    return mixed


def own_kernel(kept, mine, ready, mixed, held):
    half, _, wider = ready.shape
    width = wider // MATS
    mixed[...] = unpacked(mine, kept, held)
    for h in range(half):
        for i in range(MATS):
            at = (h * MATS + i) * width
            ready[h, :, block(i + 1, width)] = stacked(held[at:at + width])


def mixing_kernel(everyone, per, theirs, ready, mine, base, powers, table,
                  mixing, partial, out, held):
    slices, _, _, wider = powers.shape
    width = wider // (FINE_MAX + 1)
    half = slices // 2
    rate = table[0, RATE_ROW]
    core = lax.rem(lax.axis_index("cell"), 2)
    mixing[pl.ds(core * half, half)] = ready[...]
    mixed = mine[...] + unpacked(theirs, slices * ROWS, held)

    def place(h, i):
        at = (h * MATS + i) * width
        mixing[(1 - core) * half + h, :, block(i + 1, width)] = stacked(held[at:at + width])

    for h in range(half):
        for i in range(MATS):
            place(h, i)
    rows = [
        [mixed[l * ROWS + m:l * ROWS + m + 1] for m in range(FINE_MIN + 1)]
        for l in range(slices)
    ]
    a = first_averages(rows, mixing, rate, width)
    send_rows(everyone, per, a, base, rate, powers, table, partial, out, width)


def first_kernel(everyone, per, received, base, mixing, powers, table, partial, out):
    slices, _, _, wider = powers.shape
    width = wider // (FINE_MAX + 1)
    rate = table[0, RATE_ROW]
    rows = received_rows(received, width)
    known = FINE_MIN + 1
    rows = [rows[l * known:(l + 1) * known] for l in range(slices)]
    a = first_averages(rows, mixing, rate, width)
    send_rows(everyone, per, a, base, rate, powers, table, partial, out, width)


def push_kernel(received, partial, mixing, powers, table, coarse, *refs):
    starts, (pushes, end) = (None, refs) if len(refs) == 2 else (refs[0], refs[1:])
    slices, groups, _, wider = powers.shape
    width = wider // (FINE_MAX + 1)
    r = table[0, RATE_ROW]
    rows = received_rows(received, width)
    fives = [wide(rows[3 * l]) for l in range(slices)]
    fed = [mul(fives[l] * r, mixing[l, :, 4 * width:6 * width]) for l in range(slices)]
    sixes = [wide(rows[3 * l + 1]) + fed[l][:, :width] for l in range(slices)]
    late = [mul(sixes[l] * r, mixing[l, :, 6 * width:]) for l in range(slices)]
    h = [[None] * groups for _ in range(slices)]
    for l in range(slices):
        a = jnp.zeros((ROWS, width), F32)
        seven = wide(rows[3 * l + 2]) + fed[l][:, width:] + late[l]
        for m, row in ((5, fives[l]), (6, sixes[l]), (7, seven)):
            a = jnp.where(row_is(m, a.shape), row, a)
        for g in range(groups):
            z = mul(a * r, powers[l, g, :, :3 * width])
            h[l][g] = (partial[l, g] + shifted(z, width))[FINE_MIN:FINE_MIN + ROWS]
            if starts is not None:
                w = powers[l, g, :, (FINE_MIN - 1) * width:FINE_MAX * width]
                h[l][g] = h[l][g] + picked(mul(starts[l, g] * (1.0 - r), w), 1, width)
    x = [jnp.zeros((ROWS, width), F32) for _ in range(groups)]
    for l in range(slices):
        for g in range(groups):
            old = x[g] if starts is None else x[g] - starts[l, g]
            x[g] = h[l][g] + mul(old, stacked(coarse[l, g]))
            pushes[l, g] = h[l][g]
    for g in range(groups):
        end[g] = x[g]


def vectors_kernel(received, pushes, starts, coarse, end):
    slices, groups, _, _ = coarse.shape
    for g in range(groups):
        x = jnp.where(leading(), 0.0, received[g])
        for l in range(slices):
            x = pushes[l, g] + mul(x - starts[l, g], stacked(coarse[l, g]))
        end[g] = x


def second_kernel(everyone, received, pushes, coarse, sums, table, powers, ofsource,
                  starts, base, out):
    slices, groups, width, _ = coarse.shape
    keep = 1.0 - table[0, RATE_ROW]
    x = [jnp.where(leading(), 0.0, received[g]) for g in range(groups)]
    sent = []
    for l in range(slices):
        rows = 0.0
        for g in range(groups):
            starts[l, g] = x[g]
            n = table[g]
            exact = n - pltpu.roll(n, ROWS - 1, 0)
            exact = jnp.where(row_is(ROWS - 1, n.shape), 0.0, exact)
            weighted = exact * x[g]
            tail = jnp.zeros((1, width), F32)
            V = sums[l, g]
            for i in reversed(range(CLASSES)):
                tail = tail + weighted[i:i + 1]
                V = jnp.where(row_is(i, V.shape), V + tail, V)
            rows = rows + sums_of_state(V, keep, powers[l, g, :, :FINE_MAX * width], width)
            if l + 1 < slices:
                x[g] = pushes[l, g] + mul(x[g], stacked(coarse[l, g]))
        at = slice(l * ROWS, (l + 1) * ROWS)
        rows = rows / everyone + ofsource[at]
        base[at] = rows
        sent += [rows[m:m + 1] for m in range(FINE_MIN + 1)]
    send_line(sent, out)


def finish_kernel(received, pushes, starts, coarse, ends, table, out, held, sent):
    slices, groups, width, _ = coarse.shape
    per = ends.shape[1] // groups
    counts = [spread_counts(table[g, COUNT_ROW]) for g in range(groups)]
    x = [jnp.where(leading(), 0.0, received[g]) for g in range(groups)]
    copies = []
    for l in range(slices):
        for g in range(groups):
            here = group_rows(g, per)
            x[g] = pushes[l, g] + mul(x[g] - starts[l, g], stacked(coarse[l, g]))
            add = jnp.zeros((per, width), F32)
            for i in range(CLASSES):
                add = jnp.where(counts[g] == float(FINE_MIN + i), x[g][i:i + 1], add)
            held[l, here] = ends[l, here] + add
            copies.append(
                pltpu.make_async_copy(
                    held.at[l, here], out.at[l, here], sent.at[l * groups + g]
                )
            )
            copies[-1].start()
    for copy in copies:
        copy.wait()


def body(initial, source, mix_rate, fine, coarse, step_counts):
    slices, groups, width, _ = fine.shape
    cells = initial.shape[0]
    per = cells // groups
    n_cell = lax.axis_size("cell")
    turns = lax.axis_size("tm") - 1
    everyone = cells * n_cell
    half = slices // 2
    near = near_size()
    shard = half * MATS * width // near
    rate = mix_rate.reshape(1, width)
    counts = step_counts.reshape(groups, per)
    state = shape(cells, width)
    states = shape(slices, cells, width)
    vectors = shape(slices, groups, ROWS, width)
    vector = shape(groups, ROWS, width)
    rows8 = shape(slices * ROWS, width)
    line3 = shape(n_cell, 1, slices * 3 * width)
    line5 = shape(n_cell, 1, slices * (FINE_MIN + 1) * width)
    partial = shape(slices, groups, 2 * ROWS, width)
    mats = shape(half * MATS * width, width)
    opened, = call(opening_kernel, "opening", [shape(ROWS, width)], (), flops=OPENING_FLOPS)
    own, other, lows, table, sums0, source_sums, moved = call(
        functools.partial(setup_kernel, everyone), "setup",
        [mats, mats, shape(slices, groups, 4 * width, width), vector, vector, vectors, vector],
        (fine, rate, counts, initial, source, coarse, opened),
    )
    for turn in range(turns):
        moved = from_behind(moved, "tm", 1)
        if turn + 1 < turns:
            moved, = call(relay_kernel, "relay", [vector], (sums0, moved, source_sums, coarse))
    swapped = swap_core(other)
    powers, ofsource = call(
        functools.partial(extend_kernel, everyone), "extend",
        [shape(slices, groups, 2 * width, (FINE_MAX + 1) * width, dtype=BF16), rows8],
        (lows, table, source_sums),
    )
    base, = call(
        functools.partial(base_kernel, everyone), "base", [rows8],
        (sums0, moved, source_sums, coarse, powers, table, ofsource),
    )
    swapped, base = lax.optimization_barrier((swapped, base))
    mine, = call(add_kernel, "add", [mats], (own, swapped))
    parts = exchange(mine.reshape(near, shard, width), near_groups())
    block, = call(
        middle_kernel, "middle", [shape(shard + slices * ROWS, width)], (parts, base)
    )
    block, later = lax.optimization_barrier((block, initial))
    bundle = shape(3, cells, width)
    sent, = call(
        functools.partial(sweep_kernel, True, False), "sweep", [bundle],
        (later, source, coarse, powers, table),
    )
    far = jnp.zeros_like(block)
    distance = 2 * near
    while distance < n_cell:
        far = far_swap(block, distance)
        distance *= 2
        if distance < n_cell:
            block = block + far
    far, sent = lax.optimization_barrier((far, sent))
    for turn in range(turns):
        sent = from_behind(sent, "tm", 1)
        if turn + 1 < turns:
            sent, = call(
                functools.partial(sweep_kernel, False, False), "sweep", [bundle],
                (initial, sent, source, coarse, powers, table),
            )
    payload, = call(
        gather_kernel, "gather", [shape(near, shard + slices * ROWS, width)], (block, far)
    )
    gathered = exchange(payload, near_groups())
    sums, ends = call(
        functools.partial(sweep_kernel, False, True), "sweep", [vectors, states],
        (initial, sent, source, coarse, powers, table),
    )
    theirs = swap_core(gathered)
    ready, mixed = call(
        functools.partial(own_kernel, slices * ROWS), "own",
        [shape(half, 2 * width, MATS * width, dtype=BF16), rows8], (gathered,),
        scratch=[pltpu.VMEM((half * MATS * width, width), F32)],
    )
    mixing, first, out = call(
        functools.partial(mixing_kernel, everyone, per), "mixing",
        [shape(slices, 2 * width, MATS * width, dtype=BF16), partial, line3],
        (theirs, ready, mixed, base, powers, table),
        scratch=[pltpu.VMEM((half * MATS * width, width), F32)],
    )
    pushes1, end = call(
        push_kernel, "push", [vectors, vector],
        (exchange(out), first, mixing, powers, table, coarse),
    )
    nothing = jnp.zeros(vectors.shape, F32)
    moved = end
    for turn in range(turns):
        moved = from_behind(moved, "tm", 1)
        if turn + 1 < turns:
            moved, = call(vectors_kernel, "vectors", [vector], (moved, pushes1, nothing, coarse))
    moved1, base, out = call(
        functools.partial(second_kernel, everyone), "second",
        [vectors, rows8, line5],
        (moved, pushes1, coarse, sums, table, powers, ofsource),
    )
    first, out = call(
        functools.partial(first_kernel, everyone, per), "first", [partial, line3],
        (exchange(out), base, mixing, powers, table),
    )
    pushes2, end = call(
        push_kernel, "push", [vectors, vector],
        (exchange(out), first, mixing, powers, table, coarse, moved1),
    )
    moved = end
    for turn in range(turns):
        moved = from_behind(moved, "tm", 1)
        if turn + 1 < turns:
            moved, = call(vectors_kernel, "vectors", [vector], (moved, pushes2, moved1, coarse))
    out, = call(
        finish_kernel, "finish", [states], (moved, pushes2, moved1, coarse, ends, table),
        scratch=[
            pltpu.VMEM((slices, cells, width), F32),
            pltpu.SemaphoreType.DMA((slices * groups,)),
        ],
        space=pltpu.HBM,
    )
    return out


def solution(mesh):
    return jax.shard_map(
        body,
        mesh=mesh,
        in_specs=(
            P("cell", None),
            P("tm", "cell", None),
            P(),
            P("tm", "cell", None, None),
            P("tm", "cell", None, None),
            P("cell"),
        ),
        out_specs=P("tm", "cell", None),
        check_vma=False,
    )
```

```python
import functools

import jax
import jax.numpy as jnp
from jax import lax
from jax.experimental import pallas as pl
from jax.experimental.pallas import tpu as pltpu
from jax.sharding import PartitionSpec as P

FINE_MAX = 8
FINE_MIN = 4
CLASSES = FINE_MAX - FINE_MIN + 1
MATS = 7
ROWS = 8
OPENING_FLOPS = 10**9
COUNT_ROW = slice(6, 7)
RATE_ROW = slice(7, 8)
F32 = jnp.float32
BF16 = jnp.bfloat16


def high_low(x):
    high = x.astype(BF16).astype(F32)
    return high, x - high


def stacked(w):
    high, low = high_low(w)
    return jnp.concatenate([high, low], axis=0).astype(BF16)


def mul(x, w):
    rows = x.shape[0]
    high, low = high_low(x)
    left = jnp.concatenate([high, low], axis=0).astype(BF16)
    right = jnp.concatenate([high, jnp.zeros_like(low)], axis=0).astype(BF16)
    out = jnp.dot(jnp.concatenate([left, right], axis=1), w, preferred_element_type=F32)
    return out[:rows] + out[rows:]


def row_is(i, shape):
    return lax.broadcasted_iota(jnp.int32, shape, 0) == i


def leading():
    return lax.axis_index("tm") == 0


def from_behind(block, axis, distance):
    n = lax.axis_size(axis)
    return lax.ppermute(block, axis, [(i, (i + distance) % n) for i in range(n)])


def swap_core(block):
    n = lax.axis_size("cell")
    return lax.ppermute(block, "cell", [(i, i ^ 1) for i in range(n)])


def near_size():
    n = lax.axis_size("cell")
    return 4 if n % 8 == 0 else n // 2


def near_groups():
    n, near = lax.axis_size("cell"), near_size()
    return [
        [at + core + 2 * i for i in range(near)]
        for at in range(0, n, 2 * near)
        for core in range(2)
    ]


def far_swap(block, distance):
    n = lax.axis_size("cell")
    return lax.ppermute(block, "cell", [(i, i ^ distance) for i in range(n)])


def exchange(block, groups=None):
    return lax.all_to_all(block, "cell", 0, 0, axis_index_groups=groups)


def call(kernel, name, outs, args, scratch=(), flops=0):
    size = sum(x.size * x.dtype.itemsize for x in args)
    size += sum(x.size * x.dtype.itemsize for x in outs)
    return pl.pallas_call(
        kernel,
        out_shape=outs,
        in_specs=[pl.BlockSpec(memory_space=pltpu.VMEM)] * len(args),
        out_specs=[pl.BlockSpec(memory_space=pltpu.VMEM)] * len(outs),
        scratch_shapes=list(scratch),
        compiler_params=pltpu.CompilerParams(vmem_limit_bytes=24 << 20),
        cost_estimate=pl.CostEstimate(flops=flops, bytes_accessed=size, transcendentals=0),
        name=name,
    )(*args)


def shape(*dims, dtype=F32):
    return jax.ShapeDtypeStruct(dims, dtype)


def group_rows(g, per):
    return slice(g * per, (g + 1) * per)


def block(d, width):
    return slice((d - 1) * width, d * width)


def spread_counts(row):
    per = row.shape[1]
    return jnp.broadcast_to(row.astype(F32), (per, per)).T


def relay_kernel(start, received, source_sums, coarse, end):
    slices, groups, _, _ = coarse.shape
    for g in range(groups):
        V = jnp.where(leading(), start[g], received[g])
        for l in range(slices):
            V = mul(V + source_sums[l, g], stacked(coarse[l, g]))
        end[g] = V


def opening_kernel(out):
    out[...] = jnp.zeros_like(out)


def setup_kernel(everyone, fine, rate, counts, initial, source, coarse, opened,
                 own, other, lows, table, start_sums, source_sums, end):
    slices, groups, width, _ = fine.shape
    per = counts.shape[1]
    half = slices // 2
    core = lax.rem(lax.axis_index("cell"), 2)
    keep = 1.0 - rate[...]
    alive = []
    for g in range(groups):
        k = counts[g:g + 1].astype(F32)
        rows = [
            jnp.sum((k >= q).astype(F32), axis=1, keepdims=True)
            for q in range(FINE_MIN, FINE_MAX + 1)
        ]
        alive.append(rows)
        filled = jnp.zeros((ROWS, width), F32)
        for i, n in enumerate(rows + [None, k, rate[...]]):
            if n is not None:
                filled = jnp.where(row_is(i, filled.shape), n, filled)
        table[g] = filled
    for g in range(groups):
        here = group_rows(g, per)
        k = counts[g:g + 1].astype(F32)
        V = class_sums(initial[here], k)
        start_sums[g] = V
        for l in range(slices):
            S = class_sums(source[l, here], k)
            source_sums[l, g] = S
            V = mul(V + S, stacked(coarse[l, g]))
        end[g] = V
    made = []
    for l in range(slices):
        sums = [0.0] * 4
        e6, e7, e72 = 0.0, 0.0, 0.0
        for g in range(groups):
            w1 = fine[l, g]
            w2 = mul(w1 * keep, stacked(w1))
            first = jnp.concatenate([w1, w2], axis=0)
            w34 = mul(first * keep, stacked(w2))
            w3, w4 = w34[:width], w34[width:]
            lows[l, g, :2 * width] = first
            lows[l, g, 2 * width:] = w34
            sums = [t + w for t, w in zip(sums, (w1, w2, w3, w4))]
            e6 = e6 + alive[g][2] * w1
            e7 = e7 + alive[g][3] * w1
            e72 = e72 + alive[g][3] * w2
        mats = [t * (per / everyone) for t in sums]
        mats += [e6 / everyone, (e6 + e72 - e7) / everyone, e7 / everyone]
        made.append(jnp.concatenate(mats, axis=0))
    first = core == 0
    own[...] = jnp.where(first, jnp.concatenate(made[:half]), jnp.concatenate(made[half:]))
    other[...] = jnp.where(first, jnp.concatenate(made[half:]), jnp.concatenate(made[:half]))


def extend_kernel(everyone, lows, table, source_sums, powers, ofsource):
    slices, groups, _, width = lows.shape
    keep = 1.0 - table[0, RATE_ROW]
    for l in range(slices):
        for g in range(groups):
            ws = [lows[l, g, i * width:(i + 1) * width] for i in range(4)]
            w58 = mul(lows[l, g] * keep, stacked(ws[3]))
            ws += [w58[i * width:(i + 1) * width] for i in range(4)]
            ws.append((ws[0] + ws[1]) + (ws[2] + ws[3]))
            for i, w in enumerate(ws):
                powers[l, g, :, block(i + 1, width)] = stacked(w)
    for l in range(slices):
        rows = 0.0
        for g in range(groups):
            w = powers[l, g, :, :FINE_MAX * width]
            rows = rows + sums_of_source(source_sums[l, g], w, width)
        ofsource[l * ROWS:(l + 1) * ROWS] = rows / everyone


def add_kernel(a, b, out):
    out[...] = a[...] + b[...]


def class_sums(state, k):
    least = (FINE_MIN + lax.broadcasted_iota(jnp.int32, (ROWS, k.shape[1]), 0)).astype(F32)
    mask = (k >= least).astype(F32)
    left = jnp.concatenate([mask, mask], axis=1)
    left = jnp.concatenate([left, jnp.zeros_like(left)], axis=0).astype(BF16)
    return jnp.dot(left, stacked(state), preferred_element_type=F32)[:ROWS]


def picked(products, first, width):
    out = jnp.zeros((ROWS, width), F32)
    for i in range(CLASSES):
        d = first + i
        if 1 <= d <= FINE_MAX:
            out = out + jnp.where(row_is(i, out.shape), products[:, block(d, width)], 0.0)
    return out


def sums_of_state(V, keep, powers, width):
    x = mul(V * keep, powers)
    rows = [V[0:1]] + [x[0:1, block(m, width)] for m in range(1, FINE_MIN + 1)]
    gain = picked(x, FINE_MIN, width) - picked(x, FINE_MIN - 1, width)
    for i in range(1, 4):
        rows.append(rows[-1] + gain[i:i + 1])
    return jnp.concatenate(rows, axis=0)


def sums_of_source(S, powers, width):
    x = mul(S, powers)
    rows = [jnp.zeros((1, width), F32)]
    for m in range(1, FINE_MAX):
        i = max(m - FINE_MIN, 0)
        rows.append(rows[-1] + x[i:i + 1, block(m, width)])
    return jnp.concatenate(rows, axis=0)


def by_count(products, k, first, width):
    out = jnp.zeros(k.shape, F32)
    for i in range(CLASSES):
        d = i * width
        out = jnp.where(k == float(FINE_MIN + i), products[:, d:d + width], out)
    return out


def base_kernel(everyone, sums, received, source_sums, coarse, powers, table, ofsource, base):
    slices, groups, width, _ = coarse.shape
    keep = 1.0 - table[0, RATE_ROW]
    states = [jnp.where(leading(), sums[g], received[g]) for g in range(groups)]
    for l in range(slices):
        rows = 0.0
        for g in range(groups):
            V = states[g]
            rows = rows + sums_of_state(V, keep, powers[l, g, :, :FINE_MAX * width], width)
            if l + 1 < slices:
                states[g] = mul(V + source_sums[l, g], stacked(coarse[l, g]))
        at = slice(l * ROWS, (l + 1) * ROWS)
        base[at] = rows / everyone + ofsource[at]


def sweep_kernel(first, last, *refs):
    if first:
        initial, source, coarse, powers, table, *outs = refs
    else:
        initial, received, source, coarse, powers, table, *outs = refs
    slices, groups, width, _ = coarse.shape
    per = initial.shape[0] // groups
    keep = 1.0 - table[0, RATE_ROW]
    counts = [spread_counts(table[g, COUNT_ROW]) for g in range(groups)]
    held = []
    for g in range(groups):
        here = group_rows(g, per)
        start = initial[here]
        states = [start] * 3
        if not first:
            states = [jnp.where(leading(), start, received[i, here]) for i in range(3)]
        held.append(states)
    for l in range(slices):
        for g in range(groups):
            here = group_rows(g, per)
            states, n, s = held[g], counts[g], source[l, here]
            if last:
                outs[0][l, g] = class_sums(states[1], table[g, COUNT_ROW])
            w = powers[l, g, :, FINE_MIN * width:]
            x = mul(s, w)
            total = x[:, FINE_MIN * width:]
            sourced = jnp.where(n == float(FINE_MIN), total, 0.0)
            for i in range(CLASSES - 1):
                total = total + x[:, i * width:(i + 1) * width]
                sourced = jnp.where(n == float(FINE_MIN + 1 + i), total, sourced)
            both = jnp.concatenate(states[:2], axis=0) * keep
            x = mul(both, powers[l, g, :, (FINE_MIN - 1) * width:FINE_MAX * width])
            moved = mul(
                jnp.concatenate(
                    [states[0] + s, states[1] - states[0], states[2] - states[1]], axis=0
                ),
                stacked(coarse[l, g]),
            )
            held[g] = [
                moved[:per],
                sourced + by_count(x[:per], n, FINE_MIN, width) + moved[per:2 * per],
                sourced + by_count(x[per:], n, FINE_MIN, width) + moved[2 * per:],
            ]
            if last:
                outs[1][l, here] = held[g][2]
    if not last:
        for g in range(groups):
            for i in range(3):
                outs[0][i, group_rows(g, per)] = held[g][i]


def middle_kernel(parts, base, out):
    n, rows, _ = parts.shape
    total = parts[0]
    for p in range(1, n):
        total = total + parts[p]
    out[:rows] = total
    out[rows:] = base[...]


def gather_kernel(a, b, out):
    out[...] = a[...] + b[...]


def wide(row):
    return jnp.broadcast_to(row, (ROWS, row.shape[-1]))


def assembled(known, width):
    out = jnp.zeros((ROWS, width), F32)
    for m, a in enumerate(known):
        out = jnp.where(row_is(m, out.shape), a, out)
    return out


def first_averages(rows, mixing, rate, width):
    slices = len(rows)
    known = [[] for _ in range(slices)]
    sent = [[] for _ in range(slices)]
    for m in range(FINE_MIN + 1):
        for l in range(slices):
            a = wide(rows[l][m])
            for j in range(m):
                a = a + sent[l][j][:, block(m - j, width)]
            known[l].append(a)
            if m < FINE_MIN:
                sent[l].append(mul(a * rate, mixing[l, :, :(FINE_MIN - m) * width]))
    return [assembled(a, width) for a in known]


def shifted(products, width):
    out = jnp.zeros((2 * ROWS, width), F32)
    empty = jnp.zeros((ROWS, width), F32)
    for d in range(1, products.shape[1] // width + 1):
        z = jnp.concatenate([products[:, block(d, width)], empty], axis=0)
        out = out + pltpu.roll(z, d, 0)
    return out


def second_rows(everyone, per, a, base, rate, powers, table, partial, l, width):
    groups = powers.shape[1]
    rows = [0.0] * 3
    for g in range(groups):
        h = shifted(mul(a * rate, powers[l, g, :, :FINE_MAX * width]), width)
        partial[l, g] = h
        total = per * h[4:5]
        for i in range(1, 4):
            total = total + table[g, i:i + 1] * (h[4 + i:5 + i] - h[3 + i:4 + i])
            rows[i - 1] = rows[i - 1] + total
    at = l * ROWS + FINE_MIN + 1
    return [rows[i] / everyone + base[at + i:at + i + 1] for i in range(3)]


def send_line(rows, out):
    line = jnp.concatenate(rows, axis=1)
    for p in range(out.shape[0]):
        out[p] = line


def received_rows(received, width):
    total = received[0]
    for p in range(1, received.shape[0]):
        total = total + received[p]
    return [total[:, i:i + width] for i in range(0, total.shape[1], width)]


def send_rows(everyone, per, a, base, rate, powers, table, partial, out, width):
    rows = []
    for l in range(powers.shape[0]):
        rows += second_rows(everyone, per, a[l], base, rate, powers, table, partial, l, width)
    send_line(rows, out)


def mixing_kernel(everyone, per, near, *refs):
    blocks, refs = refs[:2 * near], refs[2 * near:]
    base, powers, table, mixing, partial, out, held = refs
    slices, _, _, wider = powers.shape
    width = wider // (FINE_MAX + 1)
    half = slices // 2
    rows = blocks[0].shape[0] - slices * ROWS
    rate = table[0, RATE_ROW]
    index = lax.axis_index("cell")
    core = lax.rem(index, 2)
    here = lax.rem(lax.div(index, 2), near)
    mixed = 0.0
    for refs, at in ((blocks[:near], core), (blocks[near:], 1 - core)):
        for j, ref in enumerate(refs):
            shard = jnp.bitwise_xor(here, j)
            held[pl.ds(at * (half * MATS * width) + shard * rows, rows), :] = ref[:rows]
            mixed = mixed + ref[rows:]

    def place(l, i):
        at = (l * MATS + i) * width
        mixing[l, :, block(i + 1, width)] = stacked(held[at:at + width])

    for l in range(slices):
        for i in range(FINE_MIN):
            place(l, i)
    rows = [
        [mixed[l * ROWS + m:l * ROWS + m + 1] for m in range(FINE_MIN + 1)]
        for l in range(slices)
    ]
    a = first_averages(rows, mixing, rate, width)
    for l in range(slices):
        for i in range(FINE_MIN, MATS):
            place(l, i)
    send_rows(everyone, per, a, base, rate, powers, table, partial, out, width)


def first_kernel(everyone, per, received, base, mixing, powers, table, partial, out):
    slices, _, _, wider = powers.shape
    width = wider // (FINE_MAX + 1)
    rate = table[0, RATE_ROW]
    rows = received_rows(received, width)
    known = FINE_MIN + 1
    rows = [rows[l * known:(l + 1) * known] for l in range(slices)]
    a = first_averages(rows, mixing, rate, width)
    send_rows(everyone, per, a, base, rate, powers, table, partial, out, width)


def push_kernel(received, partial, mixing, powers, table, coarse, *refs):
    starts, (pushes, end) = (None, refs) if len(refs) == 2 else (refs[0], refs[1:])
    slices, groups, _, wider = powers.shape
    width = wider // (FINE_MAX + 1)
    r = table[0, RATE_ROW]
    rows = received_rows(received, width)
    fives = [wide(rows[3 * l]) for l in range(slices)]
    fed = [mul(fives[l] * r, mixing[l, :, 4 * width:6 * width]) for l in range(slices)]
    sixes = [wide(rows[3 * l + 1]) + fed[l][:, :width] for l in range(slices)]
    late = [mul(sixes[l] * r, mixing[l, :, 6 * width:]) for l in range(slices)]
    h = [[None] * groups for _ in range(slices)]
    for l in range(slices):
        a = jnp.zeros((ROWS, width), F32)
        seven = wide(rows[3 * l + 2]) + fed[l][:, width:] + late[l]
        for m, row in ((5, fives[l]), (6, sixes[l]), (7, seven)):
            a = jnp.where(row_is(m, a.shape), row, a)
        for g in range(groups):
            z = mul(a * r, powers[l, g, :, :3 * width])
            h[l][g] = (partial[l, g] + shifted(z, width))[FINE_MIN:FINE_MIN + ROWS]
            if starts is not None:
                w = powers[l, g, :, (FINE_MIN - 1) * width:FINE_MAX * width]
                h[l][g] = h[l][g] + picked(mul(starts[l, g] * (1.0 - r), w), 1, width)
    x = [jnp.zeros((ROWS, width), F32) for _ in range(groups)]
    for l in range(slices):
        for g in range(groups):
            old = x[g] if starts is None else x[g] - starts[l, g]
            x[g] = h[l][g] + mul(old, stacked(coarse[l, g]))
            pushes[l, g] = h[l][g]
    for g in range(groups):
        end[g] = x[g]


def vectors_kernel(received, pushes, starts, coarse, end):
    slices, groups, _, _ = coarse.shape
    for g in range(groups):
        x = jnp.where(leading(), 0.0, received[g])
        for l in range(slices):
            x = pushes[l, g] + mul(x - starts[l, g], stacked(coarse[l, g]))
        end[g] = x


def second_kernel(everyone, received, pushes, coarse, sums, table, powers, ofsource,
                  starts, base, out):
    slices, groups, width, _ = coarse.shape
    keep = 1.0 - table[0, RATE_ROW]
    x = [jnp.where(leading(), 0.0, received[g]) for g in range(groups)]
    sent = []
    for l in range(slices):
        rows = 0.0
        for g in range(groups):
            starts[l, g] = x[g]
            n = table[g]
            exact = n - pltpu.roll(n, ROWS - 1, 0)
            exact = jnp.where(row_is(ROWS - 1, n.shape), 0.0, exact)
            weighted = exact * x[g]
            tail = jnp.zeros((1, width), F32)
            V = sums[l, g]
            for i in reversed(range(CLASSES)):
                tail = tail + weighted[i:i + 1]
                V = jnp.where(row_is(i, V.shape), V + tail, V)
            rows = rows + sums_of_state(V, keep, powers[l, g, :, :FINE_MAX * width], width)
            if l + 1 < slices:
                x[g] = pushes[l, g] + mul(x[g], stacked(coarse[l, g]))
        at = slice(l * ROWS, (l + 1) * ROWS)
        rows = rows / everyone + ofsource[at]
        base[at] = rows
        sent += [rows[m:m + 1] for m in range(FINE_MIN + 1)]
    send_line(sent, out)


def finish_kernel(received, pushes, starts, coarse, ends, table, out):
    slices, groups, width, _ = coarse.shape
    per = ends.shape[1] // groups
    counts = [spread_counts(table[g, COUNT_ROW]) for g in range(groups)]
    x = [jnp.where(leading(), 0.0, received[g]) for g in range(groups)]
    for l in range(slices):
        for g in range(groups):
            here = group_rows(g, per)
            x[g] = pushes[l, g] + mul(x[g] - starts[l, g], stacked(coarse[l, g]))
            add = jnp.zeros((per, width), F32)
            for i in range(CLASSES):
                add = jnp.where(counts[g] == float(FINE_MIN + i), x[g][i:i + 1], add)
            out[l, here] = ends[l, here] + add


def body(initial, source, mix_rate, fine, coarse, step_counts):
    slices, groups, width, _ = fine.shape
    cells = initial.shape[0]
    per = cells // groups
    n_cell = lax.axis_size("cell")
    turns = lax.axis_size("tm") - 1
    everyone = cells * n_cell
    half = slices // 2
    near = near_size()
    shard = half * MATS * width // near
    rate = mix_rate.reshape(1, width)
    counts = step_counts.reshape(groups, per)
    state = shape(cells, width)
    states = shape(slices, cells, width)
    vectors = shape(slices, groups, ROWS, width)
    vector = shape(groups, ROWS, width)
    rows8 = shape(slices * ROWS, width)
    line3 = shape(n_cell, 1, slices * 3 * width)
    line5 = shape(n_cell, 1, slices * (FINE_MIN + 1) * width)
    partial = shape(slices, groups, 2 * ROWS, width)
    mats = shape(half * MATS * width, width)
    opened, = call(opening_kernel, "opening", [shape(ROWS, width)], (), flops=OPENING_FLOPS)
    own, other, lows, table, sums0, source_sums, moved = call(
        functools.partial(setup_kernel, everyone), "setup",
        [mats, mats, shape(slices, groups, 4 * width, width), vector, vector, vectors, vector],
        (fine, rate, counts, initial, source, coarse, opened),
    )
    for turn in range(turns):
        moved = from_behind(moved, "tm", 1)
        if turn + 1 < turns:
            moved, = call(relay_kernel, "relay", [vector], (sums0, moved, source_sums, coarse))
    swapped = swap_core(other)
    powers, ofsource = call(
        functools.partial(extend_kernel, everyone), "extend",
        [shape(slices, groups, 2 * width, (FINE_MAX + 1) * width, dtype=BF16), rows8],
        (lows, table, source_sums),
    )
    base, = call(
        functools.partial(base_kernel, everyone), "base", [rows8],
        (sums0, moved, source_sums, coarse, powers, table, ofsource),
    )
    swapped, base = lax.optimization_barrier((swapped, base))
    mine, = call(add_kernel, "add", [mats], (own, swapped))
    parts = exchange(mine.reshape(near, shard, width), near_groups())
    block, = call(
        middle_kernel, "middle", [shape(shard + slices * ROWS, width)], (parts, base)
    )
    block, later = lax.optimization_barrier((block, initial))
    bundle = shape(3, cells, width)
    sent, = call(
        functools.partial(sweep_kernel, True, False), "sweep", [bundle],
        (later, source, coarse, powers, table),
    )
    far = jnp.zeros_like(block)
    distance = 2 * near
    while distance < n_cell:
        far = far_swap(block, distance)
        distance *= 2
        if distance < n_cell:
            block = block + far
    far, sent = lax.optimization_barrier((far, sent))
    for turn in range(turns):
        sent = from_behind(sent, "tm", 1)
        if turn + 1 < turns:
            sent, = call(
                functools.partial(sweep_kernel, False, False), "sweep", [bundle],
                (initial, sent, source, coarse, powers, table),
            )
    payload, = call(
        gather_kernel, "gather", [shape(shard + slices * ROWS, width)], (block, far)
    )
    crossed = {j: far_swap(payload, 2 * j) for j in reversed(range(1, near))}
    gathered = [payload] + [crossed[j] for j in range(1, near)]
    sums, ends = call(
        functools.partial(sweep_kernel, False, True), "sweep", [vectors, states],
        (initial, sent, source, coarse, powers, table),
    )
    theirs = [swap_core(x) for x in gathered]
    mixing, first, out = call(
        functools.partial(mixing_kernel, everyone, per, near), "mixing",
        [shape(slices, 2 * width, MATS * width, dtype=BF16), partial, line3],
        (*gathered, *theirs, base, powers, table),
        scratch=[pltpu.VMEM((slices * MATS * width, width), F32)],
    )
    pushes1, end = call(
        push_kernel, "push", [vectors, vector],
        (exchange(out), first, mixing, powers, table, coarse),
    )
    nothing = jnp.zeros(vectors.shape, F32)
    moved = end
    for turn in range(turns):
        moved = from_behind(moved, "tm", 1)
        if turn + 1 < turns:
            moved, = call(vectors_kernel, "vectors", [vector], (moved, pushes1, nothing, coarse))
    moved1, base, out = call(
        functools.partial(second_kernel, everyone), "second",
        [vectors, rows8, line5],
        (moved, pushes1, coarse, sums, table, powers, ofsource),
    )
    first, out = call(
        functools.partial(first_kernel, everyone, per), "first", [partial, line3],
        (exchange(out), base, mixing, powers, table),
    )
    pushes2, end = call(
        push_kernel, "push", [vectors, vector],
        (exchange(out), first, mixing, powers, table, coarse, moved1),
    )
    moved = end
    for turn in range(turns):
        moved = from_behind(moved, "tm", 1)
        if turn + 1 < turns:
            moved, = call(vectors_kernel, "vectors", [vector], (moved, pushes2, moved1, coarse))
    out, = call(
        finish_kernel, "finish", [states], (moved, pushes2, moved1, coarse, ends, table)
    )
    return out


def solution(mesh):
    return jax.shard_map(
        body,
        mesh=mesh,
        in_specs=(
            P("cell", None),
            P("tm", "cell", None),
            P(),
            P("tm", "cell", None, None),
            P("tm", "cell", None, None),
            P("cell"),
        ),
        out_specs=P("tm", "cell", None),
        check_vma=False,
    )
```
